128 devices in a mesh: rows: 16 (over x_hi, y, core), seq: 8 (over x_lo, z).
Axes of the slice: x: 4 (x_hi: 2, x_lo: 2; x = x_hi * 2 + x_lo), y: 4, z: 4, core: 2. Of those that a mesh axis runs over, the one named last changes fastest.
Arguments:
- block_input: bfloat16 [64, 1024, 1024], P('rows', 'seq'), may hold values from -6 to 6
- segment_ids: int32 [64, 1024], P('rows'), may hold values from 0 to 3, never falling along the last dimension, each value on 1 to 512 neighbouring positions
- padding_flags: int32 [64, 1024], P('rows'), may hold values 0 or 1
- cotangent: bfloat16 [64, 1024, 1024], P('rows', 'seq'), may hold values from -6 to 6
- norm_one_gain: bfloat16 [1024], replicated, may hold values from 0.5 to 1.5
- norm_one_bias: bfloat16 [1024], replicated, may hold values from -1.75 to 1.75
- query_key_value: bfloat16 [1024, 3072], replicated, may hold values from -0.1875 to 0.1875
- query_value_bias: bfloat16 [2048], replicated, may hold values from -1.75 to 1.75
- out_weight: bfloat16 [1024, 1024], replicated, may hold values from -0.75 to 0.75
- out_bias: bfloat16 [1024], replicated, may hold values from -1.75 to 1.75
- norm_two_gain: bfloat16 [1024], replicated, may hold values from 0.5 to 1.5
- norm_two_bias: bfloat16 [1024], replicated, may hold values from -1.75 to 1.75
- up_weight: bfloat16 [1024, 4096], replicated, may hold values from -0.1875 to 0.1875
- up_bias: bfloat16 [4096], replicated, may hold values from -1.75 to 1.75
- down_weight: bfloat16 [4096, 1024], replicated, may hold values from -0.09375 to 0.09375
- down_bias: bfloat16 [1024], replicated, may hold values from -1.75 to 1.75
Outputs:
- layer_out: bfloat16 [64, 1024, 1024], P('rows', 'seq')
- grad_input: bfloat16 [64, 1024, 1024], P('rows', 'seq')
- grad_norm_one_gain: float32 [1024], P(('rows', 'seq'))
- grad_norm_one_bias: float32 [1024], P(('rows', 'seq'))
- grad_query_key_value: float32 [1024, 3072], P(('rows', 'seq'))
- grad_query_value_bias: float32 [2048], P(('rows', 'seq'))
- grad_out_weight: float32 [1024, 1024], P(('rows', 'seq'))
- grad_out_bias: float32 [1024], P(('rows', 'seq'))
- grad_norm_two_gain: float32 [1024], P(('rows', 'seq'))
- grad_norm_two_bias: float32 [1024], P(('rows', 'seq'))
- grad_up_weight: float32 [1024, 4096], P(('rows', 'seq'))
- grad_up_bias: float32 [4096], P(('rows', 'seq'))
- grad_down_weight: float32 [4096, 1024], P(('rows', 'seq'))
- grad_down_bias: float32 [1024], P(('rows', 'seq'))
The draws below stay inside these ranges and needn't reach their ends.
Inputs may be any that keep to these rules, and one draw needn't show every extreme that they name: `segment_ids`: along each row the ids never fall; each document holds 1 to 512 positions, and some document holds exactly that many.
All inputs are finite; a program needn't handle non-finite values. No bound on the sum of `padding_flags` on one device may be relied on, other than what follows from the above.
Results may differ from the reference program's by a relative error of at most 0.017.
Values may be sent and summed in bfloat16 or wider, within the bound.
A program may use at most 256 MiB of HBM per device.

```python
import math
import jax
import jax.numpy as jnp
import numpy as np
from jax import lax

D = 1024
HEADS = 16
FF = 4096
LEN = 1024
HEAD_DIM = 64
ROWS = 64


def place_ends(values, rng, smallest, largest):
    extent = values.shape
    place = [jax.random.randint(jax.random.fold_in(rng, axis), (), 0, extent[axis]) for axis in range(len(extent))]
    values = values.at[tuple(place)].set(smallest)
    longest = extent.index(max(extent))
    place[longest] = (place[longest] + 1) % extent[longest]
    return values.at[tuple(place)].set(largest)


def raised(result, key, source, target, parts, factor):
    def block_of(dim):
        return (jnp.arange(result.shape[dim]) // (result.shape[dim] // parts)).reshape((-1,) + (1,) * (result.ndim - 1 - dim))

    one_side = jax.random.permutation(key, parts)[block_of(target)]
    second = (block_of(target) + parts // 2) % parts
    return jnp.where((block_of(source) == one_side) | (block_of(source) == second), factor * result, result)


def shard_levels(rng, shape, cuts, smallest, largest):
    def one(dim, shards_of):
        draws = jax.random.uniform(jax.random.fold_in(jax.random.fold_in(rng, 6), dim), (shards_of,), jnp.float32, smallest / len(cuts), largest / len(cuts))
        return jnp.repeat(jnp.exp(draws), shape[dim] // shards_of).reshape((-1,) + (1,) * (len(shape) - dim - 1))

    loudness = one(*cuts[0])
    for cut in cuts[1:]:
        loudness = loudness * one(*cut)
    return loudness


def split_up(count, total, reach, skew):
    weights = [(1 << 20) // math.isqrt(rank ** skew) + 1 for rank in range(2, count + 1)]
    rest, counts = total - reach - (count - 1), [1] * (count - 1)
    while rest > 0:
        movable = [i for i in range(count - 1) if counts[i] < reach]
        whole, left = sum([weights[i] for i in movable]), rest
        for i in movable:
            more = min(reach - counts[i], max(1, left * weights[i] // whole), rest)
            counts[i] = counts[i] + more
            rest = rest - more
    return np.array([reach] + counts)


def ragged_sizes(stream_key, number_of, total, reach, skew):
    if number_of == 2:
        one = jax.random.randint(stream_key, (), max(1, total - reach), min(reach, total - 1) + 1)
        return jnp.stack([one, total - one])
    lengths = jnp.asarray(split_up(number_of, total, reach, skew), jnp.int32)
    couples = (number_of - 1) // 2
    donor, receiver = lengths[1:1 + 2 * couples:2], lengths[2:2 + 2 * couples:2]
    room = jnp.minimum(donor - 1, reach - receiver)
    moved = jax.random.randint(jax.random.fold_in(stream_key, 1), (couples,), 0, 1 << 20) % (room + 1)
    lengths = lengths.at[1:1 + 2 * couples:2].set(donor - moved).at[2:2 + 2 * couples:2].set(receiver + moved)
    return lengths[jax.random.permutation(jax.random.fold_in(stream_key, 2), number_of)]


def scatter_about(rng, shape, deviation, limit, shards=(), dtype=jnp.bfloat16):
    loudness = shard_levels(rng, shape, shards, -0.22, 0.18) if shards else 1.0
    entries = jax.random.normal(rng, shape, jnp.float32) * deviation * loudness
    return jnp.minimum(jnp.maximum(entries, -limit), limit).astype(dtype)


def noise_with(rng, extent, spread, bound, cuts, heavy, kind=jnp.bfloat16):
    array = spread * jax.random.normal(rng, extent, jnp.float32)
    if cuts:
        array = array * shard_levels(rng, extent, cuts, -0.22, 0.18)
    return jnp.clip(raised(array, jax.random.fold_in(rng, 3), *heavy), -bound, bound).astype(kind)


def setup_inputs(seed: int = 0) -> dict:
    splits = jax.random.split(jax.random.key(seed), 17)
    block_input = scatter_about(splits[0], (ROWS, LEN, D), 1.0, 6.0, ((0, 16), (1, 8)))
    segment_ids = jax.vmap(lambda own: jnp.searchsorted(jnp.cumsum(ragged_sizes(own, 4, LEN, LEN // 2, 0)), jnp.arange(LEN), side="right"))(jax.random.split(splits[1], ROWS)).reshape((ROWS, LEN)).astype(jnp.int32)
    padding_flags = place_ends((jax.random.randint(splits[2], (ROWS, LEN), 0, 8) < 1).astype(jnp.int32), jax.random.fold_in(splits[2], 1), 0, 1)
    cotangent = noise_with(splits[3], (ROWS, LEN, D), 1.0, 6.0, ((0, 16), (1, 8)), (0, 2, 16, 2.0))
    norm_one_gain = jnp.clip(1.0 + 0.1 * jax.random.normal(splits[4], (D,), jnp.float32), 0.5, 1.5).astype(jnp.bfloat16)
    norm_one_bias = scatter_about(splits[5], (D,), 0.3, 1.75)
    query_key_value = scatter_about(splits[6], (D, 3 * D), D ** -0.5, 0.1875)
    query_value_bias = scatter_about(splits[7], (2 * D,), 0.3, 1.75)
    out_weight = scatter_about(splits[8], (D, D), (D // 16) ** -0.5, 0.75)
    out_bias = scatter_about(splits[9], (D,), 0.3, 1.75)
    norm_two_gain = jnp.clip(1.0 + 0.1 * jax.random.normal(splits[10], (D,), jnp.float32), 0.5, 1.5).astype(jnp.bfloat16)
    norm_two_bias = scatter_about(splits[11], (D,), 0.3, 1.75)
    up_weight = scatter_about(splits[12], (D, FF), D ** -0.5, 0.1875)
    up_bias = scatter_about(splits[13], (FF,), 0.3, 1.75)
    down_weight = scatter_about(splits[14], (FF, D), FF ** -0.5, 0.09375)
    down_bias = scatter_about(splits[15], (D,), 0.3, 1.75)
    return dict(block_input=block_input, segment_ids=segment_ids, padding_flags=padding_flags, cotangent=cotangent, norm_one_gain=norm_one_gain, norm_one_bias=norm_one_bias, query_key_value=query_key_value, query_value_bias=query_value_bias, out_weight=out_weight, out_bias=out_bias, norm_two_gain=norm_two_gain, norm_two_bias=norm_two_bias, up_weight=up_weight, up_bias=up_bias, down_weight=down_weight, down_bias=down_bias)


@jax.custom_vjp
def low(v):
    return lax.optimization_barrier(v.astype(jnp.bfloat16)).astype(jnp.float32)

@jax.custom_vjp
def low_back(v):
    return v

def low_keep(v):
    return (low(v), None)

def low_pass(kept, grad):
    return (grad,)

def back_keep(v):
    return (v, None)

def back_low(kept, grad):
    return (low(grad),)
low.defvjp(low_keep, low_pass)
low_back.defvjp(back_keep, back_low)

def layer_norm(values, gain, shift):
    center = values - lax.optimization_barrier(jnp.mean(values, axis=-1, keepdims=True))
    variance = lax.optimization_barrier(jnp.mean(center * center, axis=-1, keepdims=True))
    return center * lax.rsqrt(variance + 1e-05) * gain + shift

def allowed_keys(segment_row, flag_row):
    count = segment_row.shape[0]
    position = lax.broadcasted_iota(jnp.int32, (count, count), 0)
    column = lax.broadcasted_iota(jnp.int32, (count, count), 1)
    same = segment_row[:, None] == segment_row[None, :]
    return same & (column <= position) & ((flag_row[None, :] == 0) | (column == position))

def attend_row(items):
    packed, segment_row, flag_row = items
    query = packed[:, 0].reshape(LEN, HEADS, HEAD_DIM)
    keys_row = packed[:, 1].reshape(LEN, HEADS, HEAD_DIM)
    value_row = packed[:, 2].reshape(LEN, HEADS, HEAD_DIM)
    scores = jnp.einsum('qhd,khd->hqk', query, keys_row, precision=lax.Precision.HIGHEST) * HEAD_DIM ** (-0.5)
    scores = jnp.where(allowed_keys(segment_row, flag_row)[None], scores, -1e+30)
    scores = low_back(scores)
    probs = low(jax.nn.softmax(scores, axis=-1))
    context = jnp.einsum('hqk,khd->qhd', probs, value_row, precision=lax.Precision.HIGHEST)
    return context.reshape(LEN, D)

def layer_group(params, items):
    gain_one, bias_one, qkv_weight, qv_bias, attn_weight, attn_bias, gain_two, bias_two, w_up, b_up, w_down, b_down = params
    block, segments, flags = items
    group = block.shape[0]
    flat_in = block.reshape(group * LEN, D)
    normed_one = low(layer_norm(flat_in, gain_one, bias_one))
    bias_full = jnp.concatenate([qv_bias[:D], jnp.zeros((D,), jnp.float32), qv_bias[D:]])
    qkv = jnp.dot(normed_one, qkv_weight, precision=lax.Precision.HIGHEST) + bias_full
    qkv = low(low_back(qkv)).reshape(group, LEN, 3, D)
    context = lax.map(jax.checkpoint(attend_row), (qkv, segments, flags))
    context = low(low_back(context)).reshape(group * LEN, D)
    attn = low_back(jnp.dot(context, attn_weight, precision=lax.Precision.HIGHEST) + attn_bias)
    resid = flat_in + attn
    normed_two = low(layer_norm(resid, gain_two, bias_two))
    up_val = low_back(jnp.dot(normed_two, w_up, precision=lax.Precision.HIGHEST) + b_up)
    act = low(jax.nn.gelu(up_val, approximate=True))
    down_val = jnp.dot(act, w_down, precision=lax.Precision.HIGHEST) + b_down
    return (resid + down_val).reshape(group, LEN, D)

def reference(block_input, segment_ids, padding_flags, cotangent, norm_one_gain, norm_one_bias, query_key_value, query_value_bias, out_weight, out_bias, norm_two_gain, norm_two_bias, up_weight, up_bias, down_weight, down_bias):
    group = math.gcd(ROWS, 4)
    blocks = ROWS // group
    segments = segment_ids.reshape(blocks, group, LEN)
    flags = padding_flags.reshape(blocks, group, LEN)
    params = tuple((a.astype(jnp.float32) for a in (norm_one_gain, norm_one_bias, query_key_value, query_value_bias, out_weight, out_bias, norm_two_gain, norm_two_bias, up_weight, up_bias, down_weight, down_bias)))
    inputs = block_input.astype(jnp.float32).reshape(blocks, group, LEN, D)

    def forward(inputs, *params):
        step_fn = jax.checkpoint(lambda items: layer_group(params, items))
        return lax.map(step_fn, (inputs, segments, flags))
    outputs, backward = jax.vjp(forward, inputs, *params)
    grads = backward(cotangent.astype(jnp.float32).reshape(blocks, group, LEN, D))
    layer_out = outputs.reshape(ROWS, LEN, D).astype(jnp.bfloat16)
    grad_input = grads[0].reshape(ROWS, LEN, D).astype(jnp.bfloat16)
    return (layer_out, grad_input, grads[1], grads[2], grads[3], grads[4], grads[5], grads[6], grads[7], grads[8], grads[9], grads[10], grads[11], grads[12])
```

```python
import jax
import jax.numpy as jnp
from jax import lax
from jax.experimental import pallas as pl
from jax.experimental.pallas import tpu as pltpu
from jax.sharding import Mesh, PartitionSpec as P

BF = jnp.bfloat16
F32 = jnp.float32
AXES = ("xh", "y", "c", "xl", "z")
BY_MESH = pl.DeviceIdType.MESH
DIMS = ("x1", "y1", "z1", "x0", "y0", "z0")
UP_GROUPS = ((0, 3, 0), (3, 6, 1), (6, 9, 2), (9, 12, 3), (12, 14, 4), (14, 16, 5))
DOWN_GROUPS = ((0, 1, 0), (1, 2, 1), (2, 3, 2), (3, 4, 3), (4, 6, 4), (6, 8, 5))
OUT_GROUPS = ((0, 1, 0), (1, 2, 1), (2, 3, 2), (3, 4, 3))
BLOCK = 256
GELU = 0.7978845608028654
CUBIC = 0.044715
EPS = 1e-05
MASKED = -1e30
VMEM_LIMIT = 60 * 1024 * 1024


def dot_nn(a, b):
    return lax.dot_general(a, b, (((1,), (0,)), ((), ())), preferred_element_type=F32)


def dot_nt(a, b):
    return lax.dot_general(a, b, (((1,), (1,)), ((), ())), preferred_element_type=F32)


def dot_tn(a, b):
    return lax.dot_general(a, b, (((0,), (0,)), ((), ())), preferred_element_type=F32)


class Place:
    def __init__(self):
        self.xh, self.y, self.c, self.xl, self.z = (lax.axis_index(a) for a in AXES)
        two = jnp.int32(2)
        self.bits = {
            "x1": self.xh,
            "x0": lax.rem(self.xl + self.xh, two),
            "y1": lax.div(self.y, two),
            "y0": lax.rem(self.y + lax.div(self.y, two), two),
            "z1": lax.div(self.z, two),
            "z0": lax.rem(self.z + lax.div(self.z, two), two),
        }

    def partner(self, name):
        xh, y, c, xl, z = self.xh, self.y, self.c, self.xl, self.z
        if name == "c":
            c = 1 - c
        elif name == "x0":
            xl = 1 - xl
        elif name == "x1":
            xh, xl = 1 - xh, 1 - xl
        elif name == "y0":
            y = y + 1 - 2 * lax.rem(y, jnp.int32(2))
        elif name == "y1":
            y = 3 - y
        elif name == "z0":
            z = z + 1 - 2 * lax.rem(z, jnp.int32(2))
        elif name == "z1":
            z = 3 - z
        return (xh, y, c, xl, z)

    def ring(self, axis, step):
        four, two = jnp.int32(4), jnp.int32(2)
        xh, y, c, xl, z = self.xh, self.y, self.c, self.xl, self.z
        if axis == "x":
            at = lax.rem(2 * xh + xl + step, four)
            xh, xl = lax.div(at, two), lax.rem(at, two)
        elif axis == "y":
            y = lax.rem(y + step, four)
        else:
            z = lax.rem(z + step, four)
        return (xh, y, c, xl, z)

    def exchange(self, r):
        return (self.xh, self.y, self.xl, self.c, jnp.int32(r))

    def is_self(self, r):
        return (self.c == self.xl) & (self.z == r)


def order_of(o):
    return DIMS[o:] + DIMS[:o]


def half(n, k):
    return n >> k


def region(k):
    return 64 - (64 >> (k - 1))


def natural_code(s):
    xh, y, xl, z = s >> 5, (s >> 3) & 3, (s >> 2) & 1, s & 3
    bits = (xh, y >> 1, z >> 1, xl ^ xh, (y & 1) ^ (y >> 1), (z & 1) ^ (z >> 1))
    code = 0
    for b in bits:
        code = 2 * code + b
    return code


def turned(code, o):
    return ((code << o) & 63) | (code >> (6 - o))


def turned_by(code, power):
    scaled = code * power
    return lax.rem(scaled, jnp.int32(64)) + lax.div(scaled, jnp.int32(64))


def offset_before(place, o, k):
    off = jnp.int32(0)
    for j, name in enumerate(order_of(o)[: k - 1]):
        off = off + place.bits[name] * (64 >> (j + 1))
    return off


def scatter_copy(place, k, buf, got, lead, o, sends, recvs, at):
    name = order_of(o)[k - 1]
    n = 64 >> k
    start = offset_before(place, o, k) + (1 - place.bits[name]) * n
    return pltpu.make_async_remote_copy(
        src_ref=buf.at[lead + (pl.ds(start, n),)],
        dst_ref=got.at[lead + (pl.ds(region(k), n),)],
        send_sem=sends.at[at],
        recv_sem=recvs.at[at],
        device_id=place.partner(name),
        device_id_type=BY_MESH,
    )


def scatter_add(place, k, buf, got, piece, o):
    n = 64 >> k
    keep = offset_before(place, o, k + 1)
    mine = piece + (pl.ds(keep, n),)
    buf[mine] = buf[mine] + got[piece + (pl.ds(region(k), n),)]


def feature_rows(flat):
    parts = []
    for g in range(8):
        for c in range(2):
            parts.append(flat[(c * 8 + g) * 8 : (c * 8 + g + 1) * 8])
    return jnp.concatenate(parts, axis=0)


def transpose_features(src, dst):
    def body(f, carry):
        block = src[:, pl.ds(pl.multiple_of(f * 128, 128), 128)].astype(F32)
        dst[pl.ds(pl.multiple_of(f * 128, 128), 128), :] = feature_rows(block.T).astype(BF)
        return carry

    lax.fori_loop(0, 8, body, 0)


def norm_parts(v):
    center = v - jnp.mean(v, axis=-1, keepdims=True)
    rstd = lax.rsqrt(jnp.mean(center * center, axis=-1, keepdims=True) + EPS)
    return center * rstd, rstd


def aligned(v, m):
    return pl.multiple_of(v, m)


def window(i):
    return max(0, i - 2) * BLOCK, (i + 1) * BLOCK


def remote(src, dst, send, recv, device):
    return pltpu.make_async_remote_copy(
        src_ref=src, dst_ref=dst, send_sem=send, recv_sem=recv, device_id=device, device_id_type=BY_MESH
    )


def greet(place, devices, with_exchange):
    barrier = pltpu.get_barrier_semaphore()
    count = jnp.int32(len(devices))
    for d in devices:
        pl.semaphore_signal(barrier, inc=1, device_id=d, device_id_type=BY_MESH)
    if with_exchange:
        for r in range(4):

            @pl.when(jnp.logical_not(place.is_self(r)))
            def _(r=r):
                pl.semaphore_signal(barrier, inc=1, device_id=place.exchange(r), device_id_type=BY_MESH)

        count = count + 4 - jnp.where(place.c == place.xl, 1, 0)
    pl.semaphore_wait(barrier, count)


def exchange_start(place, src_of, dst_of, own_dst_of, sends, recvs):
    for r in range(4):
        own = place.is_self(r)

        @pl.when(own)
        def _(r=r):
            pltpu.make_async_copy(src_of(r), own_dst_of(r), recvs.at[place.z]).start()

        @pl.when(jnp.logical_not(own))
        def _(r=r):
            remote(src_of(r), dst_of(r), sends.at[r], recvs.at[place.z], place.exchange(r)).start()


def exchange_sent(place, src_of, dst_of, sends, recvs):
    for r in range(4):

        @pl.when(jnp.logical_not(place.is_self(r)))
        def _(r=r):
            remote(src_of(r), dst_of(r), sends.at[r], recvs.at[place.z], place.exchange(r)).wait_send()


def forward_kernel(
    x_in, c_in, seg_in, flag_in, par, wqkv, wout,
    resid_o, h1_o, c_o, h2_o, qkv_o, ctxp_o, ctxh_o, lse_o, seg_o, x_o,
    wq, wo, seg_got, b0, b1, b2, b3, lse_acc,
    xs, xr, cs, cr, hs, hr, fs, fr, ts, tr, gs, gr, ss, sr, ws,
):
    place = Place()
    c, xl, z = place.c, place.xl, place.z
    mate = place.partner("c")
    loads = [
        pltpu.make_async_copy(
            wqkv.at[:, pl.ds(aligned(j * 1024 + c * 512, 512), 512)], wq.at[:, pl.ds(j * 512, 512)], ws.at[j]
        )
        for j in range(3)
    ]
    loads.append(pltpu.make_async_copy(wout, wo, ws.at[3]))
    for load in loads:
        load.start()
    greet(place, [mate], True)

    def x_src(r):
        return x_in.at[r]

    def x_dst(r):
        return x_o.at[pl.ds(aligned(z * 128, 128), 128)]

    def c_src(r):
        return c_in.at[r]

    def c_dst(r):
        return c_o.at[pl.ds(aligned(xl * 512 + z * 128, 128), 128)]

    exchange_start(place, x_src, x_dst, x_dst, xs, xr)
    seg_out = [remote(ref, seg_got.at[n], ss.at[n], sr.at[n], mate) for n, ref in enumerate((seg_in, flag_in))]
    for copy in seg_out:
        copy.start()
    exchange_start(place, c_src, c_dst, c_dst, cs, cr)

    gain_one, bias_one = par[0:1, :], par[1:2, :]

    def h1_copy(b):
        rows = pl.ds(aligned(c * 512 + b * 128, 128), 128)
        return remote(h1_o.at[rows], h1_o.at[rows], hs.at[b], hr.at[b], mate)

    def c_copy(b):
        rows = pl.ds(aligned(c * 512 + b * 128, 128), 128)
        return remote(c_o.at[rows], c_o.at[rows], fs.at[b], fr.at[b], mate)

    def h1_got(b):
        rows = pl.ds(aligned((1 - c) * 512 + b * 128, 128), 128)
        return remote(h1_o.at[rows], h1_o.at[rows], hs.at[b], hr.at[b], mate)

    def c_got(b):
        rows = pl.ds(aligned((1 - c) * 512 + b * 128, 128), 128)
        return remote(c_o.at[rows], c_o.at[rows], fs.at[b], fr.at[b], mate)

    for b in range(4):
        pltpu.make_async_copy(x_in.at[0], x_o.at[b * 128 : (b + 1) * 128], xr.at[b]).wait()
        xhat, _ = norm_parts(x_o[b * 128 : (b + 1) * 128].astype(F32))
        h1_o[pl.ds(aligned(c * 512 + b * 128, 128), 128)] = (xhat * gain_one + bias_one).astype(BF)
        h1_copy(b).start()

    for copy in seg_out:
        copy.wait()
    own_seg, own_flag = seg_in[pl.ds(z, 1), :], flag_in[pl.ds(z, 1), :]
    far_seg, far_flag = seg_got[0, pl.ds(z, 1), :], seg_got[1, pl.ds(z, 1), :]
    near = jnp.where(c == xl, 1, 0)
    seg_row = jnp.where(near == 1, own_seg, far_seg).astype(F32)
    flag_row = jnp.where(near == 1, own_flag, far_flag)
    key_row = jnp.where(flag_row == 0, seg_row, -1.0)
    seg_o[...] = jnp.concatenate([seg_row, key_row, jnp.zeros((6, 1024), F32)], axis=0)
    seg_col = jnp.broadcast_to(seg_row, (128, 1024)).T
    for i, ref in enumerate((b0, b1, b2, b3)):
        w0, w1 = window(i)
        rows = lax.broadcasted_iota(jnp.int32, (BLOCK, w1 - w0), 0) + i * BLOCK
        cols = lax.broadcasted_iota(jnp.int32, (BLOCK, w1 - w0), 1) + w0
        same = seg_col[i * BLOCK : (i + 1) * BLOCK, 0:1] == key_row[:, w0:w1]
        ref[...] = jnp.where((same & (cols <= rows)) | (rows == cols), 0.0, MASKED)
    lse_acc[...] = jnp.zeros_like(lse_acc)

    for load in loads[:3]:
        load.wait()
    zero = jnp.zeros((1, 512), F32)
    heads = pl.ds(aligned(c * 512, 512), 512)
    bias = jnp.concatenate([par[2:3, heads], zero, par[3:4, heads]], axis=1)

    def project(first):
        def body(n, carry):
            rows = pl.ds(aligned(first + n * BLOCK, BLOCK), BLOCK)
            qkv_o[rows, :] = (dot_nn(h1_o[rows, :], wq[...]) + bias).astype(BF)
            return carry

        lax.fori_loop(0, 2, body, 0)

    project(c * 512)
    for b in range(4):
        h1_got(b).wait_recv()
    project((1 - c) * 512)

    for b in range(4):
        pltpu.make_async_copy(
            c_in.at[0], c_o.at[pl.ds(aligned(c * 512 + b * 128, 128), 128)], cr.at[b]
        ).wait()
        c_copy(b).start()

    lane = lax.broadcasted_iota(jnp.int32, (BLOCK, 128), 1)

    def ctx_copy(p):
        return remote(
            ctxh_o.at[pl.ds(aligned((1 - c) * 512, 512), 512), pl.ds(aligned(p * 128, 128), 128)],
            ctxp_o.at[:, pl.ds(aligned(c * 512 + p * 128, 128), 128)],
            ts.at[p], tr.at[p], mate,
        )

    def attend(p, carry):
        lo = aligned(p * 128, 128)
        for i, ref in enumerate((b0, b1, b2, b3)):
            w0, w1 = window(i)
            rows = slice(i * BLOCK, (i + 1) * BLOCK)
            query = qkv_o[rows, pl.ds(lo, 128)] * jnp.asarray(0.125, BF)
            keys = qkv_o[w0:w1, pl.ds(aligned(512 + lo, 128), 128)]
            values = qkv_o[w0:w1, pl.ds(aligned(1024 + lo, 128), 128)]
            outs = []
            lses = lse_acc[rows, :]
            for h in range(2):
                mine = (lane < 64) if h == 0 else (lane >= 64)
                scores = dot_nt(jnp.where(mine, query, jnp.zeros_like(query)), keys) + ref[...]
                top = jnp.max(scores, axis=-1, keepdims=True)
                expo = jnp.exp(scores - top)
                total = jnp.sum(expo, axis=-1, keepdims=True)
                outs.append(dot_nn(expo.astype(BF), values) * (1.0 / total))
                lses = jnp.where(lane == 2 * p + h, top + jnp.log(total), lses)
            lse_acc[rows, :] = lses
            ctxh_o[rows, pl.ds(lo, 128)] = jnp.where(lane < 64, outs[0], outs[1]).astype(BF)
        ctx_copy(p).start()
        ctxp_o[:, pl.ds(aligned(c * 512 + lo, 128), 128)] = ctxh_o[pl.ds(aligned(c * 512, 512), 512), pl.ds(lo, 128)]
        return carry

    lax.fori_loop(0, 4, attend, 0)
    lse_o[...] = lse_acc[...].T[0:16, :]

    loads[3].wait()
    for p in range(4):
        remote(
            ctxh_o.at[pl.ds(aligned((1 - c) * 512, 512), 512), pl.ds(p * 128, 128)],
            ctxp_o.at[:, pl.ds(aligned((1 - c) * 512 + p * 128, 128), 128)],
            ts.at[p], tr.at[p], mate,
        ).wait_recv()

    def h2_copy(n):
        rows = pl.ds(aligned(c * 512 + n * BLOCK, BLOCK), BLOCK)
        return remote(h2_o.at[rows], h2_o.at[rows], gs.at[n], gr.at[n], mate)

    def h2_got(n):
        rows = pl.ds(aligned((1 - c) * 512 + n * BLOCK, BLOCK), BLOCK)
        return remote(h2_o.at[rows], h2_o.at[rows], gs.at[n], gr.at[n], mate)

    def output(n, carry):
        rows = pl.ds(aligned(n * BLOCK, BLOCK), BLOCK)
        resid = x_o[rows, :].astype(F32) + (dot_nn(ctxp_o[rows, :], wo[...]) + par[4:5, :])
        resid_o[rows, :] = resid
        xhat, _ = norm_parts(resid)
        h2_o[pl.ds(aligned(c * 512 + n * BLOCK, BLOCK), BLOCK), :] = (xhat * par[5:6, :] + par[6:7, :]).astype(BF)
        h2_copy(n).start()
        return carry

    lax.fori_loop(0, 2, output, 0)

    exchange_sent(place, x_src, x_dst, xs, xr)
    exchange_sent(place, c_src, c_dst, cs, cr)
    for b in range(4):
        h1_copy(b).wait_send()
        c_copy(b).wait_send()
        c_got(b).wait_recv()
        ctx_copy(b).wait_send()
    for n in range(2):
        h2_copy(n).wait_send()
        h2_got(n).wait_recv()


def vmem(n=None):
    return pl.BlockSpec(memory_space=pltpu.VMEM)


def anywhere():
    return pl.BlockSpec(memory_space=pl.ANY)


def dma(*shape):
    return pltpu.SemaphoreType.DMA(shape)


def shaped(shape, dtype):
    return jax.ShapeDtypeStruct(shape, dtype)


def run_forward(x, cot, seg, flags, par, wqkv, wout):
    outs = (
        shaped((512, 1024), F32), shaped((1024, 1024), BF), shaped((1024, 1024), BF), shaped((1024, 1024), BF),
        shaped((1024, 1536), BF), shaped((512, 1024), BF), shaped((1024, 512), BF), shaped((16, 1024), F32),
        shaped((8, 1024), F32), shaped((512, 1024), BF),
    )
    return pl.pallas_call(
        forward_kernel,
        out_shape=outs,
        in_specs=[anywhere(), anywhere(), vmem(), vmem(), vmem(), anywhere(), anywhere()],
        out_specs=tuple(vmem() for _ in outs),
        scratch_shapes=[
            pltpu.VMEM((1024, 1536), BF), pltpu.VMEM((1024, 1024), BF), pltpu.VMEM((2, 4, 1024), jnp.int32),
            pltpu.VMEM((256, 256), F32), pltpu.VMEM((256, 512), F32), pltpu.VMEM((256, 768), F32),
            pltpu.VMEM((256, 768), F32), pltpu.VMEM((1024, 128), F32),
            dma(4), dma(4), dma(4), dma(4), dma(4), dma(4), dma(4), dma(4), dma(4), dma(4), dma(2), dma(2), dma(2),
            dma(2), dma(4),
        ],
        compiler_params=pltpu.CompilerParams(collective_id=0, has_side_effects=True, vmem_limit_bytes=VMEM_LIMIT),
        name="forward",
    )(x, cot, seg, flags, par, wqkv, wout)


def middle_kernel(
    h2, cot, resid, ctxp, par, wup, wdown, wout,
    lout_o, dres_o, dctx_o, bup_o, bdown_o, bout_o, small_o,
    wu, wd, h2t, act_s, dup_s, down_acc, dh_acc, dh_send, dh_got, dn_send, dn_got, wo_send, wo_got, dc_send, ctxt, dat,
    us, ds, es, er,
):
    place = Place()
    c = place.c
    mate = place.partner("c")

    def up_load(t):
        return pltpu.make_async_copy(
            wup.at[:, pl.ds(aligned((2 * t + c) * 256, 256), 256)], wu.at[t], us.at[t]
        )

    def down_load(t):
        return pltpu.make_async_copy(wdown.at[pl.ds(aligned((2 * t + c) * 256, 256), 256)], wd.at[t], ds.at[t])

    for t in range(8):
        up_load(t).start()
        down_load(t).start()
    greet(place, [mate], False)

    transpose_features(h2, h2t)
    small_o[...] = jnp.zeros_like(small_o)

    def tile(t, carry):
        up_load(t).wait()
        down_load(t).wait()
        col = 2 * t + c
        up_bias = par[pl.ds(8 + lax.div(col, jnp.int32(4)), 1), pl.ds(aligned(lax.rem(col, jnp.int32(4)) * 256, 256), 256)]
        dbias = jnp.zeros((1, 256), F32)
        for b in range(4):
            rows = slice(b * BLOCK, (b + 1) * BLOCK)
            u = dot_nn(h2[rows, :], wu[t]) + up_bias
            dact = dot_nt(cot[rows, :], wd[t])
            square = u * u
            th = jnp.tanh(GELU * u * (1.0 + CUBIC * square))
            act_s[rows, :] = (0.5 * u * (1.0 + th)).astype(BF)
            slope = 0.5 * (1.0 + th) + 0.5 * u * (1.0 - th * th) * (GELU * (1.0 + (3.0 * CUBIC) * square))
            dup = (dact * slope).astype(BF)
            dup_s[rows, :] = dup
            dbias = dbias + jnp.sum(dup.astype(F32), axis=0, keepdims=True)
        small_o[pl.ds(8 + lax.div(col, jnp.int32(4)), 1), pl.ds(aligned(lax.rem(col, jnp.int32(4)) * 256, 256), 256)] = dbias

        xh, y = lax.div(t, jnp.int32(4)), lax.rem(t, jnp.int32(4))
        y1 = lax.div(y, jnp.int32(2))
        y0 = lax.rem(y + y1, jnp.int32(2))
        grad = dot_tn(act_s[...], cot[...]).astype(BF)
        for s in range(8):
            sx, sz = s >> 2, s & 3
            x0 = lax.rem(xh + sx, jnp.int32(2))
            code = xh * 32 + y1 * 16 + (sz >> 1) * 8 + x0 * 4 + y0 * 2 + ((sz & 1) ^ (sz >> 1))
            for p0, p1, o in DOWN_GROUPS:
                slot = turned_by(code, 1 << o)
                for j in range(p0, p1):
                    bdown_o[j, slot] = grad[s * 32 : (s + 1) * 32, j * 128 : (j + 1) * 128]

        powers = []
        for j in range(2):
            p = 2 * t + j
            o = lax.div(p, jnp.int32(3)) + lax.div(p, jnp.int32(14)) - lax.div(p, jnp.int32(15))
            powers.append(lax.shift_left(jnp.int32(1), o))
        for b in range(4):
            grad = dot_nn(h2t[b * 256 : (b + 1) * 256, :], dup_s[...]).astype(BF)
            for s in range(16):
                code = natural_code(b * 16 + s)
                for j in range(2):
                    bup_o[2 * t + j, turned_by(jnp.int32(code), powers[j])] = grad[
                        s * 16 : (s + 1) * 16, j * 128 : (j + 1) * 128
                    ]

        @pl.when(t == 0)
        def _():
            for b in range(4):
                rows = slice(b * BLOCK, (b + 1) * BLOCK)
                down_acc[rows, :] = dot_nn(act_s[rows, :], wd[t])
                dh_acc[rows, :] = dot_nt(dup_s[rows, :], wu[t])

        @pl.when(t > 0)
        def _():
            for b in range(4):
                rows = slice(b * BLOCK, (b + 1) * BLOCK)
                down_acc[rows, :] = down_acc[rows, :] + dot_nn(act_s[rows, :], wd[t])
                dh_acc[rows, :] = dh_acc[rows, :] + dot_nt(dup_s[rows, :], wu[t])

        return carry

    lax.fori_loop(0, 8, tile, 0)

    own = pl.ds(aligned(c * 512, 512), 512)
    far = pl.ds(aligned((1 - c) * 512, 512), 512)
    dh_send[...] = dh_acc[far, :].astype(BF)
    dh_copy = remote(dh_send, dh_got, es.at[0], er.at[0], mate)
    dh_copy.start()
    dn_send[...] = down_acc[far, :].astype(BF)
    dn_copy = remote(dn_send, dn_got, es.at[1], er.at[1], mate)
    dn_copy.start()

    transpose_features(ctxp, ctxt)

    dh_copy.wait()

    def norm_back(n, sums):
        gain_sum, bias_sum, out_sum, down_sum = sums
        rows = pl.ds(aligned(n * 128, 128), 128)
        mine = pl.ds(aligned(c * 512 + n * 128, 128), 128)
        xhat, rstd = norm_parts(resid[rows, :])
        dn = dh_acc[mine, :] + dh_got[rows, :].astype(F32)
        e = dn * par[5:6, :]
        cf = cot[mine, :].astype(F32)
        dres = cf + rstd * (
            e - jnp.mean(e, axis=-1, keepdims=True) - xhat * jnp.mean(e * xhat, axis=-1, keepdims=True)
        )
        dres_o[rows, :] = dres
        low = dres.astype(BF)
        dat[rows, :] = low
        return (
            gain_sum + jnp.sum(dn * xhat, axis=0, keepdims=True),
            bias_sum + jnp.sum(dn, axis=0, keepdims=True),
            out_sum + jnp.sum(low.astype(F32), axis=0, keepdims=True),
            down_sum + jnp.sum(cf, axis=0, keepdims=True),
        )

    nothing = jnp.zeros((1, 1024), F32)
    gain_sum, bias_sum, out_sum, down_sum = lax.fori_loop(0, 4, norm_back, (nothing,) * 4)
    small_o[5:6, :] = gain_sum
    small_o[6:7, :] = bias_sum
    small_o[4:5, :] = out_sum
    small_o[7:8, :] = down_sum

    dc_send[...] = dot_nt(dat[...], wout[far, :]).astype(BF)
    dc_copy = remote(dc_send, dctx_o.at[own], es.at[2], er.at[2], mate)
    dc_copy.start()

    def out_grad(cols, dst):
        for b in range(4):
            grad = dot_nn(ctxt[b * 256 : (b + 1) * 256, :], dat[:, cols]).astype(BF)
            for s in range(16):
                code = natural_code(b * 16 + s)
                for j in range(4):
                    dst[j, turned(code, j)] = grad[s * 16 : (s + 1) * 16, j * 128 : (j + 1) * 128]

    out_grad(far, wo_send)
    wo_copy = remote(wo_send, wo_got, es.at[3], er.at[3], mate)
    wo_copy.start()
    dctx_o[own, :] = dot_nt(dat[...], wout[own, :]).astype(BF)
    out_grad(own, bout_o)
    dn_copy.wait()
    for n in range(4):
        rows = slice(n * 128, (n + 1) * 128)
        mine = pl.ds(aligned(c * 512 + n * 128, 128), 128)
        down = down_acc[mine, :] + dn_got[rows, :].astype(F32) + par[7:8, :]
        lout_o[rows, :] = (resid[rows, :] + down).astype(BF)
    wo_copy.wait()
    bout_o[...] = bout_o[...] + wo_got[...]
    dc_copy.wait_send()
    remote(dc_send, dctx_o.at[far], es.at[2], er.at[2], mate).wait_recv()


def run_middle(h2, cot, resid, ctxp, par, wup, wdown, wout):
    outs = (
        shaped((512, 1024), BF), shaped((512, 1024), F32), shaped((1024, 512), BF), shaped((16, 64, 16, 128), BF),
        shaped((8, 64, 32, 128), BF), shaped((4, 64, 16, 128), BF), shaped((16, 1024), F32),
    )
    return pl.pallas_call(
        middle_kernel,
        out_shape=outs,
        in_specs=[vmem(), vmem(), vmem(), vmem(), vmem(), anywhere(), anywhere(), vmem()],
        out_specs=tuple(vmem() for _ in outs),
        scratch_shapes=[
            pltpu.VMEM((8, 1024, 256), BF), pltpu.VMEM((8, 256, 1024), BF), pltpu.VMEM((1024, 1024), BF),
            pltpu.VMEM((1024, 256), BF), pltpu.VMEM((1024, 256), BF), pltpu.VMEM((1024, 1024), F32),
            pltpu.VMEM((1024, 1024), F32), pltpu.VMEM((512, 1024), BF), pltpu.VMEM((512, 1024), BF),
            pltpu.VMEM((512, 1024), BF), pltpu.VMEM((512, 1024), BF), pltpu.VMEM((4, 64, 16, 128), BF),
            pltpu.VMEM((4, 64, 16, 128), BF), pltpu.VMEM((512, 512), BF), pltpu.VMEM((1024, 512), BF),
            pltpu.VMEM((512, 1024), BF), dma(8), dma(8), dma(4), dma(4),
        ],
        compiler_params=pltpu.CompilerParams(collective_id=1, has_side_effects=True, vmem_limit_bytes=VMEM_LIMIT),
        name="middle",
    )(h2, cot, resid, ctxp, par, wup, wdown, wout)


MAIN = tuple(
    (which, p0, p1, o)
    for which, groups in ((0, UP_GROUPS), (1, DOWN_GROUPS), (2, OUT_GROUPS))
    for p0, p1, o in groups
)
EVENTS = {(1, 3): 1, (2, 1): 2, (2, 3): 3, (3, 0): 4, (3, 1): 5, (3, 2): 6}


def backward_kernel(
    qkv, dctx, ctxh, lse, seg, h1, x_own, dres, small_in, par, lout, bup_in, bdown_in, bout_in, wqkv,
    lout_o, gin_o, gqkv_o, gout_o, gup_o, gdown_o, small_o,
    wq, h1t, dqkv, dk_acc, dv_acc, drow, t0, t1, t2, t3, bup, bdown, bout, bqkv, rup, rdown, rout, rqkv,
    fin_up, fin_out, fin_qkv, far_up, far_out, far_qkv, dh_send, dh_got, dh_own, gin_s,
    sm, sm_first, sm_acc, sm_got, sm_last,
    ws, ms, mr, q1s, q1r, qs, qr, ls, lr, gs, gr, es, er, ps, pr,
):
    place = Place()
    c, xl, z = place.c, place.xl, place.z
    mate = place.partner("c")
    loads = [
        pltpu.make_async_copy(bup_in, bup, ws.at[0]),
        pltpu.make_async_copy(bdown_in, bdown, ws.at[1]),
        pltpu.make_async_copy(bout_in, bout, ws.at[2]),
    ]
    for p in range(4):
        for j in range(3):
            loads.append(
                pltpu.make_async_copy(
                    wqkv.at[:, pl.ds(aligned(j * 1024 + c * 512 + p * 128, 128), 128)],
                    wq.at[:, pl.ds(p * 384 + j * 128, 128)],
                    ws.at[3 + p * 3 + j],
                )
            )
    for load in loads:
        load.start()
    peers = [mate] + [place.partner(d) for d in DIMS] + [place.ring(a, s) for a in "xyz" for s in (1, 2, 3)]
    greet(place, peers, True)

    def l_src(r):
        return lout.at[pl.ds(r * 128, 128)]

    def l_dst(r):
        return lout_o.at[z]

    exchange_start(place, l_src, l_dst, l_dst, ls, lr)
    for load in loads[:3]:
        load.wait()
    bufs, gots = (bup, bdown, bout), (rup, rdown, rout)

    def main_copy(k, n):
        which, p0, p1, o = MAIN[n]
        return scatter_copy(place, k, bufs[which], gots[which], (slice(p0, p1),), o, ms, mr, (k - 1, n))

    def main_start(k):
        for n in range(len(MAIN)):
            main_copy(k, n).start()

    def main_finish(k):
        for n in range(len(MAIN)):
            main_copy(k, n).wait()
        if k < 6:
            for which, p0, p1, o in MAIN:
                for p in range(p0, p1):
                    scatter_add(place, k, bufs[which], gots[which], (p,), o)

    main_start(1)

    key_col = jnp.broadcast_to(seg[1:2, :], (128, 1024)).T
    for i, ref in enumerate((t0, t1, t2, t3)):
        w0, w1 = window(i)
        rows = lax.broadcasted_iota(jnp.int32, (w1 - w0, BLOCK), 0) + w0
        cols = lax.broadcasted_iota(jnp.int32, (w1 - w0, BLOCK), 1) + i * BLOCK
        same = key_col[w0:w1, 0:1] == seg[0:1, i * BLOCK : (i + 1) * BLOCK]
        ref[...] = jnp.where((same & (rows <= cols)) | (rows == cols), 0.0, MASKED)
    transpose_features(h1, h1t)
    sm[...] = small_in[...]

    lane = lax.broadcasted_iota(jnp.int32, (BLOCK, 128), 1)
    head_of = lax.broadcasted_iota(jnp.int32, (16, 128), 1)
    row_of = lax.broadcasted_iota(jnp.int32, (16, 128), 0)
    pick = jnp.where(lax.div(head_of, jnp.int32(64)) == row_of, 1.0, 0.0).astype(BF)

    def final_sum(buf, got, piece, o):
        off = offset_before(place, o, 7)
        return buf[piece, off].astype(F32) + got[piece, 62].astype(F32)

    def far_rows(n):
        return pl.ds(aligned((1 - c) * 8, 8), 8)

    def far_copy(src, dst, at):
        return remote(src.at[pl.ds(aligned((1 - c) * 8, 8), 8)], dst, es.at[at], er.at[at], mate)

    def main_last():
        for p0, p1, o in UP_GROUPS:
            for p in range(p0, p1):
                fin_up[:, p * 128 : (p + 1) * 128] = final_sum(bup, rup, p, o)
        far_copy(fin_up, far_up, 0).start()
        for p0, p1, o in OUT_GROUPS:
            fin_out[:, p0 * 128 : (p0 + 1) * 128] = final_sum(bout, rout, p0, o)
        far_copy(fin_out, far_out, 1).start()
        for p0, p1, o in DOWN_GROUPS:
            for p in range(p0, p1):
                gdown_o[:, p * 128 : (p + 1) * 128] = final_sum(bdown, rdown, p, o)

    def first_copy(p, j):
        o = (3 * p + j) % 6
        return scatter_copy(place, 1, bqkv, rqkv, (o, p // 2), o, q1s, q1r, p * 3 + j)

    def pair(p, carry):
        lo = aligned(p * 128, 128)
        prod = (dctx[:, pl.ds(lo, 128)].astype(F32) * ctxh[:, pl.ds(lo, 128)].astype(F32)).astype(BF)
        drow[...] = dot_nt(pick, prod)
        dk_acc[...] = jnp.zeros_like(dk_acc)
        dv_acc[...] = jnp.zeros_like(dv_acc)
        at = p * 384
        for i, ref in enumerate((t0, t1, t2, t3)):
            w0, w1 = window(i)
            rows = slice(i * BLOCK, (i + 1) * BLOCK)
            query = qkv[rows, pl.ds(lo, 128)] * jnp.asarray(0.125, BF)
            keys = qkv[w0:w1, pl.ds(aligned(512 + lo, 128), 128)]
            values = qkv[w0:w1, pl.ds(aligned(1024 + lo, 128), 128)]
            grad = dctx[rows, pl.ds(lo, 128)]
            dq = []
            for h in range(2):
                mine = (lane < 64) if h == 0 else (lane >= 64)
                query_h = jnp.where(mine, query, jnp.zeros_like(query))
                grad_h = jnp.where(mine, grad, jnp.zeros_like(grad))
                scores = dot_nt(keys, query_h) + ref[...]
                probs = jnp.exp(scores - lse[pl.ds(2 * p + h, 1), rows])
                dprobs = dot_nt(values, grad_h)
                dscores = (probs * (dprobs - drow[h : h + 1, rows])).astype(BF)
                dv_acc[w0:w1, :] = dv_acc[w0:w1, :] + dot_nn(probs.astype(BF), grad_h)
                dk_acc[w0:w1, :] = dk_acc[w0:w1, :] + dot_nn(dscores, query_h)
                dq.append(dot_tn(dscores, keys))
            dqkv[rows, pl.ds(aligned(at, 128), 128)] = (jnp.where(lane < 64, dq[0], dq[1]) * 0.125).astype(BF)
            for (ep, ei), k in EVENTS.items():
                if ei == i:

                    @pl.when(p == ep)
                    def _(k=k):
                        main_finish(k)
                        if k < 6:
                            main_start(k + 1)
                        else:
                            main_last()

        dqkv[:, pl.ds(aligned(at + 128, 128), 128)] = dk_acc[...].astype(BF)
        dqkv[:, pl.ds(aligned(at + 256, 128), 128)] = dv_acc[...].astype(BF)
        own = pl.ds(aligned(c * 512 + lo, 128), 128)
        sm[2:3, own] = jnp.sum(dqkv[:, pl.ds(aligned(at, 128), 128)].astype(F32), axis=0, keepdims=True)
        sm[3:4, own] = jnp.sum(dqkv[:, pl.ds(aligned(at + 256, 128), 128)].astype(F32), axis=0, keepdims=True)
        base = 3 * lax.rem(p, jnp.int32(2))
        powers = [lax.shift_left(jnp.int32(1), base + j) for j in range(3)]
        for b in range(4):
            grad = dot_nn(h1t[b * 256 : (b + 1) * 256, :], dqkv[:, pl.ds(aligned(at, 128), 384)]).astype(BF)
            for s in range(16):
                code = natural_code(b * 16 + s)
                for j in range(3):
                    bqkv[base + j, lax.div(p, jnp.int32(2)), turned_by(jnp.int32(code), powers[j])] = grad[
                        s * 16 : (s + 1) * 16, j * 128 : (j + 1) * 128
                    ]
        for q in range(4):

            @pl.when(p == q)
            def _(q=q):
                for j in range(3):
                    first_copy(q, j).start()

        return carry

    lax.fori_loop(0, 4, pair, 0)

    def rest_copy(k, o):
        return scatter_copy(place, k, bqkv, rqkv, (o, slice(0, 2)), o, qs, qr, (k - 2, o))

    def rest_add(k):
        for o in range(6):
            for m in range(2):
                scatter_add(place, k, bqkv, rqkv, (o, m), o)

    def rest_start(k):
        for o in range(6):
            rest_copy(k, o).start()

    def rest_finish(k):
        for o in range(6):
            rest_copy(k, o).wait()

    for q in range(4):
        for j in range(3):
            first_copy(q, j).wait()
    rest_add(1)
    rest_start(2)

    for load in loads[3:]:
        load.wait()
    dh_copy = remote(dh_send, dh_got, es.at[2], er.at[2], mate)

    def far_half(n, carry):
        rows = pl.ds(aligned((1 - c) * 512 + n * BLOCK, BLOCK), BLOCK)
        dh_send[pl.ds(aligned(n * BLOCK, BLOCK), BLOCK), :] = dot_nt(dqkv[rows, :], wq[...]).astype(BF)
        return carry

    lax.fori_loop(0, 2, far_half, 0)
    dh_copy.start()
    rest_finish(2)
    rest_add(2)
    rest_start(3)

    def own_half(n, carry):
        rows = pl.ds(aligned(c * 512 + n * BLOCK, BLOCK), BLOCK)
        dh_own[pl.ds(aligned(n * BLOCK, BLOCK), BLOCK), :] = dot_nt(dqkv[rows, :], wq[...])
        return carry

    lax.fori_loop(0, 2, own_half, 0)
    rest_finish(3)
    rest_add(3)
    rest_start(4)
    dh_copy.wait()

    def norm_back(n, sums):
        gain_sum, bias_sum = sums
        rows = pl.ds(aligned(n * 128, 128), 128)
        xhat, rstd = norm_parts(x_own[rows, :].astype(F32))
        dn = dh_own[rows, :] + dh_got[rows, :].astype(F32)
        e = dn * par[0:1, :]
        gin_s[rows, :] = (
            dres[rows, :]
            + rstd * (e - jnp.mean(e, axis=-1, keepdims=True) - xhat * jnp.mean(e * xhat, axis=-1, keepdims=True))
        ).astype(BF)
        return (
            gain_sum + jnp.sum(dn * xhat, axis=0, keepdims=True),
            bias_sum + jnp.sum(dn, axis=0, keepdims=True),
        )

    nothing = jnp.zeros((1, 1024), F32)
    gain_sum, bias_sum = lax.fori_loop(0, 4, norm_back, (nothing,) * 2)
    sm[0:1, :] = gain_sum
    sm[1:2, :] = bias_sum

    own8 = pl.ds(aligned(c * 8, 8), 8)
    far8 = pl.ds(aligned((1 - c) * 8, 8), 8)
    small_copy = remote(sm.at[far8], sm_first, es.at[3], er.at[3], mate)
    small_copy.start()

    def g_src(r):
        return gin_s.at[pl.ds(r * 128, 128)]

    def g_dst(r):
        return gin_o.at[z]

    exchange_start(place, g_src, g_dst, g_dst, gs, gr)
    rest_finish(4)
    rest_add(4)
    rest_start(5)

    small_copy.wait()
    sm_acc[0] = sm[own8, :] + sm_first[...]

    def phase_copy(n, s):
        return remote(sm_acc.at[n], sm_got.at[n, s - 1], ps.at[n, s - 1], pr.at[n, s - 1], place.ring("zyx"[n], s))

    for n in range(3):
        for s in (1, 2, 3):
            phase_copy(n, s).start()
        if n < 2:
            rest_finish(5 + n)
            if n == 0:
                rest_add(5)
                rest_start(6)
            else:
                for o in range(6):
                    for m in range(2):
                        p, j = 2 * m + o // 3, o % 3
                        off = offset_before(place, o, 7)
                        fin_qkv[:, j * 512 + p * 128 : j * 512 + (p + 1) * 128] = bqkv[o, m, off].astype(F32) + rqkv[
                            o, m, 62
                        ].astype(F32)
                far_copy(fin_qkv, far_qkv, 4).start()
        for s in (1, 2, 3):
            phase_copy(n, s).wait()
        sm_acc[n + 1] = sm_acc[n] + sm_got[n, 0] + sm_got[n, 1] + sm_got[n, 2]

    last_copy = remote(sm_acc.at[3], sm_last, es.at[5], er.at[5], mate)
    last_copy.start()

    own8 = pl.ds(aligned(c * 8, 8), 8)
    far_copy(fin_up, far_up, 0).wait()
    for t in range(8):
        mine, theirs = fin_up[own8, t * 256 : (t + 1) * 256], far_up[:, t * 256 : (t + 1) * 256]
        gup_o[:, t * 512 : t * 512 + 256] = jnp.where(c == 0, mine, theirs)
        gup_o[:, t * 512 + 256 : t * 512 + 512] = jnp.where(c == 0, theirs, mine)
    far_copy(fin_out, far_out, 1).wait()
    mine, theirs = fin_out[own8, :], far_out[...]
    gout_o[:, 0:512] = jnp.where(c == 0, mine, theirs)
    gout_o[:, 512:1024] = jnp.where(c == 0, theirs, mine)
    far_copy(fin_qkv, far_qkv, 4).wait()
    for j in range(3):
        mine, theirs = fin_qkv[own8, j * 512 : (j + 1) * 512], far_qkv[:, j * 512 : (j + 1) * 512]
        gqkv_o[:, j * 1024 : j * 1024 + 512] = jnp.where(c == 0, mine, theirs)
        gqkv_o[:, j * 1024 + 512 : j * 1024 + 1024] = jnp.where(c == 0, theirs, mine)
    last_copy.wait()
    mine, theirs = sm_acc[3], sm_last[...]
    small_o[0:8, :] = jnp.where(c == 0, mine, theirs)
    small_o[8:16, :] = jnp.where(c == 0, theirs, mine)

    exchange_sent(place, l_src, l_dst, ls, lr)
    exchange_sent(place, g_src, g_dst, gs, gr)
    for b in range(4):
        pltpu.make_async_copy(lout.at[pl.ds(0, 128)], lout_o.at[b], lr.at[b]).wait()
        pltpu.make_async_copy(gin_s.at[pl.ds(0, 128)], gin_o.at[b], gr.at[b]).wait()


def run_backward(*args):
    outs = (
        shaped((4, 128, 1024), BF), shaped((4, 128, 1024), BF), shaped((8, 3072), F32), shaped((8, 1024), F32),
        shaped((8, 4096), F32), shaped((32, 1024), F32), shaped((16, 1024), F32),
    )
    v = pltpu.VMEM
    return pl.pallas_call(
        backward_kernel,
        out_shape=outs,
        in_specs=[vmem()] * 10 + [anywhere()] * 5,
        out_specs=(anywhere(), anywhere()) + (vmem(),) * 5,
        scratch_shapes=[
            v((1024, 1536), BF), v((1024, 1024), BF), v((1024, 1536), BF), v((1024, 128), F32), v((1024, 128), F32),
            v((16, 1024), F32), v((256, 256), F32), v((512, 256), F32), v((768, 256), F32), v((768, 256), F32),
            v((16, 64, 16, 128), BF), v((8, 64, 32, 128), BF), v((4, 64, 16, 128), BF), v((6, 2, 64, 16, 128), BF),
            v((16, 63, 16, 128), BF), v((8, 63, 32, 128), BF), v((4, 63, 16, 128), BF), v((6, 2, 63, 16, 128), BF),
            v((16, 2048), F32), v((16, 512), F32), v((16, 1536), F32), v((8, 2048), F32), v((8, 512), F32),
            v((8, 1536), F32), v((512, 1024), BF), v((512, 1024), BF), v((512, 1024), F32), v((512, 1024), BF),
            v((16, 1024), F32), v((8, 1024), F32), v((4, 8, 1024), F32), v((3, 3, 8, 1024), F32), v((8, 1024), F32),
            dma(15), dma(6, 16), dma(6, 16), dma(12), dma(12), dma(5, 6), dma(5, 6), dma(4), dma(4), dma(4), dma(4),
            dma(6), dma(6), dma(3, 3), dma(3, 3),
        ],
        compiler_params=pltpu.CompilerParams(collective_id=2, has_side_effects=True, vmem_limit_bytes=VMEM_LIMIT),
        name="backward",
    )(*args)


def on_device(
    block_input, segment_ids, padding_flags, cotangent, norm_one_gain, norm_one_bias, query_key_value, query_value_bias,
    out_weight, out_bias, norm_two_gain, norm_two_bias, up_weight, up_bias, down_weight, down_bias,
):
    par = jnp.concatenate(
        [
            norm_one_gain, norm_one_bias, query_value_bias, out_bias, norm_two_gain, norm_two_bias, down_bias, up_bias,
            jnp.zeros((4096,), BF),
        ]
    ).astype(F32).reshape(16, 1024)
    resid, h1, cot, h2, qkv, ctxp, ctxh, lse, seg, x_own = run_forward(
        block_input, cotangent, segment_ids, padding_flags, par, query_key_value, out_weight
    )
    lout, dres, dctx, bup, bdown, bout, small = run_middle(h2, cot, resid, ctxp, par, up_weight, down_weight, out_weight)
    lout, gin, gqkv, gout, gup, gdown, sums = run_backward(
        qkv, dctx, ctxh, lse, seg, h1, x_own, dres, small, par, lout, bup, bdown, bout, query_key_value
    )
    device = ((lax.axis_index("xh") * 4 + lax.axis_index("y")) * 2 + lax.axis_index("c")) * 8
    device = device + lax.axis_index("xl") * 4 + lax.axis_index("z")
    flat = sums.reshape(16 * 1024)

    def part(first, size):
        return lax.dynamic_slice(flat, (first * 1024 + device * size,), (size,))

    return (
        lout, gin, part(0, 8), part(1, 8), gqkv, part(2, 16), gout, part(4, 8), part(5, 8), part(6, 8), gup,
        part(8, 32), gdown, part(7, 8),
    )


def solution(mesh):
    wide = Mesh(mesh.devices.reshape(2, 4, 2, 2, 4), AXES)
    rows, seq = ("xh", "y", "c"), ("xl", "z")
    everything = rows + seq
    whole = P()
    return jax.shard_map(
        on_device,
        mesh=wide,
        in_specs=(P(rows, seq, None), P(rows, None), P(rows, None), P(rows, seq, None)) + (whole,) * 12,
        out_specs=(
            P(rows, seq, None), P(rows, seq, None), P(everything), P(everything), P(everything, None), P(everything),
            P(everything, None), P(everything), P(everything), P(everything), P(everything, None), P(everything),
            P(everything, None), P(everything),
        ),
        check_vma=False,
    )
```

```python
import jax
import jax.numpy as jnp
from jax import lax
from jax.experimental import pallas as pl
from jax.experimental.pallas import tpu as pltpu
from jax.sharding import Mesh, PartitionSpec as P

BF = jnp.bfloat16
F32 = jnp.float32
AXES = ("xh", "y", "c", "xl", "z")
BY_MESH = pl.DeviceIdType.MESH
DIMS = ("x1", "y1", "z1", "x0", "y0", "z0")
UP_ORDERS = (("y1", "y0", "x1", "z", "x0"), ("x1", "y0", "y1", "z", "x0"))
DOWN_GROUPS = (
    (0, 3, ("z1", "z0", "x0"), ("y", "x1")),
    (3, 6, ("z0", "x0", "z1"), ("y", "x1")),
    (6, 8, ("x0", "z1", "z0"), ("x1", "y")),
)
OUT_ORDERS = (("y", "x", "z"), ("x", "y", "z"), ("y", "z", "x"), ("y", "x", "z"))
QKV_ORDERS = (("x", "y", "z"), ("z", "x", "y"), ("y", "z", "x"))
BLOCK = 256
GELU = 0.7978845608028654
CUBIC = 0.044715
EPS = 1e-05
MASKED = -1e30
VMEM_LIMIT = 60 * 1024 * 1024


def dot_nn(a, b):
    return lax.dot_general(a, b, (((1,), (0,)), ((), ())), preferred_element_type=F32)


def dot_nt(a, b):
    return lax.dot_general(a, b, (((1,), (1,)), ((), ())), preferred_element_type=F32)


def dot_tn(a, b):
    return lax.dot_general(a, b, (((0,), (0,)), ((), ())), preferred_element_type=F32)


class Place:
    def __init__(self):
        self.xh, self.y, self.c, self.xl, self.z = (lax.axis_index(a) for a in AXES)
        two = jnp.int32(2)
        self.bits = {
            "x1": self.xh,
            "x0": lax.rem(self.xl + self.xh, two),
            "y1": lax.div(self.y, two),
            "y0": lax.rem(self.y + lax.div(self.y, two), two),
            "z1": lax.div(self.z, two),
            "z0": lax.rem(self.z + lax.div(self.z, two), two),
            "x": 2 * self.xh + self.xl,
            "y": self.y,
            "z": self.z,
        }

    def partner(self, name):
        xh, y, c, xl, z = self.xh, self.y, self.c, self.xl, self.z
        if name == "c":
            c = 1 - c
        elif name == "x0":
            xl = 1 - xl
        elif name == "x1":
            xh, xl = 1 - xh, 1 - xl
        elif name == "y0":
            y = y + 1 - 2 * lax.rem(y, jnp.int32(2))
        elif name == "y1":
            y = 3 - y
        elif name == "z0":
            z = z + 1 - 2 * lax.rem(z, jnp.int32(2))
        elif name == "z1":
            z = 3 - z
        return (xh, y, c, xl, z)

    def ring(self, axis, step):
        four, two = jnp.int32(4), jnp.int32(2)
        xh, y, c, xl, z = self.xh, self.y, self.c, self.xl, self.z
        if axis == "x":
            at = lax.rem(2 * xh + xl + step, four)
            xh, xl = lax.div(at, two), lax.rem(at, two)
        elif axis == "y":
            y = lax.rem(y + step, four)
        else:
            z = lax.rem(z + step, four)
        return (xh, y, c, xl, z)

    def exchange(self, r):
        return (self.xh, self.y, self.xl, self.c, jnp.int32(r))

    def is_self(self, r):
        return (self.c == self.xl) & (self.z == r)


def bits_of(s):
    xh, y, xl, z = s >> 5, (s >> 3) & 3, (s >> 2) & 1, s & 3
    return {
        "x1": xh, "y1": y >> 1, "z1": z >> 1, "x0": xl ^ xh, "y0": (y & 1) ^ (y >> 1), "z0": (z & 1) ^ (z >> 1),
        "x": 2 * xh + xl, "y": y, "z": z,
    }


def width(name):
    return 4 if len(name) == 1 else 2


def left_after(order, k):
    n = 1
    for name in order[k:]:
        n *= width(name)
    return n


def slot_of(s, order):
    bits, slot = bits_of(s), 0
    for name in order:
        slot = width(name) * slot + bits[name]
    return slot


def offset_before(place, order, k):
    off = jnp.int32(0)
    for j, name in enumerate(order[: k - 1]):
        off = off + place.bits[name] * left_after(order, j + 1)
    return off


def region(order, k):
    return sum((width(name) - 1) * left_after(order, j + 1) for j, name in enumerate(order[: k - 1]))


class Scatter:
    def __init__(self, place, k, order, buf, got, lead, sends, recvs, at):
        name = order[k - 1]
        n = left_after(order, k)
        first = offset_before(place, order, k)
        self.copies = []
        for s in range(1, width(name)):
            if width(name) == 2:
                peer, to = place.partner(name), 1 - place.bits[name]
            else:
                peer, to = place.ring(name, s), lax.rem(place.bits[name] + s, jnp.int32(4))
            self.copies.append(
                pltpu.make_async_remote_copy(
                    src_ref=buf.at[lead + (pl.ds(first + to * n, n),)],
                    dst_ref=got.at[lead + (pl.ds(region(order, k) + (s - 1) * n, n),)],
                    send_sem=sends.at[at + (s - 1,)],
                    recv_sem=recvs.at[at + (s - 1,)],
                    device_id=peer,
                    device_id_type=BY_MESH,
                )
            )

    def start(self):
        for copy in self.copies:
            copy.start()

    def wait(self):
        for copy in self.copies:
            copy.wait()


def scatter_sum(place, k, order, buf, got, lead):
    n = left_after(order, k)
    mine = lead + (pl.ds(offset_before(place, order, k + 1), n),)
    total = buf[mine].astype(F32)
    for s in range(1, width(order[k - 1])):
        total = total + got[lead + (pl.ds(region(order, k) + (s - 1) * n, n),)].astype(F32)
    return mine, total


def scatter_add(place, k, order, buf, got, lead):
    mine, total = scatter_sum(place, k, order, buf, got, lead)
    buf[mine] = total.astype(BF)


def scatter_last(place, order, buf, got, lead):
    _, total = scatter_sum(place, len(order), order, buf, got, lead)
    return total.reshape(total.shape[-2:])


def feature_rows(flat):
    parts = []
    for g in range(8):
        for c in range(2):
            parts.append(flat[(c * 8 + g) * 8 : (c * 8 + g + 1) * 8])
    return jnp.concatenate(parts, axis=0)


def transpose_features(src, dst):
    def body(f, carry):
        block = src[:, pl.ds(pl.multiple_of(f * 128, 128), 128)].astype(F32)
        dst[pl.ds(pl.multiple_of(f * 128, 128), 128), :] = feature_rows(block.T).astype(BF)
        return carry

    lax.fori_loop(0, 8, body, 0)


def norm_parts(v):
    center = v - jnp.mean(v, axis=-1, keepdims=True)
    rstd = lax.rsqrt(jnp.mean(center * center, axis=-1, keepdims=True) + EPS)
    return center * rstd, rstd


def aligned(v, m):
    return pl.multiple_of(v, m)


def window(i):
    return max(0, i - 2) * BLOCK, (i + 1) * BLOCK


def remote(src, dst, send, recv, device):
    return pltpu.make_async_remote_copy(
        src_ref=src, dst_ref=dst, send_sem=send, recv_sem=recv, device_id=device, device_id_type=BY_MESH
    )


def greet(place, devices, with_exchange):
    barrier = pltpu.get_barrier_semaphore()
    count = jnp.int32(len(devices))
    for d in devices:
        pl.semaphore_signal(barrier, inc=1, device_id=d, device_id_type=BY_MESH)
    if with_exchange:
        for r in range(4):

            @pl.when(jnp.logical_not(place.is_self(r)))
            def _(r=r):
                pl.semaphore_signal(barrier, inc=1, device_id=place.exchange(r), device_id_type=BY_MESH)

        count = count + 4 - jnp.where(place.c == place.xl, 1, 0)
    pl.semaphore_wait(barrier, count)


def exchange_start(place, src_of, dst_of, own_dst_of, sends, recvs):
    for r in range(4):
        own = place.is_self(r)

        @pl.when(own)
        def _(r=r):
            pltpu.make_async_copy(src_of(r), own_dst_of(r), recvs.at[place.z]).start()

        @pl.when(jnp.logical_not(own))
        def _(r=r):
            remote(src_of(r), dst_of(r), sends.at[r], recvs.at[place.z], place.exchange(r)).start()


def exchange_sent(place, src_of, dst_of, sends, recvs):
    for r in range(4):

        @pl.when(jnp.logical_not(place.is_self(r)))
        def _(r=r):
            remote(src_of(r), dst_of(r), sends.at[r], recvs.at[place.z], place.exchange(r)).wait_send()


def vmem(n=None):
    return pl.BlockSpec(memory_space=pltpu.VMEM)


def anywhere():
    return pl.BlockSpec(memory_space=pl.ANY)


def dma(*shape):
    return pltpu.SemaphoreType.DMA(shape)


def shaped(shape, dtype):
    return jax.ShapeDtypeStruct(shape, dtype)


def first_kernel(
    x_in, c_in, seg_in, flag_in, g1, b1_, bqv, bo, g2, b2_, bd, bu, wqkv, wout, wup, wdown,
    h1_o, qkv_o, x_o, ctxh_o, dres_o, dctx_o, lout_o, upleft_o, downleft_o, bout_o, lse_o, seg_o, par, small_o,
    hid, cot, qkv, x_own, ctxh, ctxp, resid, h2t, lse_acc, wq, wo, wu, wd, down_acc, dh_acc, act_s, dup_s, dat, lout, dctx,
    bup, rup, bdown, rdown, bout, upleft, downleft, seg_got,
    xs, xr, cs, cr, hs, hr, fs, fr, ts, tr, gs, gr, ss, sr, ws, us, ds, es, er, ups, upr, dns, dnr, os,
):
    place = Place()
    c, xl, z = place.c, place.xl, place.z
    mate = place.partner("c")
    own = pl.ds(aligned(c * 512, 512), 512)
    far = pl.ds(aligned((1 - c) * 512, 512), 512)
    loads = [
        pltpu.make_async_copy(
            wqkv.at[:, pl.ds(aligned(j * 1024 + c * 512, 512), 512)], wq.at[:, pl.ds(j * 512, 512)], ws.at[j]
        )
        for j in range(3)
    ]
    loads.append(pltpu.make_async_copy(wout, wo, ws.at[3]))

    def up_load(t):
        return pltpu.make_async_copy(
            wup.at[:, pl.ds(aligned((2 * t + c) * 256, 256), 256)], wu.at[lax.rem(t, jnp.int32(4))], us.at[t]
        )

    def down_load(t):
        return pltpu.make_async_copy(
            wdown.at[pl.ds(aligned((2 * t + c) * 256, 256), 256)], wd.at[lax.rem(t, jnp.int32(4))], ds.at[t]
        )

    def saves(n, src, dst):
        return pltpu.make_async_copy(src, dst, os.at[n])

    for load in loads:
        load.start()
    for t in range(4):
        up_load(jnp.int32(t)).start()
        down_load(jnp.int32(t)).start()
    greet(place, [mate] + [place.partner(d) for d in DIMS], True)

    def x_src(r):
        return x_in.at[r]

    def x_dst(r):
        return x_own.at[pl.ds(aligned(z * 128, 128), 128)]

    def c_src(r):
        return c_in.at[r]

    def c_dst(r):
        return cot.at[pl.ds(aligned(xl * 512 + z * 128, 128), 128)]

    exchange_start(place, x_src, x_dst, x_dst, xs, xr)
    seg_out = [remote(ref, seg_got.at[n], ss.at[n], sr.at[n], mate) for n, ref in enumerate((seg_in, flag_in))]
    for copy in seg_out:
        copy.start()
    for n, ref in enumerate((g1, b1_, bqv, bqv, bo, g2, b2_, bd, bu, bu, bu, bu)):
        first = {3: 1024, 9: 1024, 10: 2048, 11: 3072}.get(n, 0)
        par[n : n + 1, :] = ref[first : first + 1024].astype(F32).reshape(1, 1024)
    par[12:16, :] = jnp.zeros((4, 1024), F32)

    for copy in seg_out:
        copy.wait()
    own_seg, own_flag = seg_in[pl.ds(z, 1), :], flag_in[pl.ds(z, 1), :]
    far_seg, far_flag = seg_got[0, pl.ds(z, 1), :], seg_got[1, pl.ds(z, 1), :]
    near = jnp.where(c == xl, 1, 0)
    seg_row = jnp.where(near == 1, own_seg, far_seg).astype(F32)
    flag_row = jnp.where(near == 1, own_flag, far_flag)
    key_row = jnp.where(flag_row == 0, seg_row, -1.0)
    seg_o[...] = jnp.concatenate([seg_row, key_row, jnp.zeros((6, 1024), F32)], axis=0)
    seg_col = jnp.broadcast_to(seg_row, (128, 1024)).T
    for i in range(4):
        w0, w1 = window(i)
        rows = lax.broadcasted_iota(jnp.int32, (BLOCK, w1 - w0), 0) + i * BLOCK
        cols = lax.broadcasted_iota(jnp.int32, (BLOCK, w1 - w0), 1) + w0
        same = seg_col[i * BLOCK : (i + 1) * BLOCK, 0:1] == key_row[:, w0:w1]
        dh_acc[i * BLOCK : (i + 1) * BLOCK, 0 : w1 - w0] = jnp.where(
            (same & (cols <= rows)) | (rows == cols), 0.0, MASKED
        )
    lse_acc[...] = jnp.zeros_like(lse_acc)

    gain_one, bias_one = par[0:1, :], par[1:2, :]

    def block_copy(ref, b, mine, sends, recvs):
        half = c if mine else 1 - c
        rows = pl.ds(aligned(half * 512 + b * 128, 128), 128)
        return remote(ref.at[rows], ref.at[rows], sends.at[b], recvs.at[b], mate)

    for b in range(4):
        pltpu.make_async_copy(x_in.at[0], x_own.at[b * 128 : (b + 1) * 128], xr.at[b]).wait()
        xhat, _ = norm_parts(x_own[b * 128 : (b + 1) * 128].astype(F32))
        hid[pl.ds(aligned(c * 512 + b * 128, 128), 128)] = (xhat * gain_one + bias_one).astype(BF)
        block_copy(hid, b, True, hs, hr).start()
    exchange_start(place, c_src, c_dst, c_dst, cs, cr)
    saves(0, x_own, x_o).start()

    for load in loads[:3]:
        load.wait()
    zero = jnp.zeros((1, 512), F32)
    bias = jnp.concatenate([par[2:3, own], zero, par[3:4, own]], axis=1)

    def project(first):
        def body(n, carry):
            rows = pl.ds(aligned(first + n * BLOCK, BLOCK), BLOCK)
            qkv[rows, :] = (dot_nn(hid[rows, :], wq[...]) + bias).astype(BF)
            return carry

        lax.fori_loop(0, 2, body, 0)

    project(c * 512)
    for b in range(4):
        block_copy(hid, b, False, hs, hr).wait_recv()
    saves(1, hid, h1_o).start()
    project((1 - c) * 512)
    saves(2, qkv, qkv_o).start()

    lane = lax.broadcasted_iota(jnp.int32, (BLOCK, 128), 1)

    def ctx_copy(p, half):
        return remote(
            ctxh.at[far, pl.ds(aligned(p * 128, 128), 128)],
            ctxp.at[:, pl.ds(aligned(half * 512 + p * 128, 128), 128)],
            ts.at[p], tr.at[p], mate,
        )

    def attend(p, carry):
        lo = aligned(p * 128, 128)
        for i in range(4):
            w0, w1 = window(i)
            rows = slice(i * BLOCK, (i + 1) * BLOCK)
            query = qkv[rows, pl.ds(lo, 128)] * jnp.asarray(0.125, BF)
            keys = qkv[w0:w1, pl.ds(aligned(512 + lo, 128), 128)]
            values = qkv[w0:w1, pl.ds(aligned(1024 + lo, 128), 128)]
            outs = []
            lses = lse_acc[rows, :]
            for h in range(2):
                mine = (lane < 64) if h == 0 else (lane >= 64)
                scores = dot_nt(jnp.where(mine, query, jnp.zeros_like(query)), keys) + dh_acc[rows, 0 : w1 - w0]
                top = jnp.max(scores, axis=-1, keepdims=True)
                expo = jnp.exp(scores - top)
                total = jnp.sum(expo, axis=-1, keepdims=True)
                outs.append(dot_nn(expo.astype(BF), values) * (1.0 / total))
                lses = jnp.where(lane == 2 * p + h, top + jnp.log(total), lses)
            lse_acc[rows, :] = lses
            ctxh[rows, pl.ds(lo, 128)] = jnp.where(lane < 64, outs[0], outs[1]).astype(BF)

        @pl.when(p == 3)
        def _():
            saves(1, hid, h1_o).wait()
            saves(2, qkv, qkv_o).wait()
            for b in range(4):
                block_copy(hid, b, True, hs, hr).wait_send()

        ctx_copy(p, c).start()
        ctxp[:, pl.ds(aligned(c * 512 + lo, 128), 128)] = ctxh[own, pl.ds(lo, 128)]
        return carry

    lax.fori_loop(0, 4, attend, 0)
    saves(3, ctxh, ctxh_o).start()
    lse_o[...] = lse_acc[...].T[0:16, :]

    for b in range(4):
        pltpu.make_async_copy(c_in.at[0], cot.at[pl.ds(aligned(c * 512 + b * 128, 128), 128)], cr.at[b]).wait()
        block_copy(cot, b, True, fs, fr).start()

    loads[3].wait()
    for p in range(4):
        ctx_copy(p, 1 - c).wait_recv()

    def h2_copy(n, half):
        rows = pl.ds(aligned(half * 512 + n * BLOCK, BLOCK), BLOCK)
        return remote(hid.at[rows], hid.at[rows], gs.at[n], gr.at[n], mate)

    def output(n, carry):
        rows = pl.ds(aligned(n * BLOCK, BLOCK), BLOCK)
        res = x_own[rows, :].astype(F32) + (dot_nn(ctxp[rows, :], wo[...]) + par[4:5, :])
        resid[rows, :] = res
        xhat, _ = norm_parts(res)
        hid[pl.ds(aligned(c * 512 + n * BLOCK, BLOCK), BLOCK), :] = (xhat * par[5:6, :] + par[6:7, :]).astype(BF)
        h2_copy(n, c).start()
        return carry

    lax.fori_loop(0, 2, output, 0)
    small_o[...] = jnp.zeros_like(small_o)
    for n in range(2):
        h2_copy(n, 1 - c).wait_recv()
    transpose_features(hid, h2t)
    for b in range(4):
        block_copy(cot, b, False, fs, fr).wait_recv()

    def up_copy(k, t, j):
        return Scatter(place, k, UP_ORDERS[j], bup, rup, (t, j), ups, upr, (k - 1, t, j))

    def down_copy(k, t, g):
        p0, p1, order, _ = DOWN_GROUPS[g]
        return Scatter(place, k, order, bdown, rdown, (t, slice(p0, p1)), dns, dnr, (k - 1, t, g))

    def start(k, t):
        for j in range(2):
            up_copy(k, t, j).start()
        for g in range(3):
            down_copy(k, t, g).start()

    def tile_slot(t, rest):
        bits = {"x1": lax.div(t, jnp.int32(4)), "y": lax.rem(t, jnp.int32(4))}
        slot = jnp.int32(0)
        for name in rest:
            slot = width(name) * slot + bits[name]
        return slot

    def finish(k, t):
        for j in range(2):
            up_copy(k, t, j).wait()
        for g in range(3):
            down_copy(k, t, g).wait()
        for j, order in enumerate(UP_ORDERS):
            mine, total = scatter_sum(place, k, order, bup, rup, (t, j))
            if k < 3:
                bup[mine] = total.astype(BF)
            else:
                upleft[j, t] = total.astype(BF)
        for p0, p1, order, rest in DOWN_GROUPS:
            for p in range(p0, p1):
                mine, total = scatter_sum(place, k, order, bdown, rdown, (t, p))
                if k < 3:
                    bdown[mine] = total.astype(BF)
                else:
                    downleft[p, pl.ds(tile_slot(t, rest), 1)] = total.astype(BF)
        if k < 3:
            start(k + 1, t)

    def tile(t, carry):
        four = jnp.int32(4)
        ring = lax.rem(t, four)
        up_load(t).wait()
        down_load(t).wait()
        col = 2 * t + c
        up_row = 8 + lax.div(col, four)
        up_cols = pl.ds(aligned(lax.rem(col, four) * 256, 256), 256)
        up_bias = par[pl.ds(up_row, 1), up_cols]
        dbias = jnp.zeros((1, 256), F32)
        for b in range(4):
            rows = slice(b * BLOCK, (b + 1) * BLOCK)
            u = dot_nn(hid[rows, :], wu[ring]) + up_bias
            dact = dot_nt(cot[rows, :], wd[ring])
            square = u * u
            th = jnp.tanh(GELU * u * (1.0 + CUBIC * square))
            act_s[rows, :] = (0.5 * u * (1.0 + th)).astype(BF)
            slope = 0.5 * (1.0 + th) + 0.5 * u * (1.0 - th * th) * (GELU * (1.0 + (3.0 * CUBIC) * square))
            dup = (dact * slope).astype(BF)
            dup_s[rows, :] = dup
            dbias = dbias + jnp.sum(dup.astype(F32), axis=0, keepdims=True)
        small_o[pl.ds(up_row, 1), up_cols] = dbias

        for k in (3, 2, 1):

            @pl.when(t >= k + 1)
            def _(k=k):
                finish(k, t - k - 1)

        xh = lax.div(t, four)
        grad = dot_tn(act_s[...], cot[...]).astype(BF)
        for s in range(8):
            bits = bits_of(s)
            x0 = lax.rem(xh + (s >> 2), jnp.int32(2))
            for p0, p1, order, _ in DOWN_GROUPS:
                fixed = sum(bits[name] << (2 - n) for n, name in enumerate(order) if name != "x0")
                slot = fixed + x0 * (1 << (2 - order.index("x0")))
                for j in range(p0, p1):
                    bdown[t, j, slot] = grad[s * 32 : (s + 1) * 32, j * 128 : (j + 1) * 128]
        for b in range(4):
            grad = dot_nn(h2t[b * 256 : (b + 1) * 256, :], dup_s[...]).astype(BF)
            for s in range(16):
                for j, order in enumerate(UP_ORDERS):
                    bup[t, j, slot_of(b * 16 + s, order)] = grad[s * 16 : (s + 1) * 16, j * 128 : (j + 1) * 128]
        start(1, t)

        @pl.when(t == 0)
        def _():
            for b in range(4):
                rows = slice(b * BLOCK, (b + 1) * BLOCK)
                down_acc[rows, :] = dot_nn(act_s[rows, :], wd[ring])
                dh_acc[rows, :] = dot_nt(dup_s[rows, :], wu[ring])

        @pl.when(t > 0)
        def _():
            for b in range(4):
                rows = slice(b * BLOCK, (b + 1) * BLOCK)
                down_acc[rows, :] = down_acc[rows, :] + dot_nn(act_s[rows, :], wd[ring])
                dh_acc[rows, :] = dh_acc[rows, :] + dot_nt(dup_s[rows, :], wu[ring])

        @pl.when(t < 4)
        def _():
            up_load(t + 4).start()
            down_load(t + 4).start()

        return carry

    lax.fori_loop(0, 8, tile, 0)

    dh_send, dh_got = qkv.at[0:512, 0:1024], qkv.at[512:1024, 0:1024]
    dn_send, dn_got = wq.at[0:512, 0:1024], wq.at[512:1024, 0:1024]
    dc_send = qkv.at[0:512, 1024:1536]
    ctxt = wq.at[:, 1024:1536]
    wo_send, wo_got = bup.at[0:2], bup.at[2:4]
    dh_send[...] = dh_acc[far, :].astype(BF)
    dh_copy = remote(dh_send, dh_got, es.at[0], er.at[0], mate)
    dh_copy.start()
    dn_send[...] = down_acc[far, :].astype(BF)
    dn_copy = remote(dn_send, dn_got, es.at[1], er.at[1], mate)
    dn_copy.start()
    for k in (3, 2, 1):
        finish(k, 7 - k)

    transpose_features(ctxp, ctxt)
    dh_copy.wait()
    dn_copy.wait()

    def norm_back(n, sums):
        gain_sum, bias_sum, out_sum, down_sum = sums
        rows = pl.ds(aligned(n * 128, 128), 128)
        mine = pl.ds(aligned(c * 512 + n * 128, 128), 128)
        res = resid[rows, :]
        lout[rows, :] = (res + (down_acc[mine, :] + dn_got[rows, :].astype(F32) + par[7:8, :])).astype(BF)
        xhat, rstd = norm_parts(res)
        dn = dh_acc[mine, :] + dh_got[rows, :].astype(F32)
        e = dn * par[5:6, :]
        cf = cot[mine, :].astype(F32)
        dres = cf + rstd * (
            e - jnp.mean(e, axis=-1, keepdims=True) - xhat * jnp.mean(e * xhat, axis=-1, keepdims=True)
        )
        resid[rows, :] = dres
        low = dres.astype(BF)
        dat[rows, :] = low
        return (
            gain_sum + jnp.sum(dn * xhat, axis=0, keepdims=True),
            bias_sum + jnp.sum(dn, axis=0, keepdims=True),
            out_sum + jnp.sum(low.astype(F32), axis=0, keepdims=True),
            down_sum + jnp.sum(cf, axis=0, keepdims=True),
        )

    nothing = jnp.zeros((1, 1024), F32)
    gain_sum, bias_sum, out_sum, down_sum = lax.fori_loop(0, 4, norm_back, (nothing,) * 4)
    small_o[5:6, :] = gain_sum
    small_o[6:7, :] = bias_sum
    small_o[4:5, :] = out_sum
    small_o[7:8, :] = down_sum
    saves(4, resid, dres_o).start()
    saves(5, lout, lout_o).start()

    dc_send[...] = dot_nt(dat[...], wo[far, :]).astype(BF)
    dc_copy = remote(dc_send, dctx.at[own], es.at[2], er.at[2], mate)
    dc_copy.start()
    for k in (3, 2, 1):
        finish(k, 8 - k)

    def out_grad(cols, dst, lead):
        for b in range(4):
            grad = dot_nn(ctxt[b * 256 : (b + 1) * 256, :], dat[:, cols]).astype(BF)
            for s in range(16):
                for j, order in enumerate(OUT_ORDERS):
                    dst[lead(j) + (slot_of(b * 16 + s, order),)] = grad[s * 16 : (s + 1) * 16, j * 128 : (j + 1) * 128]

    out_grad(far, wo_send, lambda j: (j // 2, j % 2))
    wo_copy = remote(wo_send, wo_got, es.at[3], er.at[3], mate)
    wo_copy.start()
    dctx[own, :] = dot_nt(dat[...], wo[own, :]).astype(BF)
    for k in (3, 2):
        finish(k, 9 - k)
    out_grad(own, bout, lambda j: (j,))
    dc_copy.wait_send()
    remote(dc_send, dctx.at[far], es.at[2], er.at[2], mate).wait_recv()
    saves(6, dctx, dctx_o).start()
    finish(3, 7)
    saves(7, upleft, upleft_o).start()
    saves(8, downleft, downleft_o).start()
    wo_copy.wait()
    for j in range(4):
        bout[j] = bout[j] + wo_got[j // 2, j % 2]
    saves(9, bout, bout_o).start()

    exchange_sent(place, x_src, x_dst, xs, xr)
    exchange_sent(place, c_src, c_dst, cs, cr)
    for b in range(4):
        block_copy(cot, b, True, fs, fr).wait_send()
        ctx_copy(b, c).wait_send()
    for n in range(2):
        h2_copy(n, c).wait_send()
    saves(0, x_own, x_o).wait()
    saves(3, ctxh, ctxh_o).wait()
    saves(4, resid, dres_o).wait()
    saves(5, lout, lout_o).wait()
    saves(6, dctx, dctx_o).wait()
    saves(7, upleft, upleft_o).wait()
    saves(8, downleft, downleft_o).wait()
    saves(9, bout, bout_o).wait()


def run_first(*args):
    outs = (
        shaped((1024, 1024), BF), shaped((1024, 1536), BF), shaped((512, 1024), BF), shaped((1024, 512), BF),
        shaped((512, 1024), F32), shaped((1024, 512), BF), shaped((512, 1024), BF), shaped((2, 8, 8, 16, 128), BF),
        shaped((8, 8, 32, 128), BF), shaped((4, 64, 16, 128), BF), shaped((16, 1024), F32), shaped((8, 1024), F32),
        shaped((16, 1024), F32), shaped((16, 1024), F32),
    )
    v = pltpu.VMEM
    return pl.pallas_call(
        first_kernel,
        out_shape=outs,
        in_specs=[anywhere(), anywhere()] + [vmem()] * 10 + [anywhere()] * 4,
        out_specs=(anywhere(),) * 10 + (vmem(),) * 4,
        scratch_shapes=[
            v((1024, 1024), BF), v((1024, 1024), BF), v((1024, 1536), BF), v((512, 1024), BF), v((1024, 512), BF),
            v((512, 1024), BF), v((512, 1024), F32), v((1024, 1024), BF), v((1024, 128), F32), v((1024, 1536), BF),
            v((1024, 1024), BF), v((4, 1024, 256), BF), v((4, 256, 1024), BF), v((1024, 1024), F32),
            v((1024, 1024), F32), v((1024, 256), BF), v((1024, 256), BF), v((512, 1024), BF), v((512, 1024), BF),
            v((1024, 512), BF), v((8, 2, 64, 16, 128), BF), v((8, 2, 56, 16, 128), BF), v((8, 8, 8, 32, 128), BF),
            v((8, 8, 7, 32, 128), BF), v((4, 64, 16, 128), BF), v((2, 8, 8, 16, 128), BF), v((8, 8, 32, 128), BF),
            v((2, 4, 1024), jnp.int32),
            dma(4), dma(4), dma(4), dma(4), dma(4), dma(4), dma(4), dma(4), dma(4), dma(4), dma(2), dma(2), dma(2),
            dma(2), dma(4), dma(8), dma(8), dma(4), dma(4), dma(3, 8, 2, 1), dma(3, 8, 2, 1), dma(3, 8, 3, 1),
            dma(3, 8, 3, 1), dma(10),
        ],
        compiler_params=pltpu.CompilerParams(collective_id=0, has_side_effects=True, vmem_limit_bytes=VMEM_LIMIT),
        name="first",
    )(*args)


MAIN = (
    tuple((0, (j, slice(0, 8)), UP_ORDERS[j][3:]) for j in range(2))
    + tuple((1, (slice(p0, p1),), rest) for p0, p1, _, rest in DOWN_GROUPS)
    + tuple((2, (j,), order) for j, order in enumerate(OUT_ORDERS))
)
EVENTS = {(0, 3): 1, (1, 3): 2, (2, 3): 3}


def backward_kernel(
    qkv, dctx, ctxh, lse, seg, h1, x_own, dres, small_in, par, lout, upleft, downleft, bout_in, wqkv,
    lout_o, gin_o, gqkv_o, gout_o, gup_o, gdown_o, small_o,
    wq, h1t, dqkv, dk_acc, dv_acc, drow, t0, t1, t2, t3, bup, bdown, bout, bqkv, rup, rdown, rout, rqkv,
    fin_up, fin_out, fin_qkv, far_up, far_out, far_qkv, dh_send, dh_got, dh_own, gin_s,
    sm, sm_first, sm_acc, sm_got, sm_last,
    ws, ms, mr, qs, qr, ls, lr, gs, gr, hs, hr, es, er, ps, pr,
):
    place = Place()
    c, xl, z = place.c, place.xl, place.z
    mate = place.partner("c")
    loads = [
        pltpu.make_async_copy(upleft, bup, ws.at[0]),
        pltpu.make_async_copy(downleft, bdown, ws.at[1]),
        pltpu.make_async_copy(bout_in, bout, ws.at[2]),
    ]
    for p in range(4):
        for j in range(3):
            loads.append(
                pltpu.make_async_copy(
                    wqkv.at[:, pl.ds(aligned(j * 1024 + c * 512 + p * 128, 128), 128)],
                    wq.at[:, pl.ds(p * 384 + j * 128, 128)],
                    ws.at[3 + p * 3 + j],
                )
            )
    for load in loads:
        load.start()
    peers = [mate] + [place.partner(d) for d in DIMS] + [place.ring(a, s) for a in "xyz" for s in (1, 2, 3)]
    greet(place, peers, True)

    def l_src(r):
        return lout.at[pl.ds(r * 128, 128)]

    def l_dst(r):
        return lout_o.at[z]

    exchange_start(place, l_src, l_dst, l_dst, ls, lr)
    for load in loads[:3]:
        load.wait()
    bufs, gots = (bup, bdown, bout), (rup, rdown, rout)

    def steps(k):
        return [n for n, (_, _, order) in enumerate(MAIN) if k <= len(order)]

    def main_copy(k, n):
        which, lead, order = MAIN[n]
        return Scatter(place, k, order, bufs[which], gots[which], lead, ms, mr, (k - 1, n))

    def main_start(k):
        for n in steps(k):
            main_copy(k, n).start()

    def main_finish(k):
        for n in steps(k):
            main_copy(k, n).wait()
        for n in steps(k):
            which, lead, order = MAIN[n]
            if k < len(order):
                scatter_add(place, k, order, bufs[which], gots[which], lead)
        if k < 3:
            main_start(k + 1)
        if k == 2:
            left_last()
        if k == 3:
            out_last()

    main_start(1)

    key_col = jnp.broadcast_to(seg[1:2, :], (128, 1024)).T
    for i, ref in enumerate((t0, t1, t2, t3)):
        w0, w1 = window(i)
        rows = lax.broadcasted_iota(jnp.int32, (w1 - w0, BLOCK), 0) + w0
        cols = lax.broadcasted_iota(jnp.int32, (w1 - w0, BLOCK), 1) + i * BLOCK
        same = key_col[w0:w1, 0:1] == seg[0:1, i * BLOCK : (i + 1) * BLOCK]
        ref[...] = jnp.where((same & (rows <= cols)) | (rows == cols), 0.0, MASKED)
    transpose_features(h1, h1t)
    sm[...] = small_in[...]

    lane = lax.broadcasted_iota(jnp.int32, (BLOCK, 128), 1)
    head_of = lax.broadcasted_iota(jnp.int32, (16, 128), 1)
    row_of = lax.broadcasted_iota(jnp.int32, (16, 128), 0)
    pick = jnp.where(lax.div(head_of, jnp.int32(64)) == row_of, 1.0, 0.0).astype(BF)

    def far_copy(src, dst, at):
        return remote(src.at[pl.ds(aligned((1 - c) * 8, 8), 8)], dst, es.at[at], er.at[at], mate)

    def left_last():
        for j in range(2):
            for t in range(8):
                p = 2 * t + j
                fin_up[:, p * 128 : (p + 1) * 128] = scatter_last(place, UP_ORDERS[j][3:], bup, rup, (j, t))
        far_copy(fin_up, far_up, 0).start()
        for p0, p1, _, rest in DOWN_GROUPS:
            for p in range(p0, p1):
                gdown_o[:, p * 128 : (p + 1) * 128] = scatter_last(place, rest, bdown, rdown, (p,))

    def out_last():
        for j, order in enumerate(OUT_ORDERS):
            fin_out[:, j * 128 : (j + 1) * 128] = scatter_last(place, order, bout, rout, (j,))
        far_copy(fin_out, far_out, 1).start()

    def qkv_copy(k, p, j):
        return Scatter(place, k, QKV_ORDERS[j], bqkv, rqkv, (p, j), qs, qr, (k - 1, p, j))

    def qkv_start(k, p):
        for j in range(3):
            qkv_copy(k, p, j).start()

    def qkv_finish(k, p):
        for j in range(3):
            qkv_copy(k, p, j).wait()
        for j, order in enumerate(QKV_ORDERS):
            if k < 3:
                scatter_add(place, k, order, bqkv, rqkv, (p, j))
            else:
                fin_qkv[:, pl.ds(aligned(j * 512 + p * 128, 128), 128)] = scatter_last(place, order, bqkv, rqkv, (p, j))
        if k < 3:
            qkv_start(k + 1, p)

    def pair(p, carry):
        lo = aligned(p * 128, 128)
        prod = (dctx[:, pl.ds(lo, 128)].astype(F32) * ctxh[:, pl.ds(lo, 128)].astype(F32)).astype(BF)
        drow[...] = dot_nt(pick, prod)
        dk_acc[...] = jnp.zeros_like(dk_acc)
        dv_acc[...] = jnp.zeros_like(dv_acc)
        at = p * 384
        for i, ref in enumerate((t0, t1, t2, t3)):
            w0, w1 = window(i)
            rows = slice(i * BLOCK, (i + 1) * BLOCK)
            query = qkv[rows, pl.ds(lo, 128)] * jnp.asarray(0.125, BF)
            keys = qkv[w0:w1, pl.ds(aligned(512 + lo, 128), 128)]
            values = qkv[w0:w1, pl.ds(aligned(1024 + lo, 128), 128)]
            grad = dctx[rows, pl.ds(lo, 128)]
            dq = []
            for h in range(2):
                mine = (lane < 64) if h == 0 else (lane >= 64)
                query_h = jnp.where(mine, query, jnp.zeros_like(query))
                grad_h = jnp.where(mine, grad, jnp.zeros_like(grad))
                scores = dot_nt(keys, query_h) + ref[...]
                probs = jnp.exp(scores - lse[pl.ds(2 * p + h, 1), rows])
                dprobs = dot_nt(values, grad_h)
                dscores = (probs * (dprobs - drow[h : h + 1, rows])).astype(BF)
                dv_acc[w0:w1, :] = dv_acc[w0:w1, :] + dot_nn(probs.astype(BF), grad_h)
                dk_acc[w0:w1, :] = dk_acc[w0:w1, :] + dot_nn(dscores, query_h)
                dq.append(dot_tn(dscores, keys))
            dqkv[rows, pl.ds(aligned(at, 128), 128)] = (jnp.where(lane < 64, dq[0], dq[1]) * 0.125).astype(BF)
            for (ep, ei), k in EVENTS.items():
                if ei == i:

                    @pl.when(p == ep)
                    def _(k=k):
                        main_finish(k)

            if i == 2:
                for back in (3, 2):

                    @pl.when(p >= back)
                    def _(back=back):
                        qkv_finish(back - 1, p - back)

        dqkv[:, pl.ds(aligned(at + 128, 128), 128)] = dk_acc[...].astype(BF)
        dqkv[:, pl.ds(aligned(at + 256, 128), 128)] = dv_acc[...].astype(BF)
        own = pl.ds(aligned(c * 512 + lo, 128), 128)
        sm[2:3, own] = jnp.sum(dqkv[:, pl.ds(aligned(at, 128), 128)].astype(F32), axis=0, keepdims=True)
        sm[3:4, own] = jnp.sum(dqkv[:, pl.ds(aligned(at + 256, 128), 128)].astype(F32), axis=0, keepdims=True)
        for b in range(4):
            grad = dot_nn(h1t[b * 256 : (b + 1) * 256, :], dqkv[:, pl.ds(aligned(at, 128), 384)]).astype(BF)
            for s in range(16):
                for j, order in enumerate(QKV_ORDERS):
                    bqkv[p, j, slot_of(b * 16 + s, order)] = grad[s * 16 : (s + 1) * 16, j * 128 : (j + 1) * 128]
        qkv_start(1, p)
        return carry

    lax.fori_loop(0, 4, pair, 0)

    def tail(n):
        for k in (3, 2, 1):
            p = n + 2 - k
            if p < 4 and (k, p) not in ((2, 0), (1, 1), (1, 0)):
                qkv_finish(k, p)

    for load in loads[3:]:
        load.wait()

    def dh_copy(n):
        rows = pl.ds(aligned(n * BLOCK, BLOCK), BLOCK)
        return remote(dh_send.at[rows], dh_got.at[rows], hs.at[n], hr.at[n], mate)

    def far_half(n, carry):
        rows = pl.ds(aligned((1 - c) * 512 + n * BLOCK, BLOCK), BLOCK)
        dh_send[pl.ds(aligned(n * BLOCK, BLOCK), BLOCK), :] = dot_nt(dqkv[rows, :], wq[...]).astype(BF)
        dh_copy(n).start()
        return carry

    lax.fori_loop(0, 2, far_half, 0)
    tail(1)

    def own_half(n, carry):
        rows = pl.ds(aligned(c * 512 + n * BLOCK, BLOCK), BLOCK)
        dh_own[pl.ds(aligned(n * BLOCK, BLOCK), BLOCK), :] = dot_nt(dqkv[rows, :], wq[...])
        return carry

    lax.fori_loop(0, 2, own_half, 0)
    tail(2)
    for n in range(2):
        dh_copy(n).wait()

    def norm_back(n, sums):
        gain_sum, bias_sum = sums
        rows = pl.ds(aligned(n * 128, 128), 128)
        xhat, rstd = norm_parts(x_own[rows, :].astype(F32))
        dn = dh_own[rows, :] + dh_got[rows, :].astype(F32)
        e = dn * par[0:1, :]
        gin_s[rows, :] = (
            dres[rows, :]
            + rstd * (e - jnp.mean(e, axis=-1, keepdims=True) - xhat * jnp.mean(e * xhat, axis=-1, keepdims=True))
        ).astype(BF)
        return (
            gain_sum + jnp.sum(dn * xhat, axis=0, keepdims=True),
            bias_sum + jnp.sum(dn, axis=0, keepdims=True),
        )

    nothing = jnp.zeros((1, 1024), F32)
    gain_sum, bias_sum = lax.fori_loop(0, 4, norm_back, (nothing,) * 2)
    sm[0:1, :] = gain_sum
    sm[1:2, :] = bias_sum

    own8 = pl.ds(aligned(c * 8, 8), 8)
    far8 = pl.ds(aligned((1 - c) * 8, 8), 8)
    small_copy = remote(sm.at[far8], sm_first, es.at[3], er.at[3], mate)
    small_copy.start()

    def g_src(r):
        return gin_s.at[pl.ds(r * 128, 128)]

    def g_dst(r):
        return gin_o.at[z]

    exchange_start(place, g_src, g_dst, g_dst, gs, gr)
    tail(3)

    small_copy.wait()
    sm_acc[0] = sm[own8, :] + sm_first[...]

    def phase_copy(n, s):
        return remote(sm_acc.at[n], sm_got.at[n, s - 1], ps.at[n, s - 1], pr.at[n, s - 1], place.ring("zyx"[n], s))

    for n in range(3):
        for s in (1, 2, 3):
            phase_copy(n, s).start()
        if n < 2:
            tail(4 + n)
        if n == 1:
            far_copy(fin_qkv, far_qkv, 4).start()
        for s in (1, 2, 3):
            phase_copy(n, s).wait()
        sm_acc[n + 1] = sm_acc[n] + sm_got[n, 0] + sm_got[n, 1] + sm_got[n, 2]

    last_copy = remote(sm_acc.at[3], sm_last, es.at[5], er.at[5], mate)
    last_copy.start()

    own8 = pl.ds(aligned(c * 8, 8), 8)
    far_copy(fin_up, far_up, 0).wait()
    for t in range(8):
        mine, theirs = fin_up[own8, t * 256 : (t + 1) * 256], far_up[:, t * 256 : (t + 1) * 256]
        gup_o[:, t * 512 : t * 512 + 256] = jnp.where(c == 0, mine, theirs)
        gup_o[:, t * 512 + 256 : t * 512 + 512] = jnp.where(c == 0, theirs, mine)
    far_copy(fin_out, far_out, 1).wait()
    mine, theirs = fin_out[own8, :], far_out[...]
    gout_o[:, 0:512] = jnp.where(c == 0, mine, theirs)
    gout_o[:, 512:1024] = jnp.where(c == 0, theirs, mine)
    far_copy(fin_qkv, far_qkv, 4).wait()
    for j in range(3):
        mine, theirs = fin_qkv[own8, j * 512 : (j + 1) * 512], far_qkv[:, j * 512 : (j + 1) * 512]
        gqkv_o[:, j * 1024 : j * 1024 + 512] = jnp.where(c == 0, mine, theirs)
        gqkv_o[:, j * 1024 + 512 : j * 1024 + 1024] = jnp.where(c == 0, theirs, mine)
    last_copy.wait()
    mine, theirs = sm_acc[3], sm_last[...]
    small_o[0:8, :] = jnp.where(c == 0, mine, theirs)
    small_o[8:16, :] = jnp.where(c == 0, theirs, mine)

    exchange_sent(place, l_src, l_dst, ls, lr)
    exchange_sent(place, g_src, g_dst, gs, gr)
    for b in range(4):
        pltpu.make_async_copy(lout.at[pl.ds(0, 128)], lout_o.at[b], lr.at[b]).wait()
        pltpu.make_async_copy(gin_s.at[pl.ds(0, 128)], gin_o.at[b], gr.at[b]).wait()


def run_backward(*args):
    outs = (
        shaped((4, 128, 1024), BF), shaped((4, 128, 1024), BF), shaped((8, 3072), F32), shaped((8, 1024), F32),
        shaped((8, 4096), F32), shaped((32, 1024), F32), shaped((16, 1024), F32),
    )
    v = pltpu.VMEM
    return pl.pallas_call(
        backward_kernel,
        out_shape=outs,
        in_specs=[vmem()] * 10 + [anywhere()] * 5,
        out_specs=(anywhere(), anywhere()) + (vmem(),) * 5,
        scratch_shapes=[
            v((1024, 1536), BF), v((1024, 1024), BF), v((1024, 1536), BF), v((1024, 128), F32), v((1024, 128), F32),
            v((16, 1024), F32), v((256, 256), F32), v((512, 256), F32), v((768, 256), F32), v((768, 256), F32),
            v((2, 8, 8, 16, 128), BF), v((8, 8, 32, 128), BF), v((4, 64, 16, 128), BF), v((4, 3, 64, 16, 128), BF),
            v((2, 8, 7, 16, 128), BF), v((8, 7, 32, 128), BF), v((4, 63, 16, 128), BF), v((4, 3, 63, 16, 128), BF),
            v((16, 2048), F32), v((16, 512), F32), v((16, 1536), F32), v((8, 2048), F32), v((8, 512), F32),
            v((8, 1536), F32), v((512, 1024), BF), v((512, 1024), BF), v((512, 1024), F32), v((512, 1024), BF),
            v((16, 1024), F32), v((8, 1024), F32), v((4, 8, 1024), F32), v((3, 3, 8, 1024), F32), v((8, 1024), F32),
            dma(15), dma(3, 9, 3), dma(3, 9, 3), dma(3, 4, 3, 3), dma(3, 4, 3, 3), dma(4), dma(4), dma(4), dma(4), dma(2), dma(2),
            dma(6), dma(6), dma(3, 3), dma(3, 3),
        ],
        compiler_params=pltpu.CompilerParams(collective_id=1, has_side_effects=True, vmem_limit_bytes=VMEM_LIMIT),
        name="backward",
    )(*args)


VECTORS = ((0, 8), (1, 8), (2, 16), (4, 8), (5, 8), (6, 8), (8, 32), (7, 8))


def finish_kernel(*refs):
    lout, gin, gqkv, gout, gup, gdown, sums = refs[:7]
    outs, vectors = refs[7:13], refs[13:21]
    for src, dst in zip((lout, gin, gqkv, gout, gup, gdown), outs):
        dst[...] = src[...]
    place = Place()
    device = ((place.xh * 4 + place.y) * 2 + place.c) * 8 + place.xl * 4 + place.z
    for (row, size), out in zip(VECTORS, vectors):
        first = device * size
        line = row + lax.div(first, jnp.int32(1024))
        turned = pltpu.roll(sums[pl.ds(line, 1), :], 1024 - lax.rem(first, jnp.int32(1024)), 1)
        out[...] = turned[0, :size]


def run_finish(*args):
    outs = tuple(shaped(a.shape, a.dtype) for a in args[:6]) + tuple(shaped((size,), F32) for _, size in VECTORS)
    return pl.pallas_call(
        finish_kernel,
        out_shape=outs,
        in_specs=[vmem()] * 7,
        out_specs=(vmem(),) * 14,
        name="finish",
    )(*args)


def on_device(
    block_input, segment_ids, padding_flags, cotangent, norm_one_gain, norm_one_bias, query_key_value, query_value_bias,
    out_weight, out_bias, norm_two_gain, norm_two_bias, up_weight, up_bias, down_weight, down_bias,
):
    h1, qkv, x_own, ctxh, dres, dctx, lout, upleft, downleft, bout, lse, seg, par, small = run_first(
        block_input, cotangent, segment_ids, padding_flags, norm_one_gain, norm_one_bias, query_value_bias, out_bias,
        norm_two_gain, norm_two_bias, down_bias, up_bias, query_key_value, out_weight, up_weight, down_weight,
    )
    results = run_backward(
        qkv, dctx, ctxh, lse, seg, h1, x_own, dres, small, par, lout, upleft, downleft, bout, query_key_value
    )
    lout, gin, gqkv, gout, gup, gdown, n1g, n1b, qvb, ob, n2g, n2b, ub, db = run_finish(*results)
    return (lout, gin, n1g, n1b, gqkv, qvb, gout, ob, n2g, n2b, gup, ub, gdown, db)


def solution(mesh):
    wide = Mesh(mesh.devices.reshape(2, 4, 2, 2, 4), AXES)
    rows, seq = ("xh", "y", "c"), ("xl", "z")
    everything = rows + seq
    whole = P()
    return jax.shard_map(
        on_device,
        mesh=wide,
        in_specs=(P(rows, seq, None), P(rows, None), P(rows, None), P(rows, seq, None)) + (whole,) * 12,
        out_specs=(
            P(rows, seq, None), P(rows, seq, None), P(everything), P(everything), P(everything, None), P(everything),
            P(everything, None), P(everything), P(everything), P(everything), P(everything, None), P(everything),
            P(everything, None), P(everything),
        ),
        check_vma=False,
    )
```

```python
import jax
import jax.numpy as jnp
from jax import lax
from jax.experimental import pallas as pl
from jax.experimental.pallas import tpu as pltpu
from jax.sharding import Mesh, PartitionSpec as P

BF = jnp.bfloat16
F32 = jnp.float32
AXES = ("xh", "y", "c", "xl", "z")
BY_MESH = pl.DeviceIdType.MESH
DIMS = ("x1", "y1", "z1", "x0", "y0", "z0")
UP_ORDERS = (("y1", "y0", "x1", "z", "x0"), ("x1", "y0", "y1", "x0", "z"))
DOWN_GROUPS = (
    (0, 3, ("z1", "z0", "x0"), ("y", "x1")),
    (3, 6, ("z0", "x0", "z1"), ("x1", "y")),
    (6, 8, ("x0", "z1", "z0"), ("x1", "y")),
)
OUT_ORDERS = (("y", "x", "z"), ("y", "z", "x"), ("y", "x", "z"), ("y", "z", "x"))
QKV_ORDERS = (("x", "y", "z"), ("z", "x", "y"), ("y", "z", "x"))
BLOCK = 256
GELU = 0.7978845608028654
CUBIC = 0.044715
EPS = 1e-05
MASKED = -1e30
VMEM_LIMIT = 60 * 1024 * 1024


def dot_nn(a, b):
    return lax.dot_general(a, b, (((1,), (0,)), ((), ())), preferred_element_type=F32)


def dot_nt(a, b):
    return lax.dot_general(a, b, (((1,), (1,)), ((), ())), preferred_element_type=F32)


def dot_tn(a, b):
    return lax.dot_general(a, b, (((0,), (0,)), ((), ())), preferred_element_type=F32)


class Place:
    def __init__(self):
        self.xh, self.y, self.c, self.xl, self.z = (lax.axis_index(a) for a in AXES)
        two = jnp.int32(2)
        self.bits = {
            "x1": self.xh,
            "x0": lax.rem(self.xl + self.xh, two),
            "y1": lax.div(self.y, two),
            "y0": lax.rem(self.y + lax.div(self.y, two), two),
            "z1": lax.div(self.z, two),
            "z0": lax.rem(self.z + lax.div(self.z, two), two),
            "x": 2 * self.xh + self.xl,
            "y": self.y,
            "z": self.z,
        }
        names = ("c", "x1", "y1", "z1", "x0", "y0", "z0")
        self.partners = {name: self.find_partner(name) for name in names}
        self.rings = {(axis, s): self.find_ring(axis, s) for axis in "xyz" for s in (1, 2, 3)}
        self.send, self.keep = {}, {}

    def prepare(self, orders):
        for order in orders:
            off = jnp.int32(0)
            for k, name in enumerate(order, 1):
                n = left_after(order, k)
                for s in range(1, width(name)):
                    to = 1 - self.bits[name] if width(name) == 2 else lax.rem(self.bits[name] + s, jnp.int32(4))
                    self.send[order, k, s] = off + to * n
                off = off + self.bits[name] * n
                self.keep[order, k] = off

    def partner(self, name):
        return self.partners[name]

    def ring(self, axis, step):
        return self.rings[axis, step]

    def find_partner(self, name):
        xh, y, c, xl, z = self.xh, self.y, self.c, self.xl, self.z
        if name == "c":
            c = 1 - c
        elif name == "x0":
            xl = 1 - xl
        elif name == "x1":
            xh, xl = 1 - xh, 1 - xl
        elif name == "y0":
            y = y + 1 - 2 * lax.rem(y, jnp.int32(2))
        elif name == "y1":
            y = 3 - y
        elif name == "z0":
            z = z + 1 - 2 * lax.rem(z, jnp.int32(2))
        elif name == "z1":
            z = 3 - z
        return (xh, y, c, xl, z)

    def find_ring(self, axis, step):
        four, two = jnp.int32(4), jnp.int32(2)
        xh, y, c, xl, z = self.xh, self.y, self.c, self.xl, self.z
        if axis == "x":
            at = lax.rem(2 * xh + xl + step, four)
            xh, xl = lax.div(at, two), lax.rem(at, two)
        elif axis == "y":
            y = lax.rem(y + step, four)
        else:
            z = lax.rem(z + step, four)
        return (xh, y, c, xl, z)

    def exchange(self, r):
        return (self.xh, self.y, self.xl, self.c, jnp.int32(r))

    def is_self(self, r):
        return (self.c == self.xl) & (self.z == r)


def bits_of(s):
    xh, y, xl, z = s >> 5, (s >> 3) & 3, (s >> 2) & 1, s & 3
    return {
        "x1": xh, "y1": y >> 1, "z1": z >> 1, "x0": xl ^ xh, "y0": (y & 1) ^ (y >> 1), "z0": (z & 1) ^ (z >> 1),
        "x": 2 * xh + xl, "y": y, "z": z,
    }


def width(name):
    return 4 if len(name) == 1 else 2


def left_after(order, k):
    n = 1
    for name in order[k:]:
        n *= width(name)
    return n


def slot_of(s, order):
    bits, slot = bits_of(s), 0
    for name in order:
        slot = width(name) * slot + bits[name]
    return slot


def region(order, k):
    return sum((width(name) - 1) * left_after(order, j + 1) for j, name in enumerate(order[: k - 1]))


class Scatter:
    def __init__(self, place, k, order, buf, got, lead, sends, recvs, at):
        name = order[k - 1]
        n = left_after(order, k)
        self.copies = []
        for s in range(1, width(name)):
            peer = place.partner(name) if width(name) == 2 else place.ring(name, s)
            self.copies.append(
                pltpu.make_async_remote_copy(
                    src_ref=buf.at[lead + (pl.ds(place.send[order, k, s], n),)],
                    dst_ref=got.at[lead + (pl.ds(region(order, k) + (s - 1) * n, n),)],
                    send_sem=sends.at[at + (s - 1,)],
                    recv_sem=recvs.at[at + (s - 1,)],
                    device_id=peer,
                    device_id_type=BY_MESH,
                )
            )

    def start(self):
        for copy in self.copies:
            copy.start()

    def wait(self):
        for copy in self.copies:
            copy.wait()


def scatter_sum(place, k, order, buf, got, lead):
    n = left_after(order, k)
    mine = lead + (pl.ds(place.keep[order, k], n),)
    if width(order[k - 1]) == 2 and k < len(order):
        return mine, buf[mine] + got[lead + (pl.ds(region(order, k), n),)]
    total = buf[mine].astype(F32)
    for s in range(1, width(order[k - 1])):
        total = total + got[lead + (pl.ds(region(order, k) + (s - 1) * n, n),)].astype(F32)
    return mine, total


def scatter_add(place, k, order, buf, got, lead):
    mine, total = scatter_sum(place, k, order, buf, got, lead)
    buf[mine] = total.astype(BF)


def scatter_last(place, order, buf, got, lead):
    _, total = scatter_sum(place, len(order), order, buf, got, lead)
    return total.reshape(total.shape[-2:])


def feature_rows(flat):
    parts = []
    for g in range(8):
        for c in range(2):
            parts.append(flat[(c * 8 + g) * 8 : (c * 8 + g + 1) * 8])
    return jnp.concatenate(parts, axis=0)


def natural_rows(flat):
    return jnp.concatenate([flat[(g * 2 + c) * 8 : (g * 2 + c + 1) * 8] for c in range(2) for g in range(8)], axis=0)


def transpose_features(src, dst, tokens):
    def body(f, carry):
        block = src[tokens, pl.ds(pl.multiple_of(f * 128, 128), 128)].astype(F32)
        dst[pl.ds(pl.multiple_of(f * 128, 128), 128), tokens] = feature_rows(block.T).astype(BF)
        return carry

    lax.fori_loop(0, 8, body, 0)


def norm_parts(v):
    center = v - jnp.mean(v, axis=-1, keepdims=True)
    rstd = lax.rsqrt(jnp.mean(center * center, axis=-1, keepdims=True) + EPS)
    return center * rstd, rstd


def aligned(v, m):
    return pl.multiple_of(v, m)


def window(i):
    return max(0, i - 2) * BLOCK, (i + 1) * BLOCK


def remote(src, dst, send, recv, device):
    return pltpu.make_async_remote_copy(
        src_ref=src, dst_ref=dst, send_sem=send, recv_sem=recv, device_id=device, device_id_type=BY_MESH
    )


def greet(place, devices, with_exchange):
    barrier = pltpu.get_barrier_semaphore()
    count = jnp.int32(len(devices))
    for d in devices:
        pl.semaphore_signal(barrier, inc=1, device_id=d, device_id_type=BY_MESH)
    if with_exchange:
        for r in range(4):

            @pl.when(jnp.logical_not(place.is_self(r)))
            def _(r=r):
                pl.semaphore_signal(barrier, inc=1, device_id=place.exchange(r), device_id_type=BY_MESH)

        count = count + 4 - jnp.where(place.c == place.xl, 1, 0)
    pl.semaphore_wait(barrier, count)


def exchange_start(place, src_of, dst_of, own_dst_of, sends, recvs, which=(0, 1, 2, 3)):
    for r in which:
        own = place.is_self(r)

        @pl.when(own)
        def _(r=r):
            pltpu.make_async_copy(src_of(r), own_dst_of(r), recvs.at[place.z]).start()

        @pl.when(jnp.logical_not(own))
        def _(r=r):
            remote(src_of(r), dst_of(r), sends.at[r], recvs.at[place.z], place.exchange(r)).start()


def exchange_sent(place, src_of, dst_of, sends, recvs):
    for r in range(4):

        @pl.when(jnp.logical_not(place.is_self(r)))
        def _(r=r):
            remote(src_of(r), dst_of(r), sends.at[r], recvs.at[place.z], place.exchange(r)).wait_send()


def vmem(n=None):
    return pl.BlockSpec(memory_space=pltpu.VMEM)


def anywhere():
    return pl.BlockSpec(memory_space=pl.ANY)


def dma(*shape):
    return pltpu.SemaphoreType.DMA(shape)


def shaped(shape, dtype):
    return jax.ShapeDtypeStruct(shape, dtype)


def first_kernel(
    x_in, c_in, seg_in, flag_in, g1, b1_, bqv, bo, g2, b2_, bd, bu, wqkv, wout, wup, wdown,
    h1_o, qkv_o, x_o, ctxh_o, dres_o, dctx_o, lout_o, upleft_o, downleft_o, bout_o, lse_o, seg_o, par, small_o,
    hid, cot, qkv, x_own, ctxh, ctxp, resid, h2t, lse_acc, wq, wo, wu, wd, down_acc, dh_acc, act_s, dup_s, dat, lout, dctx,
    bup, rup, bdown, rdown, bout, upleft, downleft, seg_got,
    xs, xr, cs, cr, hs, hr, fs, fr, ts, tr, gs, gr, ss, sr, ws, us, ds, es, er, ups, upr, dns, dnr, os,
):
    place = Place()
    c, xl, z = place.c, place.xl, place.z
    mate = place.partner("c")
    place.prepare(UP_ORDERS + tuple(g[2] for g in DOWN_GROUPS))
    own = pl.ds(aligned(c * 512, 512), 512)
    far = pl.ds(aligned((1 - c) * 512, 512), 512)
    loads = [
        pltpu.make_async_copy(
            wqkv.at[:, pl.ds(aligned(j * 1024 + c * 512, 512), 512)], wq.at[:, pl.ds(j * 512, 512)], ws.at[j]
        )
        for j in range(3)
    ]
    loads.append(pltpu.make_async_copy(wout, wo, ws.at[3]))

    def up_load(t):
        return pltpu.make_async_copy(
            wup.at[:, pl.ds(aligned((2 * t + c) * 256, 256), 256)], wu.at[lax.rem(t, jnp.int32(4))], us.at[t]
        )

    def down_load(t):
        return pltpu.make_async_copy(
            wdown.at[pl.ds(aligned((2 * t + c) * 256, 256), 256)], wd.at[lax.rem(t, jnp.int32(4))], ds.at[t]
        )

    def saves(n, src, dst):
        return pltpu.make_async_copy(src, dst, os.at[n])

    for load in loads:
        load.start()
    for t in range(4):
        up_load(jnp.int32(t)).start()
        down_load(jnp.int32(t)).start()
    greet(place, [mate] + [place.partner(d) for d in DIMS], True)

    def x_src(r):
        return x_in.at[r]

    def x_dst(r):
        return x_own.at[pl.ds(aligned(z * 128, 128), 128)]

    def c_src(r):
        return c_in.at[r]

    def c_dst(r):
        return cot.at[pl.ds(aligned(xl * 512 + z * 128, 128), 128)]

    exchange_start(place, x_src, x_dst, x_dst, xs, xr)
    seg_out = [remote(ref, seg_got.at[n], ss.at[n], sr.at[n], mate) for n, ref in enumerate((seg_in, flag_in))]
    for copy in seg_out:
        copy.start()
    for n, ref in enumerate((g1, b1_, bqv, bqv, bo, g2, b2_, bd, bu, bu, bu, bu)):
        first = {3: 1024, 9: 1024, 10: 2048, 11: 3072}.get(n, 0)
        par[n : n + 1, :] = ref[first : first + 1024].astype(F32).reshape(1, 1024)
    par[12:16, :] = jnp.zeros((4, 1024), F32)

    for copy in seg_out:
        copy.wait()
    own_seg, own_flag = seg_in[pl.ds(z, 1), :], flag_in[pl.ds(z, 1), :]
    far_seg, far_flag = seg_got[0, pl.ds(z, 1), :], seg_got[1, pl.ds(z, 1), :]
    near = jnp.where(c == xl, 1, 0)
    seg_row = jnp.where(near == 1, own_seg, far_seg).astype(F32)
    flag_row = jnp.where(near == 1, own_flag, far_flag)
    key_row = jnp.where(flag_row == 0, seg_row, -1.0)
    seg_o[...] = jnp.concatenate([seg_row, key_row, jnp.zeros((6, 1024), F32)], axis=0)
    seg_col = jnp.broadcast_to(seg_row, (128, 1024)).T
    for i in range(4):
        w0, w1 = window(i)
        rows = lax.broadcasted_iota(jnp.int32, (BLOCK, w1 - w0), 0) + i * BLOCK
        cols = lax.broadcasted_iota(jnp.int32, (BLOCK, w1 - w0), 1) + w0
        same = seg_col[i * BLOCK : (i + 1) * BLOCK, 0:1] == key_row[:, w0:w1]
        dh_acc[i * BLOCK : (i + 1) * BLOCK, 0 : w1 - w0] = jnp.where(
            (same & (cols <= rows)) | (rows == cols), 0.0, MASKED
        )
    lse_acc[...] = jnp.zeros_like(lse_acc)

    gain_one, bias_one = par[0:1, :], par[1:2, :]

    def block_copy(ref, b, mine, sends, recvs):
        half = c if mine else 1 - c
        rows = pl.ds(aligned(half * 512 + b * 128, 128), 128)
        return remote(ref.at[rows], ref.at[rows], sends.at[b], recvs.at[b], mate)

    for b in range(4):
        pltpu.make_async_copy(x_in.at[0], x_own.at[b * 128 : (b + 1) * 128], xr.at[b]).wait()
        xhat, _ = norm_parts(x_own[b * 128 : (b + 1) * 128].astype(F32))
        hid[pl.ds(aligned(c * 512 + b * 128, 128), 128)] = (xhat * gain_one + bias_one).astype(BF)
        block_copy(hid, b, True, hs, hr).start()
    exchange_start(place, c_src, c_dst, c_dst, cs, cr)
    saves(0, x_own, x_o).start()

    for load in loads[:3]:
        load.wait()
    zero = jnp.zeros((1, 512), F32)
    bias = jnp.concatenate([par[2:3, own], zero, par[3:4, own]], axis=1)

    def project(first):
        def body(n, carry):
            rows = pl.ds(aligned(first + n * BLOCK, BLOCK), BLOCK)
            qkv[rows, :] = (dot_nn(hid[rows, :], wq[...]) + bias).astype(BF)
            return carry

        lax.fori_loop(0, 2, body, 0)

    project(c * 512)
    for b in range(4):
        block_copy(hid, b, False, hs, hr).wait_recv()
    saves(1, hid, h1_o).start()
    project((1 - c) * 512)
    saves(2, qkv, qkv_o).start()

    lane = lax.broadcasted_iota(jnp.int32, (BLOCK, 128), 1)

    def ctx_copy(p, half):
        return remote(
            ctxh.at[far, pl.ds(aligned(p * 128, 128), 128)],
            ctxp.at[:, pl.ds(aligned(half * 512 + p * 128, 128), 128)],
            ts.at[p], tr.at[p], mate,
        )

    def attend(p, carry):
        lo = aligned(p * 128, 128)
        for i in range(4):
            w0, w1 = window(i)
            rows = slice(i * BLOCK, (i + 1) * BLOCK)
            query = qkv[rows, pl.ds(lo, 128)] * jnp.asarray(0.125, BF)
            keys = qkv[w0:w1, pl.ds(aligned(512 + lo, 128), 128)]
            values = qkv[w0:w1, pl.ds(aligned(1024 + lo, 128), 128)]
            zero = jnp.zeros_like(query)
            both = jnp.concatenate([jnp.where(lane < 64, query, zero), jnp.where(lane < 64, zero, query)], axis=0)
            mask = dh_acc[rows, 0 : w1 - w0]
            scores = dot_nt(both, keys) + jnp.concatenate([mask, mask], axis=0)
            top = jnp.max(scores, axis=-1, keepdims=True)
            expo = jnp.exp(scores - top)
            found = dot_nn(expo.astype(BF), jnp.concatenate([values, jnp.ones_like(values)], axis=1))
            total = found[:, 128:256]
            log_total = top + jnp.log(total)
            outs = found[:, 0:128] / total
            lse_acc[rows, :] = jnp.where(
                lane == 2 * p, log_total[:BLOCK], jnp.where(lane == 2 * p + 1, log_total[BLOCK:], lse_acc[rows, :])
            )
            ctxh[rows, pl.ds(lo, 128)] = jnp.where(lane < 64, outs[:BLOCK], outs[BLOCK:]).astype(BF)

        @pl.when(p == 3)
        def _():
            saves(1, hid, h1_o).wait()
            saves(2, qkv, qkv_o).wait()
            for b in range(4):
                block_copy(hid, b, True, hs, hr).wait_send()

        ctx_copy(p, c).start()
        ctxp[:, pl.ds(aligned(c * 512 + lo, 128), 128)] = ctxh[own, pl.ds(lo, 128)]
        return carry

    lax.fori_loop(0, 4, attend, 0)
    saves(3, ctxh, ctxh_o).start()
    lse_o[...] = lse_acc[...].T[0:16, :]

    for b in range(4):
        pltpu.make_async_copy(c_in.at[0], cot.at[pl.ds(aligned(c * 512 + b * 128, 128), 128)], cr.at[b]).wait()
        block_copy(cot, b, True, fs, fr).start()

    loads[3].wait()
    for p in range(4):
        ctx_copy(p, 1 - c).wait_recv()

    def h2_copy(n, half):
        rows = pl.ds(aligned(half * 512 + n * BLOCK, BLOCK), BLOCK)
        return remote(hid.at[rows], hid.at[rows], gs.at[n], gr.at[n], mate)

    def output(n, carry):
        rows = pl.ds(aligned(n * BLOCK, BLOCK), BLOCK)
        res = x_own[rows, :].astype(F32) + (dot_nn(ctxp[rows, :], wo[...]) + par[4:5, :])
        resid[rows, :] = res
        xhat, _ = norm_parts(res)
        hid[pl.ds(aligned(c * 512 + n * BLOCK, BLOCK), BLOCK), :] = (xhat * par[5:6, :] + par[6:7, :]).astype(BF)
        h2_copy(n, c).start()
        return carry

    lax.fori_loop(0, 2, output, 0)
    small_o[...] = jnp.zeros_like(small_o)
    transpose_features(hid, h2t, own)
    for n in range(2):
        h2_copy(n, 1 - c).wait_recv()
    transpose_features(hid, h2t, far)
    for b in range(4):
        block_copy(cot, b, False, fs, fr).wait_recv()

    def up_copy(k, t, j):
        return Scatter(place, k, UP_ORDERS[j], bup, rup, (t, j), ups, upr, (k - 1, t, j))

    def down_copy(k, t, g):
        p0, p1, order, _ = DOWN_GROUPS[g]
        return Scatter(place, k, order, bdown, rdown, (t, slice(p0, p1)), dns, dnr, (k - 1, t, g))

    def start(k, t):
        for j in range(2):
            up_copy(k, t, j).start()
        for g in range(3):
            down_copy(k, t, g).start()

    def tile_slot(t, rest):
        bits = {"x1": lax.div(t, jnp.int32(4)), "y": lax.rem(t, jnp.int32(4))}
        slot = jnp.int32(0)
        for name in rest:
            slot = width(name) * slot + bits[name]
        return slot

    def finish(k, t):
        for j in range(2):
            up_copy(k, t, j).wait()
        for g in range(3):
            down_copy(k, t, g).wait()
        for j, order in enumerate(UP_ORDERS):
            mine, total = scatter_sum(place, k, order, bup, rup, (t, j))
            if k < 3:
                bup[mine] = total.astype(BF)
            else:
                upleft[j, t] = total.astype(BF)
        for p0, p1, order, rest in DOWN_GROUPS:
            for p in range(p0, p1):
                mine, total = scatter_sum(place, k, order, bdown, rdown, (t, p))
                if k < 3:
                    bdown[mine] = total.astype(BF)
                else:
                    downleft[p, pl.ds(tile_slot(t, rest), 1)] = total.astype(BF)
        if k < 3:
            start(k + 1, t)

    def tile(t, carry):
        four = jnp.int32(4)
        ring = lax.rem(t, four)
        up_load(t).wait()
        down_load(t).wait()
        col = 2 * t + c
        up_row = 8 + lax.div(col, four)
        up_cols = pl.ds(aligned(lax.rem(col, four) * 256, 256), 256)
        up_bias = par[pl.ds(up_row, 1), up_cols]
        dbias = jnp.zeros((1, 256), F32)
        for b in range(4):
            rows = slice(b * BLOCK, (b + 1) * BLOCK)
            u = dot_nn(hid[rows, :], wu[ring]) + up_bias
            dact = dot_nt(cot[rows, :], wd[ring])
            square = u * u
            th = jnp.tanh(GELU * u * (1.0 + CUBIC * square))
            act_s[rows, :] = (0.5 * u * (1.0 + th)).astype(BF)
            slope = 0.5 * (1.0 + th) + 0.5 * u * (1.0 - th * th) * (GELU * (1.0 + (3.0 * CUBIC) * square))
            dup = (dact * slope).astype(BF)
            dup_s[rows, :] = dup
            dbias = dbias + jnp.sum(dup.astype(F32), axis=0, keepdims=True)
        small_o[pl.ds(up_row, 1), up_cols] = dbias

        for k in (3, 2, 1):

            @pl.when(t >= k + 1)
            def _(k=k):
                finish(k, t - k - 1)

        xh = lax.div(t, four)
        grad = dot_tn(act_s[...], cot[...]).astype(BF)
        for s in range(8):
            bits = bits_of(s)
            x0 = lax.rem(xh + (s >> 2), jnp.int32(2))
            for p0, p1, order, _ in DOWN_GROUPS:
                fixed = sum(bits[name] << (2 - n) for n, name in enumerate(order) if name != "x0")
                slot = fixed + x0 * (1 << (2 - order.index("x0")))
                for j in range(p0, p1):
                    bdown[t, j, slot] = grad[s * 32 : (s + 1) * 32, j * 128 : (j + 1) * 128]
        for b in range(4):
            grad = dot_nn(h2t[b * 256 : (b + 1) * 256, :], dup_s[...]).astype(BF)
            for s in range(16):
                for j, order in enumerate(UP_ORDERS):
                    bup[t, j, slot_of(b * 16 + s, order)] = grad[s * 16 : (s + 1) * 16, j * 128 : (j + 1) * 128]
        start(1, t)

        @pl.when(t == 0)
        def _():
            for b in range(4):
                rows = slice(b * BLOCK, (b + 1) * BLOCK)
                down_acc[rows, :] = dot_nn(act_s[rows, :], wd[ring])
                dh_acc[rows, :] = dot_nt(dup_s[rows, :], wu[ring])

        @pl.when(t > 0)
        def _():
            for b in range(4):
                rows = slice(b * BLOCK, (b + 1) * BLOCK)
                down_acc[rows, :] = down_acc[rows, :] + dot_nn(act_s[rows, :], wd[ring])
                dh_acc[rows, :] = dh_acc[rows, :] + dot_nt(dup_s[rows, :], wu[ring])

        @pl.when(t < 4)
        def _():
            up_load(t + 4).start()
            down_load(t + 4).start()

        return carry

    lax.fori_loop(0, 8, tile, 0)

    dh_send, dh_got = qkv.at[0:512, 0:1024], qkv.at[512:1024, 0:1024]
    dn_send, dn_got = wq.at[0:512, 0:1024], wq.at[512:1024, 0:1024]
    dc_send = qkv.at[0:512, 1024:1536]
    ctxt = wq.at[:, 1024:1536]
    wo_send, wo_got = bup.at[0:2], bup.at[2:4]
    dh_send[...] = dh_acc[far, :].astype(BF)
    dh_copy = remote(dh_send, dh_got, es.at[0], er.at[0], mate)
    dh_copy.start()
    dn_send[...] = down_acc[far, :].astype(BF)
    dn_copy = remote(dn_send, dn_got, es.at[1], er.at[1], mate)
    dn_copy.start()
    for k in (3, 2, 1):
        finish(k, 7 - k)

    transpose_features(ctxp, ctxt, slice(0, 512))
    dh_copy.wait()
    dn_copy.wait()

    def norm_back(n, sums):
        gain_sum, bias_sum, out_sum, down_sum = sums
        rows = pl.ds(aligned(n * 128, 128), 128)
        mine = pl.ds(aligned(c * 512 + n * 128, 128), 128)
        res = resid[rows, :]
        lout[rows, :] = (res + (down_acc[mine, :] + dn_got[rows, :].astype(F32) + par[7:8, :])).astype(BF)
        xhat, rstd = norm_parts(res)
        dn = dh_acc[mine, :] + dh_got[rows, :].astype(F32)
        e = dn * par[5:6, :]
        cf = cot[mine, :].astype(F32)
        dres = cf + rstd * (
            e - jnp.mean(e, axis=-1, keepdims=True) - xhat * jnp.mean(e * xhat, axis=-1, keepdims=True)
        )
        resid[rows, :] = dres
        low = dres.astype(BF)
        dat[rows, :] = low
        return (
            gain_sum + jnp.sum(dn * xhat, axis=0, keepdims=True),
            bias_sum + jnp.sum(dn, axis=0, keepdims=True),
            out_sum + jnp.sum(low.astype(F32), axis=0, keepdims=True),
            down_sum + jnp.sum(cf, axis=0, keepdims=True),
        )

    nothing = jnp.zeros((1, 1024), F32)
    gain_sum, bias_sum, out_sum, down_sum = lax.fori_loop(0, 4, norm_back, (nothing,) * 4)
    small_o[5:6, :] = gain_sum
    small_o[6:7, :] = bias_sum
    small_o[4:5, :] = out_sum
    small_o[7:8, :] = down_sum
    saves(4, resid, dres_o).start()
    saves(5, lout, lout_o).start()

    dc_send[...] = dot_nt(dat[...], wo[far, :]).astype(BF)
    dc_copy = remote(dc_send, dctx.at[own], es.at[2], er.at[2], mate)
    dc_copy.start()
    for k in (3, 2, 1):
        finish(k, 8 - k)

    def out_grad(cols, dst, lead):
        for b in range(4):
            grad = dot_nn(ctxt[b * 256 : (b + 1) * 256, :], dat[:, cols]).astype(BF)
            for s in range(16):
                for j, order in enumerate(OUT_ORDERS):
                    dst[lead(j) + (slot_of(b * 16 + s, order),)] = grad[s * 16 : (s + 1) * 16, j * 128 : (j + 1) * 128]

    out_grad(far, wo_send, lambda j: (j // 2, j % 2))
    wo_copy = remote(wo_send, wo_got, es.at[3], er.at[3], mate)
    wo_copy.start()
    dctx[own, :] = dot_nt(dat[...], wo[own, :]).astype(BF)
    for k in (3, 2):
        finish(k, 9 - k)
    out_grad(own, bout, lambda j: (j,))
    dc_copy.wait_send()
    remote(dc_send, dctx.at[far], es.at[2], er.at[2], mate).wait_recv()
    saves(6, dctx, dctx_o).start()
    finish(3, 7)
    saves(7, upleft, upleft_o).start()
    saves(8, downleft, downleft_o).start()
    wo_copy.wait()
    for j in range(4):
        bout[j] = bout[j] + wo_got[j // 2, j % 2]
    saves(9, bout, bout_o).start()

    exchange_sent(place, x_src, x_dst, xs, xr)
    exchange_sent(place, c_src, c_dst, cs, cr)
    for b in range(4):
        block_copy(cot, b, True, fs, fr).wait_send()
        ctx_copy(b, c).wait_send()
    for n in range(2):
        h2_copy(n, c).wait_send()
    saves(0, x_own, x_o).wait()
    saves(3, ctxh, ctxh_o).wait()
    saves(4, resid, dres_o).wait()
    saves(5, lout, lout_o).wait()
    saves(6, dctx, dctx_o).wait()
    saves(7, upleft, upleft_o).wait()
    saves(8, downleft, downleft_o).wait()
    saves(9, bout, bout_o).wait()


def run_first(*args):
    outs = (
        shaped((1024, 1024), BF), shaped((1024, 1536), BF), shaped((512, 1024), BF), shaped((1024, 512), BF),
        shaped((512, 1024), F32), shaped((1024, 512), BF), shaped((512, 1024), BF), shaped((2, 8, 8, 16, 128), BF),
        shaped((8, 8, 32, 128), BF), shaped((4, 64, 16, 128), BF), shaped((16, 1024), F32), shaped((8, 1024), F32),
        shaped((16, 1024), F32), shaped((16, 1024), F32),
    )
    v = pltpu.VMEM
    return pl.pallas_call(
        first_kernel,
        out_shape=outs,
        in_specs=[anywhere(), anywhere()] + [vmem()] * 10 + [anywhere()] * 4,
        out_specs=(anywhere(),) * 10 + (vmem(),) * 4,
        scratch_shapes=[
            v((1024, 1024), BF), v((1024, 1024), BF), v((1024, 1536), BF), v((512, 1024), BF), v((1024, 512), BF),
            v((512, 1024), BF), v((512, 1024), F32), v((1024, 1024), BF), v((1024, 128), F32), v((1024, 1536), BF),
            v((1024, 1024), BF), v((4, 1024, 256), BF), v((4, 256, 1024), BF), v((1024, 1024), F32),
            v((1024, 1024), F32), v((1024, 256), BF), v((1024, 256), BF), v((512, 1024), BF), v((512, 1024), BF),
            v((1024, 512), BF), v((8, 2, 64, 16, 128), BF), v((8, 2, 56, 16, 128), BF), v((8, 8, 8, 32, 128), BF),
            v((8, 8, 7, 32, 128), BF), v((4, 64, 16, 128), BF), v((2, 8, 8, 16, 128), BF), v((8, 8, 32, 128), BF),
            v((2, 4, 1024), jnp.int32),
            dma(4), dma(4), dma(4), dma(4), dma(4), dma(4), dma(4), dma(4), dma(4), dma(4), dma(2), dma(2), dma(2),
            dma(2), dma(4), dma(8), dma(8), dma(4), dma(4), dma(3, 8, 2, 1), dma(3, 8, 2, 1), dma(3, 8, 3, 1),
            dma(3, 8, 3, 1), dma(10),
        ],
        compiler_params=pltpu.CompilerParams(collective_id=0, has_side_effects=True, vmem_limit_bytes=VMEM_LIMIT),
        name="first",
    )(*args)


MAIN = (
    tuple((0, (j, slice(0, 8)), UP_ORDERS[j][3:]) for j in range(2))
    + tuple((1, (slice(p0, p1),), rest) for p0, p1, _, rest in DOWN_GROUPS)
    + tuple((2, (j,), order) for j, order in enumerate(OUT_ORDERS))
)
LEFT = (0, 1, 2, 3, 4)
OUT = (5, 6, 7, 8)
EVENTS = {
    (0, 3): (("left", 1), ("early", 0)),
    (1, 3): (("left", 2), ("early", 1)),
    (2, 1): (("out", 1),),
    (2, 3): (("early", 2),),
    (3, 1): (("out", 2),),
}


def backward_kernel(
    lse, seg, small_in, par, upleft, downleft, bout_in, qkv_in, dctx_in, ctxh_in, h1_in, lout_in, wqkv, x_in, dres_in,
    lout_o, gin_o, gqkv_o, gout_o, gup_o, gdown_o, small_o,
    qkv, dctx, ctxh, h1, lout, x_own, dres,
    wq, h1t, dqkv, dk_acc, dv_acc, drow, t0, t1, t2, t3, bup, bdown, bout, bqkv, rup, rdown, rout, rqkv,
    fin_up, fin_out, fin_qkv, far_up, far_out, far_qkv, dh_send, dh_got, dh_acc, gin_s, gain_acc, bias_acc,
    early, early_got, early_far, late, late_got, late_far,
    ws, ms, mr, qs, qr, ls, lr, gs, gr, hs, hr, es, er, ps, pr, vs, vr,
):
    place = Place()
    c, xl, z = place.c, place.xl, place.z
    mate = place.partner("c")
    place.prepare(tuple(order for _, _, order in MAIN) + QKV_ORDERS)
    moves = (
        (upleft, bup), (downleft, bdown), (bout_in, bout), (qkv_in, qkv), (dctx_in, dctx), (ctxh_in, ctxh), (h1_in, h1),
        (lout_in, lout), (x_in, x_own), (dres_in, dres),
    )
    loads = [pltpu.make_async_copy(src, dst, ws.at[n]) for n, (src, dst) in enumerate(moves)]
    for p in range(4):
        for j in range(3):
            loads.append(
                pltpu.make_async_copy(
                    wqkv.at[:, pl.ds(aligned(j * 1024 + c * 512 + p * 128, 128), 128)],
                    wq.at[:, pl.ds(p * 384 + j * 128, 128)],
                    ws.at[10 + p * 3 + j],
                )
            )
    for load in loads:
        load.start()
    peers = [mate] + [place.partner(d) for d in DIMS] + [place.ring(a, s) for a in "xyz" for s in (1, 2, 3)]
    greet(place, peers, True)

    def l_src(r):
        return lout.at[pl.ds(r * 128, 128)]

    def l_dst(r):
        return lout_o.at[z]

    for load in loads[:3]:
        load.wait()
    bufs, gots = (bup, bdown, bout), (rup, rdown, rout)

    def main_copy(k, n):
        which, lead, order = MAIN[n]
        return Scatter(place, k, order, bufs[which], gots[which], lead, ms, mr, (k - 1, n))

    def main_start(k, which):
        for n in which:
            main_copy(k, n).start()

    def main_finish(k, which):
        for n in which:
            main_copy(k, n).wait()
        for n in which:
            b, lead, order = MAIN[n]
            if k < len(order):
                scatter_add(place, k, order, bufs[b], gots[b], lead)
        if k < len(MAIN[which[0]][2]):
            main_start(k + 1, which)
        elif which is LEFT:
            left_last()
        else:
            out_last()

    def vector_copy(ref, got, sends, recvs, n, s):
        return remote(ref.at[n], got.at[n, s - 1], sends.at[n, s - 1], recvs.at[n, s - 1], place.ring("yxz"[n], s))

    def vector_start(ref, got, sends, recvs, n):
        for s in (1, 2, 3):
            vector_copy(ref, got, sends, recvs, n, s).start()

    def vector_finish(ref, got, sends, recvs, n):
        for s in (1, 2, 3):
            vector_copy(ref, got, sends, recvs, n, s).wait()
        ref[n + 1] = ref[n] + got[n, 0] + got[n, 1] + got[n, 2]
        if n < 2:
            vector_start(ref, got, sends, recvs, n + 1)

    early_copy = remote(early.at[3], early_far, es.at[3], er.at[3], mate)
    late_copy = remote(late.at[3], late_far, es.at[5], er.at[5], mate)

    def happen(what, k):
        if what == "left":
            main_finish(k, LEFT)
        elif what == "out":
            main_finish(k, OUT)
        else:
            vector_finish(early, early_got, ps, pr, k)
            if k == 2:
                early_copy.start()

    main_start(1, LEFT)
    early[0] = small_in[4:12, :]
    vector_start(early, early_got, ps, pr, 0)
    main_start(1, OUT)
    loads[7].wait()
    exchange_start(place, l_src, l_dst, l_dst, ls, lr)
    late[0] = jnp.zeros((32, 128), F32)

    key_col = jnp.broadcast_to(seg[1:2, :], (128, 1024)).T
    for i, ref in enumerate((t0, t1, t2, t3)):
        w0, w1 = window(i)
        rows = lax.broadcasted_iota(jnp.int32, (w1 - w0, BLOCK), 0) + w0
        cols = lax.broadcasted_iota(jnp.int32, (w1 - w0, BLOCK), 1) + i * BLOCK
        same = key_col[w0:w1, 0:1] == seg[0:1, i * BLOCK : (i + 1) * BLOCK]
        ref[...] = jnp.where((same & (rows <= cols)) | (rows == cols), 0.0, MASKED)
    for load in loads[3:7]:
        load.wait()
    transpose_features(h1, h1t, slice(0, 1024))
    gain_acc[...] = jnp.zeros_like(gain_acc)
    bias_acc[...] = jnp.zeros_like(bias_acc)

    lane = lax.broadcasted_iota(jnp.int32, (BLOCK, 128), 1)
    row = lax.broadcasted_iota(jnp.int32, (128, BLOCK), 0)
    head_of = lax.broadcasted_iota(jnp.int32, (16, 128), 1)
    row_of = lax.broadcasted_iota(jnp.int32, (16, 128), 0)
    pick = jnp.where(lax.div(head_of, jnp.int32(64)) == row_of, 1.0, 0.0).astype(BF)

    def far_copy(src, dst, at):
        return remote(src.at[pl.ds(aligned((1 - c) * 8, 8), 8)], dst, es.at[at], er.at[at], mate)

    def left_last():
        for j in range(2):
            for t in range(8):
                p = 2 * t + j
                fin_up[:, p * 128 : (p + 1) * 128] = scatter_last(place, UP_ORDERS[j][3:], bup, rup, (j, t))
        far_copy(fin_up, far_up, 0).start()
        for p0, p1, _, rest in DOWN_GROUPS:
            for p in range(p0, p1):
                gdown_o[:, p * 128 : (p + 1) * 128] = scatter_last(place, rest, bdown, rdown, (p,))

    def out_last():
        for j, order in enumerate(OUT_ORDERS):
            fin_out[:, j * 128 : (j + 1) * 128] = scatter_last(place, order, bout, rout, (j,))
        far_copy(fin_out, far_out, 1).start()

    def qkv_copy(k, p, j):
        return Scatter(place, k, QKV_ORDERS[j], bqkv, rqkv, (p, j), qs, qr, (k - 1, p, j))

    def qkv_start(k, p):
        for j in range(3):
            qkv_copy(k, p, j).start()

    def qkv_finish(k, p):
        for j in range(3):
            qkv_copy(k, p, j).wait()
        for j, order in enumerate(QKV_ORDERS):
            if k < 3:
                scatter_add(place, k, order, bqkv, rqkv, (p, j))
            else:
                fin_qkv[:, pl.ds(aligned(j * 512 + p * 128, 128), 128)] = scatter_last(place, order, bqkv, rqkv, (p, j))
        if k < 3:
            qkv_start(k + 1, p)

    def pair(p, carry):
        lo = aligned(p * 128, 128)
        prod = (dctx[:, pl.ds(lo, 128)].astype(F32) * ctxh[:, pl.ds(lo, 128)].astype(F32)).astype(BF)
        drow[...] = dot_nt(pick, prod)
        dk_acc[...] = jnp.zeros_like(dk_acc)
        dv_acc[...] = jnp.zeros_like(dv_acc)
        at = p * 384
        for i, ref in enumerate((t0, t1, t2, t3)):
            w0, w1 = window(i)
            rows = slice(i * BLOCK, (i + 1) * BLOCK)
            query = qkv[rows, pl.ds(lo, 128)] * jnp.asarray(0.125, BF)
            keys = qkv[w0:w1, pl.ds(aligned(512 + lo, 128), 128)]
            values = qkv[w0:w1, pl.ds(aligned(1024 + lo, 128), 128)]
            grad = dctx[rows, pl.ds(lo, 128)]
            zero = jnp.zeros_like(query)
            both = jnp.concatenate([jnp.where(lane < 64, query, zero), jnp.where(lane < 64, zero, query)], axis=0)
            grads = jnp.concatenate([jnp.where(lane < 64, grad, zero), jnp.where(lane < 64, zero, grad)], axis=0)
            mask = ref[...]
            log_total = jnp.concatenate([lse[pl.ds(2 * p, 1), rows], lse[pl.ds(2 * p + 1, 1), rows]], axis=1)
            inner = jnp.concatenate([drow[0:1, rows], drow[1:2, rows]], axis=1)
            probs = jnp.exp(dot_nt(keys, both) + jnp.concatenate([mask, mask], axis=1) - log_total)
            dscores = (probs * (dot_nt(values, grads) - inner)).astype(BF)
            dv_acc[w0:w1, :] = dv_acc[w0:w1, :] + dot_nn(probs.astype(BF), grads)
            dk_acc[w0:w1, :] = dk_acc[w0:w1, :] + dot_nn(dscores, both)
            dq = dot_tn(keys, dscores)
            dq = jnp.where(row < 64, dq[:, :BLOCK], dq[:, BLOCK:]).T
            dqkv[rows, pl.ds(aligned(at, 128), 128)] = (dq * 0.125).astype(BF)
            for (ep, ei), events in EVENTS.items():
                if ei == i:

                    @pl.when(p == ep)
                    def _(events=events):
                        for event in events:
                            happen(*event)

            if i == 2:
                for back in (3, 2):

                    @pl.when(p >= back)
                    def _(back=back):
                        qkv_finish(back - 1, p - back)

        dqkv[:, pl.ds(aligned(at + 128, 128), 128)] = dk_acc[...].astype(BF)
        dqkv[:, pl.ds(aligned(at + 256, 128), 128)] = dv_acc[...].astype(BF)
        cols = pl.ds(aligned(at, 128), 384)
        sums = jnp.sum(dqkv[:, cols].astype(F32), axis=0, keepdims=True)
        late[0, pl.ds(16 + c * 4 + p, 1), :] = sums[:, 0:128]
        late[0, pl.ds(24 + c * 4 + p, 1), :] = sums[:, 256:384]

        @pl.when(p == 0)
        def _():
            for load in loads[10:]:
                load.wait()

        for b in range(4):
            block = slice(b * 256, (b + 1) * 256)
            grad = dot_nn(h1t[block, :], dqkv[:, cols])
            low = grad.astype(BF)
            for s in range(16):
                for j, order in enumerate(QKV_ORDERS):
                    bqkv[p, j, slot_of(b * 16 + s, order)] = low[s * 16 : (s + 1) * 16, j * 128 : (j + 1) * 128]
            weight = wq[block, cols].astype(F32)
            weight = jnp.concatenate([feature_rows(weight[0:128]), feature_rows(weight[128:256])], axis=0)
            by_gain, by_bias = grad * weight, weight * sums
            gain_acc[block, :] = gain_acc[block, :] + by_gain[:, 0:128] + by_gain[:, 128:256] + by_gain[:, 256:384]
            bias_acc[block, :] = bias_acc[block, :] + by_bias[:, 0:128] + by_bias[:, 128:256] + by_bias[:, 256:384]

        @pl.when(p == 1)
        def _():
            for b in range(4):
                block = slice(b * 256, (b + 1) * 256)
                dh_acc[block, :] = dot_nt(dqkv[block, 0:768], wq[:, 0:768])

        qkv_start(1, p)
        return carry

    lax.fori_loop(0, 4, pair, 0)

    def tail(n):
        for k in (3, 2, 1):
            p = n + 2 - k
            if p < 4 and (k, p) not in ((2, 0), (1, 1), (1, 0)):
                qkv_finish(k, p)

    def total_of(acc):
        flat = jnp.concatenate([natural_rows(acc[g * 128 : (g + 1) * 128, :]) for g in range(8)], axis=0)
        return jnp.sum(flat.T, axis=0, keepdims=True)

    bias_sum = total_of(bias_acc)
    gain_sum = (total_of(gain_acc) - par[1:2, :] * bias_sum) / par[0:1, :]
    for l in range(8):
        late[0, l : l + 1, :] = gain_sum[:, l * 128 : (l + 1) * 128]
        late[0, 8 + l : 9 + l, :] = bias_sum[:, l * 128 : (l + 1) * 128]
    vector_start(late, late_got, vs, vr, 0)

    def dh_copy(n):
        rows = pl.ds(aligned(n * BLOCK, BLOCK), BLOCK)
        return remote(dh_send.at[rows], dh_got.at[rows], hs.at[n], hr.at[n], mate)

    def second_half(rows):
        return dh_acc[rows, :] + dot_nt(dqkv[rows, 768:1536], wq[:, 768:1536])

    for n in range(2):
        rows = pl.ds(aligned((1 - c) * 512 + n * BLOCK, BLOCK), BLOCK)
        dh_send[n * BLOCK : (n + 1) * BLOCK, :] = second_half(rows).astype(BF)
        dh_copy(n).start()
    tail(1)
    for load in loads[8:10]:
        load.wait()

    def g_src(r):
        return gin_s.at[pl.ds(r * 128, 128)]

    def g_dst(r):
        return gin_o.at[z]

    for n in range(2):
        block = slice(n * BLOCK, (n + 1) * BLOCK)
        dh = second_half(pl.ds(aligned(c * 512 + n * BLOCK, BLOCK), BLOCK))
        dh_copy(n).wait()
        xhat, rstd = norm_parts(x_own[block, :].astype(F32))
        e = (dh + dh_got[block, :].astype(F32)) * par[0:1, :]
        gin_s[block, :] = (
            dres[block, :]
            + rstd * (e - jnp.mean(e, axis=-1, keepdims=True) - xhat * jnp.mean(e * xhat, axis=-1, keepdims=True))
        ).astype(BF)
        exchange_start(place, g_src, g_dst, g_dst, gs, gr, (2 * n, 2 * n + 1))
        if n == 0:
            vector_finish(late, late_got, vs, vr, 0)
    tail(2)
    main_finish(3, OUT)
    vector_finish(late, late_got, vs, vr, 1)
    tail(3)
    vector_finish(late, late_got, vs, vr, 2)
    late_copy.start()
    tail(4)
    far_copy(fin_qkv, far_qkv, 4).start()

    own8 = pl.ds(aligned(c * 8, 8), 8)
    far_copy(fin_up, far_up, 0).wait()
    for t in range(8):
        mine, theirs = fin_up[own8, t * 256 : (t + 1) * 256], far_up[:, t * 256 : (t + 1) * 256]
        gup_o[:, t * 512 : t * 512 + 256] = jnp.where(c == 0, mine, theirs)
        gup_o[:, t * 512 + 256 : t * 512 + 512] = jnp.where(c == 0, theirs, mine)
    far_copy(fin_out, far_out, 1).wait()
    mine, theirs = fin_out[own8, :], far_out[...]
    gout_o[:, 0:512] = jnp.where(c == 0, mine, theirs)
    gout_o[:, 512:1024] = jnp.where(c == 0, theirs, mine)
    far_copy(fin_qkv, far_qkv, 4).wait()
    for j in range(3):
        mine, theirs = fin_qkv[own8, j * 512 : (j + 1) * 512], far_qkv[:, j * 512 : (j + 1) * 512]
        gqkv_o[:, j * 1024 : j * 1024 + 512] = jnp.where(c == 0, mine, theirs)
        gqkv_o[:, j * 1024 + 512 : j * 1024 + 1024] = jnp.where(c == 0, theirs, mine)
    early_copy.wait()
    small_o[4:12, :] = early[3] + early_far[...]
    small_o[12:16, :] = jnp.zeros((4, 1024), F32)
    late_copy.wait()
    total = late[3] + late_far[...]
    for n in range(4):
        for l in range(8):
            small_o[n : n + 1, l * 128 : (l + 1) * 128] = total[n * 8 + l : n * 8 + l + 1, :]

    exchange_sent(place, l_src, l_dst, ls, lr)
    exchange_sent(place, g_src, g_dst, gs, gr)
    for b in range(4):
        pltpu.make_async_copy(lout.at[pl.ds(0, 128)], lout_o.at[b], lr.at[b]).wait()
        pltpu.make_async_copy(gin_s.at[pl.ds(0, 128)], gin_o.at[b], gr.at[b]).wait()


def run_backward(*args):
    outs = (
        shaped((4, 128, 1024), BF), shaped((4, 128, 1024), BF), shaped((8, 3072), F32), shaped((8, 1024), F32),
        shaped((8, 4096), F32), shaped((32, 1024), F32), shaped((16, 1024), F32),
    )
    v = pltpu.VMEM
    return pl.pallas_call(
        backward_kernel,
        out_shape=outs,
        in_specs=[vmem()] * 4 + [anywhere()] * 11,
        out_specs=(anywhere(), anywhere()) + (vmem(),) * 5,
        scratch_shapes=[
            v((1024, 1536), BF), v((1024, 512), BF), v((1024, 512), BF), v((1024, 1024), BF), v((512, 1024), BF),
            v((512, 1024), BF), v((512, 1024), F32),
            v((1024, 1536), BF), v((1024, 1024), BF), v((1024, 1536), BF), v((1024, 128), F32), v((1024, 128), F32),
            v((16, 1024), F32), v((256, 256), F32), v((512, 256), F32), v((768, 256), F32), v((768, 256), F32),
            v((2, 8, 8, 16, 128), BF), v((8, 8, 32, 128), BF), v((4, 64, 16, 128), BF), v((4, 3, 64, 16, 128), BF),
            v((2, 8, 7, 16, 128), BF), v((8, 7, 32, 128), BF), v((4, 63, 16, 128), BF), v((4, 3, 63, 16, 128), BF),
            v((16, 2048), F32), v((16, 512), F32), v((16, 1536), F32), v((8, 2048), F32), v((8, 512), F32),
            v((8, 1536), F32), v((512, 1024), BF), v((512, 1024), BF), v((1024, 1024), F32), v((512, 1024), BF),
            v((1024, 128), F32), v((1024, 128), F32),
            v((4, 8, 1024), F32), v((3, 3, 8, 1024), F32), v((8, 1024), F32), v((4, 32, 128), F32), v((3, 3, 32, 128), F32),
            v((32, 128), F32), dma(22), dma(3, 9, 3), dma(3, 9, 3), dma(3, 4, 3, 3), dma(3, 4, 3, 3), dma(4), dma(4), dma(4), dma(4), dma(2), dma(2),
            dma(6), dma(6), dma(3, 3), dma(3, 3), dma(3, 3), dma(3, 3),
        ],
        compiler_params=pltpu.CompilerParams(collective_id=1, has_side_effects=True, vmem_limit_bytes=VMEM_LIMIT),
        name="backward",
    )(*args)


VECTORS = ((0, 8), (1, 8), (2, 16), (4, 8), (5, 8), (6, 8), (8, 32), (7, 8))


def finish_kernel(*refs):
    lout, gin, gqkv, gout, gup, gdown, sums = refs[:7]
    outs, vectors = refs[7:13], refs[13:21]
    for src, dst in zip((lout, gin, gqkv, gout, gup, gdown), outs):
        dst[...] = src[...]
    place = Place()
    device = ((place.xh * 4 + place.y) * 2 + place.c) * 8 + place.xl * 4 + place.z
    for (row, size), out in zip(VECTORS, vectors):
        first = device * size
        line = row + lax.div(first, jnp.int32(1024))
        turned = pltpu.roll(sums[pl.ds(line, 1), :], 1024 - lax.rem(first, jnp.int32(1024)), 1)
        out[...] = turned[0, :size]


def run_finish(*args):
    outs = tuple(shaped(a.shape, a.dtype) for a in args[:6]) + tuple(shaped((size,), F32) for _, size in VECTORS)
    return pl.pallas_call(
        finish_kernel,
        out_shape=outs,
        in_specs=[vmem()] * 7,
        out_specs=(vmem(),) * 14,
        name="finish",
    )(*args)


def on_device(
    block_input, segment_ids, padding_flags, cotangent, norm_one_gain, norm_one_bias, query_key_value, query_value_bias,
    out_weight, out_bias, norm_two_gain, norm_two_bias, up_weight, up_bias, down_weight, down_bias,
):
    h1, qkv, x_own, ctxh, dres, dctx, lout, upleft, downleft, bout, lse, seg, par, small = run_first(
        block_input, cotangent, segment_ids, padding_flags, norm_one_gain, norm_one_bias, query_value_bias, out_bias,
        norm_two_gain, norm_two_bias, down_bias, up_bias, query_key_value, out_weight, up_weight, down_weight,
    )
    results = run_backward(
        lse, seg, small, par, upleft, downleft, bout, qkv, dctx, ctxh, h1, lout, query_key_value, x_own, dres
    )
    lout, gin, gqkv, gout, gup, gdown, n1g, n1b, qvb, ob, n2g, n2b, ub, db = run_finish(*results)
    return (lout, gin, n1g, n1b, gqkv, qvb, gout, ob, n2g, n2b, gup, ub, gdown, db)


def solution(mesh):
    wide = Mesh(mesh.devices.reshape(2, 4, 2, 2, 4), AXES)
    rows, seq = ("xh", "y", "c"), ("xl", "z")
    everything = rows + seq
    whole = P()
    return jax.shard_map(
        on_device,
        mesh=wide,
        in_specs=(P(rows, seq, None), P(rows, None), P(rows, None), P(rows, seq, None)) + (whole,) * 12,
        out_specs=(
            P(rows, seq, None), P(rows, seq, None), P(everything), P(everything), P(everything, None), P(everything),
            P(everything, None), P(everything), P(everything), P(everything), P(everything, None), P(everything),
            P(everything, None), P(everything),
        ),
        check_vma=False,
    )
```

```python
import jax
import jax.numpy as jnp
from jax import lax
from jax.experimental import pallas as pl
from jax.experimental.pallas import tpu as pltpu
from jax.sharding import Mesh, PartitionSpec as P

BF = jnp.bfloat16
F32 = jnp.float32
AXES = ("xh", "y", "c", "xl", "z")
BY_MESH = pl.DeviceIdType.MESH
DIMS = ("x1", "y1", "z1", "x0", "y0", "z0")
UP_ORDERS = (("y1", "y0", "x1", "z", "x0"), ("x1", "y0", "y1", "x0", "z"))
DOWN_GROUPS = (
    (0, 3, ("z1", "z0", "x0"), ("y", "x1")),
    (3, 6, ("z0", "x0", "z1"), ("x1", "y")),
    (6, 8, ("x0", "z1", "z0"), ("x1", "y")),
)
OUT_ORDERS = (("y", "x", "z"), ("y", "z", "x"), ("y", "x", "z"), ("y", "z", "x"))
QKV_ORDERS = (("x", "z", "y"), ("z", "x", "y"), ("y", "z", "x"))
LAG = {1: 2, 2: 3, 3: 4}
BLOCK = 256
GELU = 0.7978845608028654
CUBIC = 0.044715
EPS = 1e-05
MASKED = -1e30
VMEM_LIMIT = 60 * 1024 * 1024


def dot_nn(a, b):
    return lax.dot_general(a, b, (((1,), (0,)), ((), ())), preferred_element_type=F32)


def dot_nt(a, b):
    return lax.dot_general(a, b, (((1,), (1,)), ((), ())), preferred_element_type=F32)


def dot_tn(a, b):
    return lax.dot_general(a, b, (((0,), (0,)), ((), ())), preferred_element_type=F32)


class Place:
    def __init__(self):
        self.xh, self.y, self.c, self.xl, self.z = (lax.axis_index(a) for a in AXES)
        two = jnp.int32(2)
        self.bits = {
            "x1": self.xh,
            "x0": lax.rem(self.xl + self.xh, two),
            "y1": lax.div(self.y, two),
            "y0": lax.rem(self.y + lax.div(self.y, two), two),
            "z1": lax.div(self.z, two),
            "z0": lax.rem(self.z + lax.div(self.z, two), two),
            "x": 2 * self.xh + self.xl,
            "y": self.y,
            "z": self.z,
        }
        names = ("c", "x1", "y1", "z1", "x0", "y0", "z0")
        self.partners = {name: self.find_partner(name) for name in names}
        self.rings = {(axis, s): self.find_ring(axis, s) for axis in "xyz" for s in (1, 2, 3)}
        self.send, self.keep = {}, {}

    def prepare(self, orders):
        for order in orders:
            off = jnp.int32(0)
            for k, name in enumerate(order, 1):
                n = left_after(order, k)
                for s in range(1, width(name)):
                    to = 1 - self.bits[name] if width(name) == 2 else lax.rem(self.bits[name] + s, jnp.int32(4))
                    self.send[order, k, s] = off + to * n
                off = off + self.bits[name] * n
                self.keep[order, k] = off

    def partner(self, name):
        return self.partners[name]

    def ring(self, axis, step):
        return self.rings[axis, step]

    def find_partner(self, name):
        xh, y, c, xl, z = self.xh, self.y, self.c, self.xl, self.z
        if name == "c":
            c = 1 - c
        elif name == "x0":
            xl = 1 - xl
        elif name == "x1":
            xh, xl = 1 - xh, 1 - xl
        elif name == "y0":
            y = y + 1 - 2 * lax.rem(y, jnp.int32(2))
        elif name == "y1":
            y = 3 - y
        elif name == "z0":
            z = z + 1 - 2 * lax.rem(z, jnp.int32(2))
        elif name == "z1":
            z = 3 - z
        return (xh, y, c, xl, z)

    def find_ring(self, axis, step):
        four, two = jnp.int32(4), jnp.int32(2)
        xh, y, c, xl, z = self.xh, self.y, self.c, self.xl, self.z
        if axis == "x":
            at = lax.rem(2 * xh + xl + step, four)
            xh, xl = lax.div(at, two), lax.rem(at, two)
        elif axis == "y":
            y = lax.rem(y + step, four)
        else:
            z = lax.rem(z + step, four)
        return (xh, y, c, xl, z)

    def exchange(self, r):
        return (self.xh, self.y, self.xl, self.c, jnp.int32(r))

    def is_self(self, r):
        return (self.c == self.xl) & (self.z == r)


def bits_of(s):
    xh, y, xl, z = s >> 5, (s >> 3) & 3, (s >> 2) & 1, s & 3
    return {
        "x1": xh, "y1": y >> 1, "z1": z >> 1, "x0": xl ^ xh, "y0": (y & 1) ^ (y >> 1), "z0": (z & 1) ^ (z >> 1),
        "x": 2 * xh + xl, "y": y, "z": z,
    }


def width(name):
    return 4 if len(name) == 1 else 2


def left_after(order, k):
    n = 1
    for name in order[k:]:
        n *= width(name)
    return n


def slot_of(s, order):
    bits, slot = bits_of(s), 0
    for name in order:
        slot = width(name) * slot + bits[name]
    return slot


def region(order, k):
    return sum((width(name) - 1) * left_after(order, j + 1) for j, name in enumerate(order[: k - 1]))


class Scatter:
    def __init__(self, place, k, order, buf, got, lead, sends, recvs, at):
        name = order[k - 1]
        n = left_after(order, k)
        self.copies = []
        for s in range(1, width(name)):
            peer = place.partner(name) if width(name) == 2 else place.ring(name, s)
            self.copies.append(
                pltpu.make_async_remote_copy(
                    src_ref=buf.at[lead + (pl.ds(place.send[order, k, s], n),)],
                    dst_ref=got.at[lead + (pl.ds(region(order, k) + (s - 1) * n, n),)],
                    send_sem=sends.at[at + (s - 1,)],
                    recv_sem=recvs.at[at + (s - 1,)],
                    device_id=peer,
                    device_id_type=BY_MESH,
                )
            )

    def start(self):
        for copy in self.copies:
            copy.start()

    def wait(self):
        for copy in self.copies:
            copy.wait()


def scatter_sum(place, k, order, buf, got, lead):
    n = left_after(order, k)
    mine = lead + (pl.ds(place.keep[order, k], n),)
    if width(order[k - 1]) == 2 and k < len(order):
        return mine, buf[mine] + got[lead + (pl.ds(region(order, k), n),)]
    total = buf[mine].astype(F32)
    for s in range(1, width(order[k - 1])):
        total = total + got[lead + (pl.ds(region(order, k) + (s - 1) * n, n),)].astype(F32)
    return mine, total


def scatter_add(place, k, order, buf, got, lead):
    mine, total = scatter_sum(place, k, order, buf, got, lead)
    buf[mine] = total.astype(BF)


def scatter_last(place, order, buf, got, lead):
    _, total = scatter_sum(place, len(order), order, buf, got, lead)
    return total.reshape(total.shape[-2:])


def feature_rows(flat):
    parts = []
    for g in range(8):
        for c in range(2):
            parts.append(flat[(c * 8 + g) * 8 : (c * 8 + g + 1) * 8])
    return jnp.concatenate(parts, axis=0)


def natural_rows(flat):
    return jnp.concatenate([flat[(g * 2 + c) * 8 : (g * 2 + c + 1) * 8] for c in range(2) for g in range(8)], axis=0)


def transpose_features(src, dst, tokens):
    def body(f, carry):
        block = src[tokens, pl.ds(pl.multiple_of(f * 128, 128), 128)].astype(F32)
        dst[pl.ds(pl.multiple_of(f * 128, 128), 128), tokens] = feature_rows(block.T).astype(BF)
        return carry

    lax.fori_loop(0, 8, body, 0)


def norm_parts(v):
    center = v - jnp.mean(v, axis=-1, keepdims=True)
    rstd = lax.rsqrt(jnp.mean(center * center, axis=-1, keepdims=True) + EPS)
    return center * rstd, rstd


def aligned(v, m):
    return pl.multiple_of(v, m)


def window(i):
    return max(0, i - 2) * BLOCK, (i + 1) * BLOCK


def remote(src, dst, send, recv, device):
    return pltpu.make_async_remote_copy(
        src_ref=src, dst_ref=dst, send_sem=send, recv_sem=recv, device_id=device, device_id_type=BY_MESH
    )


def greet(place, devices, with_exchange):
    barrier = pltpu.get_barrier_semaphore()
    count = jnp.int32(len(devices))
    for d in devices:
        pl.semaphore_signal(barrier, inc=1, device_id=d, device_id_type=BY_MESH)
    if with_exchange:
        for r in range(4):

            @pl.when(jnp.logical_not(place.is_self(r)))
            def _(r=r):
                pl.semaphore_signal(barrier, inc=1, device_id=place.exchange(r), device_id_type=BY_MESH)

        count = count + 4 - jnp.where(place.c == place.xl, 1, 0)
    pl.semaphore_wait(barrier, count)


def exchange_start(place, src_of, dst_of, own_dst_of, sends, recvs, which=(0, 1, 2, 3)):
    for r in which:
        own = place.is_self(r)

        @pl.when(own)
        def _(r=r):
            pltpu.make_async_copy(src_of(r), own_dst_of(r), recvs.at[place.z]).start()

        @pl.when(jnp.logical_not(own))
        def _(r=r):
            remote(src_of(r), dst_of(r), sends.at[r], recvs.at[place.z], place.exchange(r)).start()


def exchange_sent(place, src_of, dst_of, sends, recvs):
    for r in range(4):

        @pl.when(jnp.logical_not(place.is_self(r)))
        def _(r=r):
            remote(src_of(r), dst_of(r), sends.at[r], recvs.at[place.z], place.exchange(r)).wait_send()


def vmem(n=None):
    return pl.BlockSpec(memory_space=pltpu.VMEM)


def anywhere():
    return pl.BlockSpec(memory_space=pl.ANY)


def dma(*shape):
    return pltpu.SemaphoreType.DMA(shape)


def shaped(shape, dtype):
    return jax.ShapeDtypeStruct(shape, dtype)


def first_kernel(
    x_in, c_in, seg_in, flag_in, g1, b1_, bqv, bo, g2, b2_, bd, bu, wqkv, wout, wup, wdown,
    h1_o, qkv_o, x_o, ctxh_o, dres_o, dctx_o, lout_o, upleft_o, downleft_o, bout_o, lse_o, seg_o, par, small_o,
    hid, cot, qkv, x_own, ctxh, ctxp, resid, h2t, lse_acc, wq, wo, wu, wd, down_acc, dh_acc, act_s, dup_s, dat, lout, dctx,
    bup, rup, bdown, rdown, bout, upleft, downleft, seg_got,
    xs, xr, cs, cr, hs, hr, fs, fr, ts, tr, gs, gr, ss, sr, ws, us, ds, es, er, ups, upr, dns, dnr, os,
):
    place = Place()
    c, xl, z = place.c, place.xl, place.z
    mate = place.partner("c")
    place.prepare(UP_ORDERS + tuple(g[2] for g in DOWN_GROUPS))
    own = pl.ds(aligned(c * 512, 512), 512)
    far = pl.ds(aligned((1 - c) * 512, 512), 512)
    loads = [
        pltpu.make_async_copy(
            wqkv.at[:, pl.ds(aligned(j * 1024 + c * 512, 512), 512)], wq.at[:, pl.ds(j * 512, 512)], ws.at[j]
        )
        for j in range(3)
    ]
    loads.append(pltpu.make_async_copy(wout, wo, ws.at[3]))

    def up_load(t):
        return pltpu.make_async_copy(
            wup.at[:, pl.ds(aligned((2 * t + c) * 256, 256), 256)], wu.at[lax.rem(t, jnp.int32(4))], us.at[t]
        )

    def down_load(t):
        return pltpu.make_async_copy(
            wdown.at[pl.ds(aligned((2 * t + c) * 256, 256), 256)], wd.at[lax.rem(t, jnp.int32(4))], ds.at[t]
        )

    def saves(n, src, dst):
        return pltpu.make_async_copy(src, dst, os.at[n])

    for load in loads:
        load.start()
    for t in range(4):
        up_load(jnp.int32(t)).start()
        down_load(jnp.int32(t)).start()
    greet(place, [mate] + [place.partner(d) for d in DIMS], True)

    def x_src(r):
        return x_in.at[r]

    def x_dst(r):
        return x_own.at[pl.ds(aligned(z * 128, 128), 128)]

    def c_src(r):
        return c_in.at[r]

    def c_dst(r):
        return cot.at[pl.ds(aligned(xl * 512 + z * 128, 128), 128)]

    exchange_start(place, x_src, x_dst, x_dst, xs, xr)
    seg_out = [remote(ref, seg_got.at[n], ss.at[n], sr.at[n], mate) for n, ref in enumerate((seg_in, flag_in))]
    for copy in seg_out:
        copy.start()
    for n, ref in enumerate((g1, b1_, bqv, bqv, bo, g2, b2_, bd, bu, bu, bu, bu)):
        first = {3: 1024, 9: 1024, 10: 2048, 11: 3072}.get(n, 0)
        par[n : n + 1, :] = ref[first : first + 1024].astype(F32).reshape(1, 1024)
    par[12:16, :] = jnp.zeros((4, 1024), F32)

    for copy in seg_out:
        copy.wait()
    own_seg, own_flag = seg_in[pl.ds(z, 1), :], flag_in[pl.ds(z, 1), :]
    far_seg, far_flag = seg_got[0, pl.ds(z, 1), :], seg_got[1, pl.ds(z, 1), :]
    near = jnp.where(c == xl, 1, 0)
    seg_row = jnp.where(near == 1, own_seg, far_seg).astype(F32)
    flag_row = jnp.where(near == 1, own_flag, far_flag)
    key_row = jnp.where(flag_row == 0, seg_row, -1.0)
    seg_o[...] = jnp.concatenate([seg_row, key_row, jnp.zeros((6, 1024), F32)], axis=0)
    seg_col = jnp.broadcast_to(seg_row, (128, 1024)).T
    for i in range(4):
        w0, w1 = window(i)
        rows = lax.broadcasted_iota(jnp.int32, (BLOCK, w1 - w0), 0) + i * BLOCK
        cols = lax.broadcasted_iota(jnp.int32, (BLOCK, w1 - w0), 1) + w0
        same = seg_col[i * BLOCK : (i + 1) * BLOCK, 0:1] == key_row[:, w0:w1]
        dh_acc[i * BLOCK : (i + 1) * BLOCK, 0 : w1 - w0] = jnp.where(
            (same & (cols <= rows)) | (rows == cols), 0.0, MASKED
        )
    lse_acc[...] = jnp.zeros_like(lse_acc)

    gain_one, bias_one = par[0:1, :], par[1:2, :]

    def block_copy(ref, b, mine, sends, recvs):
        half = c if mine else 1 - c
        rows = pl.ds(aligned(half * 512 + b * 128, 128), 128)
        return remote(ref.at[rows], ref.at[rows], sends.at[b], recvs.at[b], mate)

    for b in range(4):
        pltpu.make_async_copy(x_in.at[0], x_own.at[b * 128 : (b + 1) * 128], xr.at[b]).wait()
        xhat, _ = norm_parts(x_own[b * 128 : (b + 1) * 128].astype(F32))
        hid[pl.ds(aligned(c * 512 + b * 128, 128), 128)] = (xhat * gain_one + bias_one).astype(BF)
        block_copy(hid, b, True, hs, hr).start()
    exchange_start(place, c_src, c_dst, c_dst, cs, cr)
    saves(0, x_own, x_o).start()

    for load in loads[:3]:
        load.wait()
    zero = jnp.zeros((1, 512), F32)
    bias = jnp.concatenate([par[2:3, own], zero, par[3:4, own]], axis=1)

    def project(first):
        def body(n, carry):
            rows = pl.ds(aligned(first + n * BLOCK, BLOCK), BLOCK)
            qkv[rows, :] = (dot_nn(hid[rows, :], wq[...]) + bias).astype(BF)
            return carry

        lax.fori_loop(0, 2, body, 0)

    project(c * 512)
    for b in range(4):
        block_copy(hid, b, False, hs, hr).wait_recv()
    saves(1, hid, h1_o).start()
    project((1 - c) * 512)
    saves(2, qkv, qkv_o).start()

    lane = lax.broadcasted_iota(jnp.int32, (BLOCK, 128), 1)

    def ctx_copy(p, half):
        return remote(
            ctxh.at[far, pl.ds(aligned(p * 128, 128), 128)],
            ctxp.at[:, pl.ds(aligned(half * 512 + p * 128, 128), 128)],
            ts.at[p], tr.at[p], mate,
        )

    def attend(p, carry):
        lo = aligned(p * 128, 128)
        for i in range(4):
            w0, w1 = window(i)
            rows = slice(i * BLOCK, (i + 1) * BLOCK)
            query = qkv[rows, pl.ds(lo, 128)] * jnp.asarray(0.125, BF)
            keys = qkv[w0:w1, pl.ds(aligned(512 + lo, 128), 128)]
            values = qkv[w0:w1, pl.ds(aligned(1024 + lo, 128), 128)]
            zero = jnp.zeros_like(query)
            both = jnp.concatenate([jnp.where(lane < 64, query, zero), jnp.where(lane < 64, zero, query)], axis=0)
            mask = dh_acc[rows, 0 : w1 - w0]
            scores = dot_nt(both, keys) + jnp.concatenate([mask, mask], axis=0)
            top = jnp.max(scores, axis=-1, keepdims=True)
            expo = jnp.exp(scores - top)
            found = dot_nn(expo.astype(BF), jnp.concatenate([values, jnp.ones_like(values)], axis=1))
            total = found[:, 128:256]
            log_total = top + jnp.log(total)
            outs = found[:, 0:128] / total
            lse_acc[rows, :] = jnp.where(
                lane == 2 * p, log_total[:BLOCK], jnp.where(lane == 2 * p + 1, log_total[BLOCK:], lse_acc[rows, :])
            )
            ctxh[rows, pl.ds(lo, 128)] = jnp.where(lane < 64, outs[:BLOCK], outs[BLOCK:]).astype(BF)

        @pl.when(p == 3)
        def _():
            saves(1, hid, h1_o).wait()
            saves(2, qkv, qkv_o).wait()
            for b in range(4):
                block_copy(hid, b, True, hs, hr).wait_send()

        ctx_copy(p, c).start()
        ctxp[:, pl.ds(aligned(c * 512 + lo, 128), 128)] = ctxh[own, pl.ds(lo, 128)]
        return carry

    lax.fori_loop(0, 4, attend, 0)
    saves(3, ctxh, ctxh_o).start()
    lse_o[...] = lse_acc[...].T[0:16, :]

    for b in range(4):
        pltpu.make_async_copy(c_in.at[0], cot.at[pl.ds(aligned(c * 512 + b * 128, 128), 128)], cr.at[b]).wait()
        block_copy(cot, b, True, fs, fr).start()

    loads[3].wait()
    for p in range(4):
        ctx_copy(p, 1 - c).wait_recv()

    def h2_copy(n, half):
        rows = pl.ds(aligned(half * 512 + n * BLOCK, BLOCK), BLOCK)
        return remote(hid.at[rows], hid.at[rows], gs.at[n], gr.at[n], mate)

    def output(n, carry):
        rows = pl.ds(aligned(n * BLOCK, BLOCK), BLOCK)
        res = x_own[rows, :].astype(F32) + (dot_nn(ctxp[rows, :], wo[...]) + par[4:5, :])
        resid[rows, :] = res
        xhat, _ = norm_parts(res)
        hid[pl.ds(aligned(c * 512 + n * BLOCK, BLOCK), BLOCK), :] = (xhat * par[5:6, :] + par[6:7, :]).astype(BF)
        h2_copy(n, c).start()
        return carry

    lax.fori_loop(0, 2, output, 0)
    small_o[...] = jnp.zeros_like(small_o)
    transpose_features(hid, h2t, own)
    for n in range(2):
        h2_copy(n, 1 - c).wait_recv()
    transpose_features(hid, h2t, far)
    for b in range(4):
        block_copy(cot, b, False, fs, fr).wait_recv()

    def up_copy(k, t, j):
        return Scatter(place, k, UP_ORDERS[j], bup, rup, (t, j), ups, upr, (k - 1, t, j))

    def down_copy(k, t, g):
        p0, p1, order, _ = DOWN_GROUPS[g]
        return Scatter(place, k, order, bdown, rdown, (t, slice(p0, p1)), dns, dnr, (k - 1, t, g))

    def start(k, t):
        for j in range(2):
            up_copy(k, t, j).start()
        for g in range(3):
            down_copy(k, t, g).start()

    def tile_slot(t, rest):
        bits = {"x1": lax.div(t, jnp.int32(4)), "y": lax.rem(t, jnp.int32(4))}
        slot = jnp.int32(0)
        for name in rest:
            slot = width(name) * slot + bits[name]
        return slot

    def finish(k, t):
        for j in range(2):
            up_copy(k, t, j).wait()
        for g in range(3):
            down_copy(k, t, g).wait()
        for j, order in enumerate(UP_ORDERS):
            mine, total = scatter_sum(place, k, order, bup, rup, (t, j))
            if k < 3:
                bup[mine] = total.astype(BF)
            else:
                upleft[j, t] = total.astype(BF)
        for p0, p1, order, rest in DOWN_GROUPS:
            for p in range(p0, p1):
                mine, total = scatter_sum(place, k, order, bdown, rdown, (t, p))
                if k < 3:
                    bdown[mine] = total.astype(BF)
                else:
                    downleft[p, pl.ds(tile_slot(t, rest), 1)] = total.astype(BF)
        if k < 3:
            start(k + 1, t)

    def tile(t, carry):
        four = jnp.int32(4)
        ring = lax.rem(t, four)
        up_load(t).wait()
        down_load(t).wait()
        col = 2 * t + c
        up_row = 8 + lax.div(col, four)
        up_cols = pl.ds(aligned(lax.rem(col, four) * 256, 256), 256)
        up_bias = par[pl.ds(up_row, 1), up_cols]
        dbias = jnp.zeros((1, 256), F32)
        for b in range(4):
            rows = slice(b * BLOCK, (b + 1) * BLOCK)
            u = dot_nn(hid[rows, :], wu[ring]) + up_bias
            dact = dot_nt(cot[rows, :], wd[ring])
            square = u * u
            th = jnp.tanh(GELU * u * (1.0 + CUBIC * square))
            act_s[rows, :] = (0.5 * u * (1.0 + th)).astype(BF)
            slope = 0.5 * (1.0 + th) + 0.5 * u * (1.0 - th * th) * (GELU * (1.0 + (3.0 * CUBIC) * square))
            dup = (dact * slope).astype(BF)
            dup_s[rows, :] = dup
            dbias = dbias + jnp.sum(dup.astype(F32), axis=0, keepdims=True)
        small_o[pl.ds(up_row, 1), up_cols] = dbias

        for k in (3, 2, 1):

            @pl.when(t >= LAG[k])
            def _(k=k):
                finish(k, t - LAG[k])

        xh = lax.div(t, four)
        grad = dot_tn(act_s[...], cot[...]).astype(BF)
        for s in range(8):
            bits = bits_of(s)
            x0 = lax.rem(xh + (s >> 2), jnp.int32(2))
            for p0, p1, order, _ in DOWN_GROUPS:
                fixed = sum(bits[name] << (2 - n) for n, name in enumerate(order) if name != "x0")
                slot = fixed + x0 * (1 << (2 - order.index("x0")))
                for j in range(p0, p1):
                    bdown[t, j, slot] = grad[s * 32 : (s + 1) * 32, j * 128 : (j + 1) * 128]
        for b in range(4):
            grad = dot_nn(h2t[b * 256 : (b + 1) * 256, :], dup_s[...]).astype(BF)
            for s in range(16):
                for j, order in enumerate(UP_ORDERS):
                    bup[t, j, slot_of(b * 16 + s, order)] = grad[s * 16 : (s + 1) * 16, j * 128 : (j + 1) * 128]
        start(1, t)

        @pl.when(t == 0)
        def _():
            for b in range(4):
                rows = slice(b * BLOCK, (b + 1) * BLOCK)
                down_acc[rows, :] = dot_nn(act_s[rows, :], wd[ring])
                dh_acc[rows, :] = dot_nt(dup_s[rows, :], wu[ring])

        @pl.when(t > 0)
        def _():
            for b in range(4):
                rows = slice(b * BLOCK, (b + 1) * BLOCK)
                down_acc[rows, :] = down_acc[rows, :] + dot_nn(act_s[rows, :], wd[ring])
                dh_acc[rows, :] = dh_acc[rows, :] + dot_nt(dup_s[rows, :], wu[ring])

        @pl.when(t < 4)
        def _():
            up_load(t + 4).start()
            down_load(t + 4).start()

        return carry

    lax.fori_loop(0, 8, tile, 0)

    def rounds(n):
        for k in (3, 2, 1):
            if 0 <= n - LAG[k] < 8:
                finish(k, n - LAG[k])

    dh_send, dh_got = qkv.at[0:512, 0:1024], qkv.at[512:1024, 0:1024]
    dn_send, dn_got = wq.at[0:512, 0:1024], wq.at[512:1024, 0:1024]
    dc_send = qkv.at[0:512, 1024:1536]
    ctxt = wq.at[:, 1024:1536]
    wo_send, wo_got = bup.at[0:2], bup.at[2:4]
    dh_send[...] = dh_acc[far, :].astype(BF)
    dh_copy = remote(dh_send, dh_got, es.at[0], er.at[0], mate)
    dh_copy.start()
    dn_send[...] = down_acc[far, :].astype(BF)
    dn_copy = remote(dn_send, dn_got, es.at[1], er.at[1], mate)
    dn_copy.start()
    rounds(8)

    transpose_features(ctxp, ctxt, slice(0, 512))
    dh_copy.wait()
    dn_copy.wait()

    def norm_back(n, sums):
        gain_sum, bias_sum, out_sum, down_sum = sums
        rows = pl.ds(aligned(n * 128, 128), 128)
        mine = pl.ds(aligned(c * 512 + n * 128, 128), 128)
        res = resid[rows, :]
        lout[rows, :] = (res + (down_acc[mine, :] + dn_got[rows, :].astype(F32) + par[7:8, :])).astype(BF)
        xhat, rstd = norm_parts(res)
        dn = dh_acc[mine, :] + dh_got[rows, :].astype(F32)
        e = dn * par[5:6, :]
        cf = cot[mine, :].astype(F32)
        dres = cf + rstd * (
            e - jnp.mean(e, axis=-1, keepdims=True) - xhat * jnp.mean(e * xhat, axis=-1, keepdims=True)
        )
        resid[rows, :] = dres
        low = dres.astype(BF)
        dat[rows, :] = low
        return (
            gain_sum + jnp.sum(dn * xhat, axis=0, keepdims=True),
            bias_sum + jnp.sum(dn, axis=0, keepdims=True),
            out_sum + jnp.sum(low.astype(F32), axis=0, keepdims=True),
            down_sum + jnp.sum(cf, axis=0, keepdims=True),
        )

    nothing = jnp.zeros((1, 1024), F32)
    gain_sum, bias_sum, out_sum, down_sum = lax.fori_loop(0, 4, norm_back, (nothing,) * 4)
    small_o[5:6, :] = gain_sum
    small_o[6:7, :] = bias_sum
    small_o[4:5, :] = out_sum
    small_o[7:8, :] = down_sum
    saves(4, resid, dres_o).start()
    saves(5, lout, lout_o).start()

    dc_send[...] = dot_nt(dat[...], wo[far, :]).astype(BF)
    dc_copy = remote(dc_send, dctx.at[own], es.at[2], er.at[2], mate)
    dc_copy.start()
    rounds(9)

    def out_grad(cols, dst, lead):
        for b in range(4):
            grad = dot_nn(ctxt[b * 256 : (b + 1) * 256, :], dat[:, cols]).astype(BF)
            for s in range(16):
                for j, order in enumerate(OUT_ORDERS):
                    dst[lead(j) + (slot_of(b * 16 + s, order),)] = grad[s * 16 : (s + 1) * 16, j * 128 : (j + 1) * 128]

    out_grad(far, wo_send, lambda j: (j // 2, j % 2))
    wo_copy = remote(wo_send, wo_got, es.at[3], er.at[3], mate)
    wo_copy.start()
    dctx[own, :] = dot_nt(dat[...], wo[own, :]).astype(BF)
    rounds(10)
    out_grad(own, bout, lambda j: (j,))
    dc_copy.wait_send()
    remote(dc_send, dctx.at[far], es.at[2], er.at[2], mate).wait_recv()
    saves(6, dctx, dctx_o).start()
    for n in range(11, 8 + LAG[3]):
        rounds(n)
    saves(7, upleft, upleft_o).start()
    saves(8, downleft, downleft_o).start()
    wo_copy.wait()
    for j in range(4):
        bout[j] = bout[j] + wo_got[j // 2, j % 2]
    saves(9, bout, bout_o).start()

    exchange_sent(place, x_src, x_dst, xs, xr)
    exchange_sent(place, c_src, c_dst, cs, cr)
    for b in range(4):
        block_copy(cot, b, True, fs, fr).wait_send()
        ctx_copy(b, c).wait_send()
    for n in range(2):
        h2_copy(n, c).wait_send()
    saves(0, x_own, x_o).wait()
    saves(3, ctxh, ctxh_o).wait()
    saves(4, resid, dres_o).wait()
    saves(5, lout, lout_o).wait()
    saves(6, dctx, dctx_o).wait()
    saves(7, upleft, upleft_o).wait()
    saves(8, downleft, downleft_o).wait()
    saves(9, bout, bout_o).wait()


def run_first(*args):
    outs = (
        shaped((1024, 1024), BF), shaped((1024, 1536), BF), shaped((512, 1024), BF), shaped((1024, 512), BF),
        shaped((512, 1024), F32), shaped((1024, 512), BF), shaped((512, 1024), BF), shaped((2, 8, 8, 16, 128), BF),
        shaped((8, 8, 32, 128), BF), shaped((4, 64, 16, 128), BF), shaped((16, 1024), F32), shaped((8, 1024), F32),
        shaped((16, 1024), F32), shaped((16, 1024), F32),
    )
    v = pltpu.VMEM
    return pl.pallas_call(
        first_kernel,
        out_shape=outs,
        in_specs=[anywhere(), anywhere()] + [vmem()] * 10 + [anywhere()] * 4,
        out_specs=(anywhere(),) * 10 + (vmem(),) * 4,
        scratch_shapes=[
            v((1024, 1024), BF), v((1024, 1024), BF), v((1024, 1536), BF), v((512, 1024), BF), v((1024, 512), BF),
            v((512, 1024), BF), v((512, 1024), F32), v((1024, 1024), BF), v((1024, 128), F32), v((1024, 1536), BF),
            v((1024, 1024), BF), v((4, 1024, 256), BF), v((4, 256, 1024), BF), v((1024, 1024), F32),
            v((1024, 1024), F32), v((1024, 256), BF), v((1024, 256), BF), v((512, 1024), BF), v((512, 1024), BF),
            v((1024, 512), BF), v((8, 2, 64, 16, 128), BF), v((8, 2, 56, 16, 128), BF), v((8, 8, 8, 32, 128), BF),
            v((8, 8, 7, 32, 128), BF), v((4, 64, 16, 128), BF), v((2, 8, 8, 16, 128), BF), v((8, 8, 32, 128), BF),
            v((2, 4, 1024), jnp.int32),
            dma(4), dma(4), dma(4), dma(4), dma(4), dma(4), dma(4), dma(4), dma(4), dma(4), dma(2), dma(2), dma(2),
            dma(2), dma(4), dma(8), dma(8), dma(4), dma(4), dma(3, 8, 2, 1), dma(3, 8, 2, 1), dma(3, 8, 3, 1),
            dma(3, 8, 3, 1), dma(10),
        ],
        compiler_params=pltpu.CompilerParams(collective_id=0, has_side_effects=True, vmem_limit_bytes=VMEM_LIMIT),
        name="first",
    )(*args)


MAIN = (
    tuple((0, (j, slice(0, 8)), UP_ORDERS[j][3:]) for j in range(2))
    + tuple((1, (slice(p0, p1),), rest) for p0, p1, _, rest in DOWN_GROUPS)
    + tuple((2, (j,), order) for j, order in enumerate(OUT_ORDERS))
)
LEFT = (0, 1, 2, 3, 4)
OUT = (5, 6, 7, 8)
EVENTS = {
    (1, 0): (("left", 1), ("early", 0)),
    (2, 0): (("left", 2), ("early", 1)),
    (2, 1): (("out", 1),),
    (3, 0): (("early", 2),),
    (3, 2): (("out", 2),),
}


def backward_kernel(
    lse, seg, small_in, par, upleft, downleft, bout_in, qkv_in, dctx_in, ctxh_in, h1_in, lout_in, wqkv, x_in, dres_in,
    lout_o, gin_o, gqkv_o, gout_o, gup_o, gdown_o, small_o,
    qkv, dctx, ctxh, h1, lout, x_own, dres,
    wq, h1t, dqkv, dk_acc, dv_acc, drow, t0, t1, t2, t3, bup, bdown, bout, bqkv, rup, rdown, rout, rqkv,
    fin_up, fin_out, fin_qkv, far_up, far_out, far_qkv, dh_send, dh_got, dh_acc, gin_s, gain_acc, bias_acc,
    early, early_got, early_far, late, late_got, late_far,
    ws, ms, mr, qs, qr, ls, lr, gs, gr, hs, hr, es, er, ps, pr, vs, vr,
):
    place = Place()
    c, xl, z = place.c, place.xl, place.z
    mate = place.partner("c")
    place.prepare(tuple(order for _, _, order in MAIN) + QKV_ORDERS)
    moves = (
        (upleft, bup), (downleft, bdown), (bout_in, bout), (qkv_in, qkv), (dctx_in, dctx), (ctxh_in, ctxh), (h1_in, h1),
        (lout_in, lout), (x_in, x_own), (dres_in, dres),
    )
    loads = [pltpu.make_async_copy(src, dst, ws.at[n]) for n, (src, dst) in enumerate(moves)]
    for p in range(4):
        for j in range(3):
            loads.append(
                pltpu.make_async_copy(
                    wqkv.at[:, pl.ds(aligned(j * 1024 + c * 512 + p * 128, 128), 128)],
                    wq.at[:, pl.ds(p * 384 + j * 128, 128)],
                    ws.at[10 + p * 3 + j],
                )
            )
    for load in loads:
        load.start()
    peers = [mate] + [place.partner(d) for d in DIMS] + [place.ring(a, s) for a in "xyz" for s in (1, 2, 3)]
    greet(place, peers, True)

    def l_src(r):
        return lout.at[pl.ds(r * 128, 128)]

    def l_dst(r):
        return lout_o.at[z]

    for load in loads[:3]:
        load.wait()
    bufs, gots = (bup, bdown, bout), (rup, rdown, rout)

    def main_copy(k, n):
        which, lead, order = MAIN[n]
        return Scatter(place, k, order, bufs[which], gots[which], lead, ms, mr, (k - 1, n))

    def main_start(k, which):
        for n in which:
            main_copy(k, n).start()

    def main_finish(k, which):
        for n in which:
            main_copy(k, n).wait()
        for n in which:
            b, lead, order = MAIN[n]
            if k < len(order):
                scatter_add(place, k, order, bufs[b], gots[b], lead)
        if k < len(MAIN[which[0]][2]):
            main_start(k + 1, which)
        elif which is LEFT:
            left_last()
        else:
            out_last()

    def vector_copy(ref, got, sends, recvs, n, s):
        return remote(ref.at[n], got.at[n, s - 1], sends.at[n, s - 1], recvs.at[n, s - 1], place.ring("zxy"[n], s))

    def vector_start(ref, got, sends, recvs, n):
        for s in (1, 2, 3):
            vector_copy(ref, got, sends, recvs, n, s).start()

    def vector_finish(ref, got, sends, recvs, n):
        for s in (1, 2, 3):
            vector_copy(ref, got, sends, recvs, n, s).wait()
        ref[n + 1] = ref[n] + got[n, 0] + got[n, 1] + got[n, 2]
        if n < 2:
            vector_start(ref, got, sends, recvs, n + 1)

    early_copy = remote(early.at[3], early_far, es.at[3], er.at[3], mate)
    late_copy = remote(late.at[3], late_far, es.at[5], er.at[5], mate)

    def happen(what, k):
        if what == "left":
            main_finish(k, LEFT)
        elif what == "out":
            main_finish(k, OUT)
        else:
            vector_finish(early, early_got, ps, pr, k)
            if k == 2:
                early_copy.start()

    main_start(1, LEFT)
    early[0] = small_in[4:12, :]
    vector_start(early, early_got, ps, pr, 0)
    main_start(1, OUT)
    loads[7].wait()
    exchange_start(place, l_src, l_dst, l_dst, ls, lr)
    late[0] = jnp.zeros((32, 128), F32)

    key_col = jnp.broadcast_to(seg[1:2, :], (128, 1024)).T
    for i, ref in enumerate((t0, t1, t2, t3)):
        w0, w1 = window(i)
        rows = lax.broadcasted_iota(jnp.int32, (w1 - w0, BLOCK), 0) + w0
        cols = lax.broadcasted_iota(jnp.int32, (w1 - w0, BLOCK), 1) + i * BLOCK
        same = key_col[w0:w1, 0:1] == seg[0:1, i * BLOCK : (i + 1) * BLOCK]
        ref[...] = jnp.where((same & (rows <= cols)) | (rows == cols), 0.0, MASKED)
    for load in loads[3:7]:
        load.wait()
    transpose_features(h1, h1t, slice(0, 1024))
    gain_acc[...] = jnp.zeros_like(gain_acc)
    bias_acc[...] = jnp.zeros_like(bias_acc)

    lane = lax.broadcasted_iota(jnp.int32, (BLOCK, 128), 1)
    row = lax.broadcasted_iota(jnp.int32, (128, BLOCK), 0)
    head_of = lax.broadcasted_iota(jnp.int32, (16, 128), 1)
    row_of = lax.broadcasted_iota(jnp.int32, (16, 128), 0)
    pick = jnp.where(lax.div(head_of, jnp.int32(64)) == row_of, 1.0, 0.0).astype(BF)

    def far_copy(src, dst, at):
        return remote(src.at[pl.ds(aligned((1 - c) * 8, 8), 8)], dst, es.at[at], er.at[at], mate)

    def left_last():
        for j in range(2):
            for t in range(8):
                p = 2 * t + j
                fin_up[:, p * 128 : (p + 1) * 128] = scatter_last(place, UP_ORDERS[j][3:], bup, rup, (j, t))
        far_copy(fin_up, far_up, 0).start()
        for p0, p1, _, rest in DOWN_GROUPS:
            for p in range(p0, p1):
                gdown_o[:, p * 128 : (p + 1) * 128] = scatter_last(place, rest, bdown, rdown, (p,))

    def out_last():
        for j, order in enumerate(OUT_ORDERS):
            fin_out[:, j * 128 : (j + 1) * 128] = scatter_last(place, order, bout, rout, (j,))
        far_copy(fin_out, far_out, 1).start()

    def qkv_copy(k, p, j):
        return Scatter(place, k, QKV_ORDERS[j], bqkv, rqkv, (p, j), qs, qr, (k - 1, p, j))

    def qkv_start(k, p):
        for j in range(3):
            qkv_copy(k, p, j).start()

    def qkv_finish(k, p):
        for j in range(3):
            qkv_copy(k, p, j).wait()
        for j, order in enumerate(QKV_ORDERS):
            if k < 3:
                scatter_add(place, k, order, bqkv, rqkv, (p, j))
            else:
                fin_qkv[:, pl.ds(aligned(j * 512 + p * 128, 128), 128)] = scatter_last(place, order, bqkv, rqkv, (p, j))
        if k < 3:
            qkv_start(k + 1, p)

    def pair(p, carry):
        lo = aligned(p * 128, 128)
        prod = (dctx[:, pl.ds(lo, 128)].astype(F32) * ctxh[:, pl.ds(lo, 128)].astype(F32)).astype(BF)
        drow[...] = dot_nt(pick, prod)
        dk_acc[...] = jnp.zeros_like(dk_acc)
        dv_acc[...] = jnp.zeros_like(dv_acc)
        at = p * 384
        for i, ref in enumerate((t0, t1, t2, t3)):
            w0, w1 = window(i)
            rows = slice(i * BLOCK, (i + 1) * BLOCK)
            query = qkv[rows, pl.ds(lo, 128)] * jnp.asarray(0.125, BF)
            keys = qkv[w0:w1, pl.ds(aligned(512 + lo, 128), 128)]
            values = qkv[w0:w1, pl.ds(aligned(1024 + lo, 128), 128)]
            grad = dctx[rows, pl.ds(lo, 128)]
            zero = jnp.zeros_like(query)
            both = jnp.concatenate([jnp.where(lane < 64, query, zero), jnp.where(lane < 64, zero, query)], axis=0)
            grads = jnp.concatenate([jnp.where(lane < 64, grad, zero), jnp.where(lane < 64, zero, grad)], axis=0)
            mask = ref[...]
            log_total = jnp.concatenate([lse[pl.ds(2 * p, 1), rows], lse[pl.ds(2 * p + 1, 1), rows]], axis=1)
            inner = jnp.concatenate([drow[0:1, rows], drow[1:2, rows]], axis=1)
            probs = jnp.exp(dot_nt(keys, both) + jnp.concatenate([mask, mask], axis=1) - log_total)
            dscores = (probs * (dot_nt(values, grads) - inner)).astype(BF)
            dv_acc[w0:w1, :] = dv_acc[w0:w1, :] + dot_nn(probs.astype(BF), grads)
            dk_acc[w0:w1, :] = dk_acc[w0:w1, :] + dot_nn(dscores, both)
            dq = dot_tn(keys, dscores)
            dq = jnp.where(row < 64, dq[:, :BLOCK], dq[:, BLOCK:]).T
            dqkv[rows, pl.ds(aligned(at, 128), 128)] = (dq * 0.125).astype(BF)
            for (ep, ei), events in EVENTS.items():
                if ei == i:

                    @pl.when(p == ep)
                    def _(events=events):
                        for event in events:
                            happen(*event)

            if i == 2:
                for back in (3, 2):

                    @pl.when(p >= back)
                    def _(back=back):
                        qkv_finish(back - 1, p - back)

        dqkv[:, pl.ds(aligned(at + 128, 128), 128)] = dk_acc[...].astype(BF)
        dqkv[:, pl.ds(aligned(at + 256, 128), 128)] = dv_acc[...].astype(BF)
        cols = pl.ds(aligned(at, 128), 384)
        sums = jnp.sum(dqkv[:, cols].astype(F32), axis=0, keepdims=True)
        late[0, pl.ds(16 + c * 4 + p, 1), :] = sums[:, 0:128]
        late[0, pl.ds(24 + c * 4 + p, 1), :] = sums[:, 256:384]

        @pl.when(p == 0)
        def _():
            for load in loads[10:]:
                load.wait()

        for b in range(4):
            block = slice(b * 256, (b + 1) * 256)
            grad = dot_nn(h1t[block, :], dqkv[:, cols])
            low = grad.astype(BF)
            for s in range(16):
                for j, order in enumerate(QKV_ORDERS):
                    bqkv[p, j, slot_of(b * 16 + s, order)] = low[s * 16 : (s + 1) * 16, j * 128 : (j + 1) * 128]
            weight = wq[block, cols].astype(F32)
            weight = jnp.concatenate([feature_rows(weight[0:128]), feature_rows(weight[128:256])], axis=0)
            by_gain, by_bias = grad * weight, weight * sums
            gain_acc[block, :] = gain_acc[block, :] + by_gain[:, 0:128] + by_gain[:, 128:256] + by_gain[:, 256:384]
            bias_acc[block, :] = bias_acc[block, :] + by_bias[:, 0:128] + by_bias[:, 128:256] + by_bias[:, 256:384]

        @pl.when(p == 1)
        def _():
            for b in range(4):
                block = slice(b * 256, (b + 1) * 256)
                dh_acc[block, :] = dot_nt(dqkv[block, 0:768], wq[:, 0:768])

        qkv_start(1, p)
        return carry

    lax.fori_loop(0, 4, pair, 0)

    def tail(n):
        for k in (3, 2, 1):
            p = n + 2 - k
            if p < 4 and (k, p) not in ((2, 0), (1, 1), (1, 0)):
                qkv_finish(k, p)

    def total_of(acc):
        flat = jnp.concatenate([natural_rows(acc[g * 128 : (g + 1) * 128, :]) for g in range(8)], axis=0)
        return jnp.sum(flat.T, axis=0, keepdims=True)

    bias_sum = total_of(bias_acc)
    gain_sum = (total_of(gain_acc) - par[1:2, :] * bias_sum) / par[0:1, :]
    for l in range(8):
        late[0, l : l + 1, :] = gain_sum[:, l * 128 : (l + 1) * 128]
        late[0, 8 + l : 9 + l, :] = bias_sum[:, l * 128 : (l + 1) * 128]
    vector_start(late, late_got, vs, vr, 0)

    def dh_copy(n):
        rows = pl.ds(aligned(n * BLOCK, BLOCK), BLOCK)
        return remote(dh_send.at[rows], dh_got.at[rows], hs.at[n], hr.at[n], mate)

    def second_half(rows):
        return dh_acc[rows, :] + dot_nt(dqkv[rows, 768:1536], wq[:, 768:1536])

    for n in range(2):
        rows = pl.ds(aligned((1 - c) * 512 + n * BLOCK, BLOCK), BLOCK)
        dh_send[n * BLOCK : (n + 1) * BLOCK, :] = second_half(rows).astype(BF)
        dh_copy(n).start()
    tail(1)
    for load in loads[8:10]:
        load.wait()

    def g_src(r):
        return gin_s.at[pl.ds(r * 128, 128)]

    def g_dst(r):
        return gin_o.at[z]

    for n in range(2):
        block = slice(n * BLOCK, (n + 1) * BLOCK)
        dh = second_half(pl.ds(aligned(c * 512 + n * BLOCK, BLOCK), BLOCK))
        dh_copy(n).wait()
        xhat, rstd = norm_parts(x_own[block, :].astype(F32))
        e = (dh + dh_got[block, :].astype(F32)) * par[0:1, :]
        gin_s[block, :] = (
            dres[block, :]
            + rstd * (e - jnp.mean(e, axis=-1, keepdims=True) - xhat * jnp.mean(e * xhat, axis=-1, keepdims=True))
        ).astype(BF)
        if n == 0:
            vector_finish(late, late_got, vs, vr, 0)
            tail(2)
        exchange_start(place, g_src, g_dst, g_dst, gs, gr, (2 * n, 2 * n + 1))
    vector_finish(late, late_got, vs, vr, 1)
    tail(3)
    main_finish(3, OUT)
    vector_finish(late, late_got, vs, vr, 2)
    late_copy.start()
    tail(4)
    far_copy(fin_qkv, far_qkv, 4).start()

    own8 = pl.ds(aligned(c * 8, 8), 8)
    far_copy(fin_up, far_up, 0).wait()
    for t in range(8):
        mine, theirs = fin_up[own8, t * 256 : (t + 1) * 256], far_up[:, t * 256 : (t + 1) * 256]
        gup_o[:, t * 512 : t * 512 + 256] = jnp.where(c == 0, mine, theirs)
        gup_o[:, t * 512 + 256 : t * 512 + 512] = jnp.where(c == 0, theirs, mine)
    far_copy(fin_out, far_out, 1).wait()
    mine, theirs = fin_out[own8, :], far_out[...]
    gout_o[:, 0:512] = jnp.where(c == 0, mine, theirs)
    gout_o[:, 512:1024] = jnp.where(c == 0, theirs, mine)
    far_copy(fin_qkv, far_qkv, 4).wait()
    for j in range(3):
        mine, theirs = fin_qkv[own8, j * 512 : (j + 1) * 512], far_qkv[:, j * 512 : (j + 1) * 512]
        gqkv_o[:, j * 1024 : j * 1024 + 512] = jnp.where(c == 0, mine, theirs)
        gqkv_o[:, j * 1024 + 512 : j * 1024 + 1024] = jnp.where(c == 0, theirs, mine)
    early_copy.wait()
    small_o[4:12, :] = early[3] + early_far[...]
    small_o[12:16, :] = jnp.zeros((4, 1024), F32)
    late_copy.wait()
    total = late[3] + late_far[...]
    for n in range(4):
        for l in range(8):
            small_o[n : n + 1, l * 128 : (l + 1) * 128] = total[n * 8 + l : n * 8 + l + 1, :]

    exchange_sent(place, l_src, l_dst, ls, lr)
    exchange_sent(place, g_src, g_dst, gs, gr)
    for b in range(4):
        pltpu.make_async_copy(lout.at[pl.ds(0, 128)], lout_o.at[b], lr.at[b]).wait()
        pltpu.make_async_copy(gin_s.at[pl.ds(0, 128)], gin_o.at[b], gr.at[b]).wait()


def run_backward(*args):
    outs = (
        shaped((4, 128, 1024), BF), shaped((4, 128, 1024), BF), shaped((8, 3072), F32), shaped((8, 1024), F32),
        shaped((8, 4096), F32), shaped((32, 1024), F32), shaped((16, 1024), F32),
    )
    v = pltpu.VMEM
    return pl.pallas_call(
        backward_kernel,
        out_shape=outs,
        in_specs=[vmem()] * 4 + [anywhere()] * 11,
        out_specs=(anywhere(), anywhere()) + (vmem(),) * 5,
        scratch_shapes=[
            v((1024, 1536), BF), v((1024, 512), BF), v((1024, 512), BF), v((1024, 1024), BF), v((512, 1024), BF),
            v((512, 1024), BF), v((512, 1024), F32),
            v((1024, 1536), BF), v((1024, 1024), BF), v((1024, 1536), BF), v((1024, 128), F32), v((1024, 128), F32),
            v((16, 1024), F32), v((256, 256), F32), v((512, 256), F32), v((768, 256), F32), v((768, 256), F32),
            v((2, 8, 8, 16, 128), BF), v((8, 8, 32, 128), BF), v((4, 64, 16, 128), BF), v((4, 3, 64, 16, 128), BF),
            v((2, 8, 7, 16, 128), BF), v((8, 7, 32, 128), BF), v((4, 63, 16, 128), BF), v((4, 3, 63, 16, 128), BF),
            v((16, 2048), F32), v((16, 512), F32), v((16, 1536), F32), v((8, 2048), F32), v((8, 512), F32),
            v((8, 1536), F32), v((512, 1024), BF), v((512, 1024), BF), v((1024, 1024), F32), v((512, 1024), BF),
            v((1024, 128), F32), v((1024, 128), F32),
            v((4, 8, 1024), F32), v((3, 3, 8, 1024), F32), v((8, 1024), F32), v((4, 32, 128), F32), v((3, 3, 32, 128), F32),
            v((32, 128), F32), dma(22), dma(3, 9, 3), dma(3, 9, 3), dma(3, 4, 3, 3), dma(3, 4, 3, 3), dma(4), dma(4), dma(4), dma(4), dma(2), dma(2),
            dma(6), dma(6), dma(3, 3), dma(3, 3), dma(3, 3), dma(3, 3),
        ],
        compiler_params=pltpu.CompilerParams(collective_id=1, has_side_effects=True, vmem_limit_bytes=VMEM_LIMIT),
        name="backward",
    )(*args)


VECTORS = ((0, 8), (1, 8), (2, 16), (4, 8), (5, 8), (6, 8), (8, 32), (7, 8))


def finish_kernel(*refs):
    lout, gin, gqkv, gout, gup, gdown, sums = refs[:7]
    outs, vectors = refs[7:13], refs[13:21]
    for src, dst in zip((lout, gin, gqkv, gout, gup, gdown), outs):
        dst[...] = src[...]
    place = Place()
    device = ((place.xh * 4 + place.y) * 2 + place.c) * 8 + place.xl * 4 + place.z
    for (row, size), out in zip(VECTORS, vectors):
        first = device * size
        line = row + lax.div(first, jnp.int32(1024))
        turned = pltpu.roll(sums[pl.ds(line, 1), :], 1024 - lax.rem(first, jnp.int32(1024)), 1)
        out[...] = turned[0, :size]


def run_finish(*args):
    outs = tuple(shaped(a.shape, a.dtype) for a in args[:6]) + tuple(shaped((size,), F32) for _, size in VECTORS)
    return pl.pallas_call(
        finish_kernel,
        out_shape=outs,
        in_specs=[vmem()] * 7,
        out_specs=(vmem(),) * 14,
        name="finish",
    )(*args)


def on_device(
    block_input, segment_ids, padding_flags, cotangent, norm_one_gain, norm_one_bias, query_key_value, query_value_bias,
    out_weight, out_bias, norm_two_gain, norm_two_bias, up_weight, up_bias, down_weight, down_bias,
):
    h1, qkv, x_own, ctxh, dres, dctx, lout, upleft, downleft, bout, lse, seg, par, small = run_first(
        block_input, cotangent, segment_ids, padding_flags, norm_one_gain, norm_one_bias, query_value_bias, out_bias,
        norm_two_gain, norm_two_bias, down_bias, up_bias, query_key_value, out_weight, up_weight, down_weight,
    )
    results = run_backward(
        lse, seg, small, par, upleft, downleft, bout, qkv, dctx, ctxh, h1, lout, query_key_value, x_own, dres
    )
    lout, gin, gqkv, gout, gup, gdown, n1g, n1b, qvb, ob, n2g, n2b, ub, db = run_finish(*results)
    return (lout, gin, n1g, n1b, gqkv, qvb, gout, ob, n2g, n2b, gup, ub, gdown, db)


def solution(mesh):
    wide = Mesh(mesh.devices.reshape(2, 4, 2, 2, 4), AXES)
    rows, seq = ("xh", "y", "c"), ("xl", "z")
    everything = rows + seq
    whole = P()
    return jax.shard_map(
        on_device,
        mesh=wide,
        in_specs=(P(rows, seq, None), P(rows, None), P(rows, None), P(rows, seq, None)) + (whole,) * 12,
        out_specs=(
            P(rows, seq, None), P(rows, seq, None), P(everything), P(everything), P(everything, None), P(everything),
            P(everything, None), P(everything), P(everything), P(everything), P(everything, None), P(everything),
            P(everything, None), P(everything),
        ),
        check_vma=False,
    )
```

```python
import jax
import jax.numpy as jnp
from jax import lax
from jax.experimental import pallas as pl
from jax.experimental.pallas import tpu as pltpu
from jax.sharding import Mesh, PartitionSpec as P

BF = jnp.bfloat16
F32 = jnp.float32
AXES = ("xh", "y", "c", "xl", "z")
BY_MESH = pl.DeviceIdType.MESH
DIMS = ("x1", "y1", "z1", "x0", "y0", "z0")
UP_ORDERS = (("y1", "y0", "x1", "z", "x0"), ("x1", "y0", "y1", "x0", "z"))
DOWN_GROUPS = (
    (0, 3, ("z1", "z0", "x0"), ("y", "x1")),
    (3, 6, ("z0", "x0", "z1"), ("x1", "y")),
    (6, 8, ("x0", "z1", "z0"), ("x1", "y")),
)
OUT_ORDERS = (("y", "x", "z"), ("y", "z", "x"), ("y", "x", "z"), ("y", "z", "x"))
QKV_ORDERS = (("x", "z", "y"), ("z", "x", "y"), ("y", "z", "x"))
LAG = {1: 2, 2: 3, 3: 4}
BLOCK = 256
GELU = 0.7978845608028654
CUBIC = 0.044715
EPS = 1e-05
MASKED = -1e30
VMEM_LIMIT = 60 * 1024 * 1024


def dot_nn(a, b):
    return lax.dot_general(a, b, (((1,), (0,)), ((), ())), preferred_element_type=F32)


def dot_nt(a, b):
    return lax.dot_general(a, b, (((1,), (1,)), ((), ())), preferred_element_type=F32)


def dot_tn(a, b):
    return lax.dot_general(a, b, (((0,), (0,)), ((), ())), preferred_element_type=F32)


class Place:
    def __init__(self):
        self.xh, self.y, self.c, self.xl, self.z = (lax.axis_index(a) for a in AXES)
        two = jnp.int32(2)
        self.bits = {
            "x1": self.xh,
            "x0": lax.rem(self.xl + self.xh, two),
            "y1": lax.div(self.y, two),
            "y0": lax.rem(self.y + lax.div(self.y, two), two),
            "z1": lax.div(self.z, two),
            "z0": lax.rem(self.z + lax.div(self.z, two), two),
            "x": 2 * self.xh + self.xl,
            "y": self.y,
            "z": self.z,
        }
        names = ("c", "x1", "y1", "z1", "x0", "y0", "z0")
        self.partners = {name: self.find_partner(name) for name in names}
        self.rings = {(axis, s): self.find_ring(axis, s) for axis in "xyz" for s in (1, 2, 3)}
        self.send, self.keep = {}, {}

    def prepare(self, orders):
        for order in orders:
            off = jnp.int32(0)
            for k, name in enumerate(order, 1):
                n = left_after(order, k)
                for s in range(1, width(name)):
                    to = 1 - self.bits[name] if width(name) == 2 else lax.rem(self.bits[name] + s, jnp.int32(4))
                    self.send[order, k, s] = off + to * n
                off = off + self.bits[name] * n
                self.keep[order, k] = off

    def partner(self, name):
        return self.partners[name]

    def ring(self, axis, step):
        return self.rings[axis, step]

    def find_partner(self, name):
        xh, y, c, xl, z = self.xh, self.y, self.c, self.xl, self.z
        if name == "c":
            c = 1 - c
        elif name == "x0":
            xl = 1 - xl
        elif name == "x1":
            xh, xl = 1 - xh, 1 - xl
        elif name == "y0":
            y = y + 1 - 2 * lax.rem(y, jnp.int32(2))
        elif name == "y1":
            y = 3 - y
        elif name == "z0":
            z = z + 1 - 2 * lax.rem(z, jnp.int32(2))
        elif name == "z1":
            z = 3 - z
        return (xh, y, c, xl, z)

    def find_ring(self, axis, step):
        four, two = jnp.int32(4), jnp.int32(2)
        xh, y, c, xl, z = self.xh, self.y, self.c, self.xl, self.z
        if axis == "x":
            at = lax.rem(2 * xh + xl + step, four)
            xh, xl = lax.div(at, two), lax.rem(at, two)
        elif axis == "y":
            y = lax.rem(y + step, four)
        else:
            z = lax.rem(z + step, four)
        return (xh, y, c, xl, z)

    def exchange(self, r):
        return (self.xh, self.y, self.xl, self.c, jnp.int32(r))

    def is_self(self, r):
        return (self.c == self.xl) & (self.z == r)


def bits_of(s):
    xh, y, xl, z = s >> 5, (s >> 3) & 3, (s >> 2) & 1, s & 3
    return {
        "x1": xh, "y1": y >> 1, "z1": z >> 1, "x0": xl ^ xh, "y0": (y & 1) ^ (y >> 1), "z0": (z & 1) ^ (z >> 1),
        "x": 2 * xh + xl, "y": y, "z": z,
    }


def width(name):
    return 4 if len(name) == 1 else 2


def left_after(order, k):
    n = 1
    for name in order[k:]:
        n *= width(name)
    return n


def slot_of(s, order):
    bits, slot = bits_of(s), 0
    for name in order:
        slot = width(name) * slot + bits[name]
    return slot


def region(order, k):
    return sum((width(name) - 1) * left_after(order, j + 1) for j, name in enumerate(order[: k - 1]))


class Scatter:
    def __init__(self, place, k, order, buf, got, lead, sends, recvs, at):
        name = order[k - 1]
        n = left_after(order, k)
        self.copies = []
        for s in range(1, width(name)):
            peer = place.partner(name) if width(name) == 2 else place.ring(name, s)
            self.copies.append(
                pltpu.make_async_remote_copy(
                    src_ref=buf.at[lead + (pl.ds(place.send[order, k, s], n),)],
                    dst_ref=got.at[lead + (pl.ds(region(order, k) + (s - 1) * n, n),)],
                    send_sem=sends.at[at + (s - 1,)],
                    recv_sem=recvs.at[at + (s - 1,)],
                    device_id=peer,
                    device_id_type=BY_MESH,
                )
            )

    def start(self):
        for copy in self.copies:
            copy.start()

    def wait(self):
        for copy in self.copies:
            copy.wait()


def scatter_sum(place, k, order, buf, got, lead):
    n = left_after(order, k)
    mine = lead + (pl.ds(place.keep[order, k], n),)
    if width(order[k - 1]) == 2 and k < len(order):
        return mine, buf[mine] + got[lead + (pl.ds(region(order, k), n),)]
    total = buf[mine].astype(F32)
    for s in range(1, width(order[k - 1])):
        total = total + got[lead + (pl.ds(region(order, k) + (s - 1) * n, n),)].astype(F32)
    return mine, total


def scatter_add(place, k, order, buf, got, lead):
    mine, total = scatter_sum(place, k, order, buf, got, lead)
    buf[mine] = total.astype(BF)


def scatter_last(place, order, buf, got, lead):
    _, total = scatter_sum(place, len(order), order, buf, got, lead)
    return total.reshape(total.shape[-2:])


def feature_rows(flat):
    parts = []
    for g in range(8):
        for c in range(2):
            parts.append(flat[(c * 8 + g) * 8 : (c * 8 + g + 1) * 8])
    return jnp.concatenate(parts, axis=0)


def natural_rows(flat):
    return jnp.concatenate([flat[(g * 2 + c) * 8 : (g * 2 + c + 1) * 8] for c in range(2) for g in range(8)], axis=0)


def transpose_features(src, dst, tokens):
    def body(f, carry):
        block = src[tokens, pl.ds(pl.multiple_of(f * 128, 128), 128)].astype(F32)
        dst[pl.ds(pl.multiple_of(f * 128, 128), 128), tokens] = feature_rows(block.T).astype(BF)
        return carry

    lax.fori_loop(0, 8, body, 0)


def norm_parts(v):
    center = v - jnp.mean(v, axis=-1, keepdims=True)
    rstd = lax.rsqrt(jnp.mean(center * center, axis=-1, keepdims=True) + EPS)
    return center * rstd, rstd


def aligned(v, m):
    return pl.multiple_of(v, m)


def window(i):
    return max(0, i - 2) * BLOCK, (i + 1) * BLOCK


def remote(src, dst, send, recv, device):
    return pltpu.make_async_remote_copy(
        src_ref=src, dst_ref=dst, send_sem=send, recv_sem=recv, device_id=device, device_id_type=BY_MESH
    )


def greet(place, devices, with_exchange):
    barrier = pltpu.get_barrier_semaphore()
    count = jnp.int32(len(devices))
    for d in devices:
        pl.semaphore_signal(barrier, inc=1, device_id=d, device_id_type=BY_MESH)
    if with_exchange:
        for r in range(4):

            @pl.when(jnp.logical_not(place.is_self(r)))
            def _(r=r):
                pl.semaphore_signal(barrier, inc=1, device_id=place.exchange(r), device_id_type=BY_MESH)

        count = count + 4 - jnp.where(place.c == place.xl, 1, 0)
    pl.semaphore_wait(barrier, count)


def exchange_start(place, src_of, dst_of, own_dst_of, sends, recvs, which=(0, 1, 2, 3)):
    for r in which:
        own = place.is_self(r)

        @pl.when(own)
        def _(r=r):
            pltpu.make_async_copy(src_of(r), own_dst_of(r), recvs.at[place.z]).start()

        @pl.when(jnp.logical_not(own))
        def _(r=r):
            remote(src_of(r), dst_of(r), sends.at[r], recvs.at[place.z], place.exchange(r)).start()


def exchange_sent(place, src_of, dst_of, sends, recvs):
    for r in range(4):

        @pl.when(jnp.logical_not(place.is_self(r)))
        def _(r=r):
            remote(src_of(r), dst_of(r), sends.at[r], recvs.at[place.z], place.exchange(r)).wait_send()


def vmem(n=None):
    return pl.BlockSpec(memory_space=pltpu.VMEM)


def anywhere():
    return pl.BlockSpec(memory_space=pl.ANY)


def dma(*shape):
    return pltpu.SemaphoreType.DMA(shape)


def shaped(shape, dtype):
    return jax.ShapeDtypeStruct(shape, dtype)


def first_kernel(
    x_in, c_in, seg_in, flag_in, g1, b1_, bqv, bo, g2, b2_, bd, bu, wqkv, wout, wup, wdown,
    h1_o, qkv_o, x_o, ctxh_o, dres_o, dctx_o, lout_o, upleft_o, downleft_o, bout_o, lse_o, seg_o, par, small_o,
    hid, cot, qkv, x_own, ctxh, ctxp, resid, h2t, lse_acc, wq, wo, wu, wd, down_acc, dh_acc, act_s, dup_s, dat, lout, dctx,
    bup, rup, bdown, rdown, bout, upleft, downleft, seg_got,
    xs, xr, cs, cr, hs, hr, fs, fr, ts, tr, gs, gr, ss, sr, ws, us, ds, es, er, ups, upr, dns, dnr, os,
):
    place = Place()
    c, xl, z = place.c, place.xl, place.z
    mate = place.partner("c")
    place.prepare(UP_ORDERS + tuple(g[2] for g in DOWN_GROUPS))
    own = pl.ds(aligned(c * 512, 512), 512)
    far = pl.ds(aligned((1 - c) * 512, 512), 512)
    loads = [
        pltpu.make_async_copy(
            wqkv.at[:, pl.ds(aligned(j * 1024 + c * 512, 512), 512)], wq.at[:, pl.ds(j * 512, 512)], ws.at[j]
        )
        for j in range(3)
    ]
    loads.append(pltpu.make_async_copy(wout, wo, ws.at[3]))

    def up_load(t):
        return pltpu.make_async_copy(
            wup.at[:, pl.ds(aligned((2 * t + c) * 256, 256), 256)], wu.at[lax.rem(t, jnp.int32(4))], us.at[t]
        )

    def down_load(t):
        return pltpu.make_async_copy(
            wdown.at[pl.ds(aligned((2 * t + c) * 256, 256), 256)], wd.at[lax.rem(t, jnp.int32(4))], ds.at[t]
        )

    def saves(n, src, dst):
        return pltpu.make_async_copy(src, dst, os.at[n])

    for load in loads:
        load.start()
    for t in range(4):
        up_load(jnp.int32(t)).start()
        down_load(jnp.int32(t)).start()
    greet(place, [mate] + [place.partner(d) for d in DIMS], True)

    def x_src(r):
        return x_in.at[r]

    def x_dst(r):
        return x_own.at[pl.ds(aligned(z * 128, 128), 128)]

    def c_src(r):
        return c_in.at[r]

    def c_dst(r):
        return cot.at[pl.ds(aligned(xl * 512 + z * 128, 128), 128)]

    exchange_start(place, x_src, x_dst, x_dst, xs, xr)
    seg_out = [remote(ref, seg_got.at[n], ss.at[n], sr.at[n], mate) for n, ref in enumerate((seg_in, flag_in))]
    for copy in seg_out:
        copy.start()
    for n, ref in enumerate((g1, b1_, bqv, bqv, bo, g2, b2_, bd, bu, bu, bu, bu)):
        first = {3: 1024, 9: 1024, 10: 2048, 11: 3072}.get(n, 0)
        par[n : n + 1, :] = ref[first : first + 1024].astype(F32).reshape(1, 1024)
    par[12:16, :] = jnp.zeros((4, 1024), F32)

    for copy in seg_out:
        copy.wait()
    own_seg, own_flag = seg_in[pl.ds(z, 1), :], flag_in[pl.ds(z, 1), :]
    far_seg, far_flag = seg_got[0, pl.ds(z, 1), :], seg_got[1, pl.ds(z, 1), :]
    near = jnp.where(c == xl, 1, 0)
    seg_row = jnp.where(near == 1, own_seg, far_seg).astype(F32)
    flag_row = jnp.where(near == 1, own_flag, far_flag)
    key_row = jnp.where(flag_row == 0, seg_row, -1.0)
    seg_o[...] = jnp.concatenate([seg_row, key_row, jnp.zeros((6, 1024), F32)], axis=0)
    seg_col = jnp.broadcast_to(seg_row, (128, 1024)).T
    for i in range(4):
        w0, w1 = window(i)
        rows = lax.broadcasted_iota(jnp.int32, (BLOCK, w1 - w0), 0) + i * BLOCK
        cols = lax.broadcasted_iota(jnp.int32, (BLOCK, w1 - w0), 1) + w0
        same = seg_col[i * BLOCK : (i + 1) * BLOCK, 0:1] == key_row[:, w0:w1]
        dh_acc[i * BLOCK : (i + 1) * BLOCK, 0 : w1 - w0] = jnp.where(
            (same & (cols <= rows)) | (rows == cols), 0.0, MASKED
        )
    lse_acc[...] = jnp.zeros_like(lse_acc)

    gain_one, bias_one = par[0:1, :], par[1:2, :]

    def block_copy(ref, b, mine, sends, recvs):
        half = c if mine else 1 - c
        rows = pl.ds(aligned(half * 512 + b * 128, 128), 128)
        return remote(ref.at[rows], ref.at[rows], sends.at[b], recvs.at[b], mate)

    for b in range(4):
        pltpu.make_async_copy(x_in.at[0], x_own.at[b * 128 : (b + 1) * 128], xr.at[b]).wait()
        xhat, _ = norm_parts(x_own[b * 128 : (b + 1) * 128].astype(F32))
        hid[pl.ds(aligned(c * 512 + b * 128, 128), 128)] = (xhat * gain_one + bias_one).astype(BF)
        block_copy(hid, b, True, hs, hr).start()
    exchange_start(place, c_src, c_dst, c_dst, cs, cr)
    saves(0, x_own, x_o).start()

    for load in loads[:3]:
        load.wait()
    zero = jnp.zeros((1, 512), F32)
    bias = jnp.concatenate([par[2:3, own], zero, par[3:4, own]], axis=1)

    def project(first):
        def body(n, carry):
            rows = pl.ds(aligned(first + n * BLOCK, BLOCK), BLOCK)
            qkv[rows, :] = (dot_nn(hid[rows, :], wq[...]) + bias).astype(BF)
            return carry

        lax.fori_loop(0, 2, body, 0)

    project(c * 512)
    for b in range(4):
        block_copy(hid, b, False, hs, hr).wait_recv()
    saves(1, hid, h1_o).start()
    project((1 - c) * 512)
    saves(2, qkv, qkv_o).start()

    lane = lax.broadcasted_iota(jnp.int32, (BLOCK, 128), 1)

    def ctx_copy(p, half):
        return remote(
            ctxh.at[far, pl.ds(aligned(p * 128, 128), 128)],
            ctxp.at[:, pl.ds(aligned(half * 512 + p * 128, 128), 128)],
            ts.at[p], tr.at[p], mate,
        )

    def attend(p, carry):
        lo = aligned(p * 128, 128)
        for i in range(4):
            w0, w1 = window(i)
            rows = slice(i * BLOCK, (i + 1) * BLOCK)
            query = qkv[rows, pl.ds(lo, 128)] * jnp.asarray(0.125, BF)
            keys = qkv[w0:w1, pl.ds(aligned(512 + lo, 128), 128)]
            values = qkv[w0:w1, pl.ds(aligned(1024 + lo, 128), 128)]
            zero = jnp.zeros_like(query)
            both = jnp.concatenate([jnp.where(lane < 64, query, zero), jnp.where(lane < 64, zero, query)], axis=0)
            mask = dh_acc[rows, 0 : w1 - w0]
            scores = dot_nt(both, keys) + jnp.concatenate([mask, mask], axis=0)
            top = jnp.max(scores, axis=-1, keepdims=True)
            expo = jnp.exp(scores - top)
            found = dot_nn(expo.astype(BF), jnp.concatenate([values, jnp.ones_like(values)], axis=1))
            total = found[:, 128:256]
            log_total = top + jnp.log(total)
            outs = found[:, 0:128] / total
            lse_acc[rows, :] = jnp.where(
                lane == 2 * p, log_total[:BLOCK], jnp.where(lane == 2 * p + 1, log_total[BLOCK:], lse_acc[rows, :])
            )
            ctxh[rows, pl.ds(lo, 128)] = jnp.where(lane < 64, outs[:BLOCK], outs[BLOCK:]).astype(BF)

        @pl.when(p == 3)
        def _():
            saves(1, hid, h1_o).wait()
            saves(2, qkv, qkv_o).wait()
            for b in range(4):
                block_copy(hid, b, True, hs, hr).wait_send()

        ctx_copy(p, c).start()
        ctxp[:, pl.ds(aligned(c * 512 + lo, 128), 128)] = ctxh[own, pl.ds(lo, 128)]
        return carry

    lax.fori_loop(0, 4, attend, 0)
    saves(3, ctxh, ctxh_o).start()
    lse_o[...] = lse_acc[...].T[0:16, :]

    for b in range(4):
        pltpu.make_async_copy(c_in.at[0], cot.at[pl.ds(aligned(c * 512 + b * 128, 128), 128)], cr.at[b]).wait()
        block_copy(cot, b, True, fs, fr).start()

    loads[3].wait()
    for p in range(4):
        ctx_copy(p, 1 - c).wait_recv()

    def h2_copy(n, half):
        rows = pl.ds(aligned(half * 512 + n * BLOCK, BLOCK), BLOCK)
        return remote(hid.at[rows], hid.at[rows], gs.at[n], gr.at[n], mate)

    def output(n, carry):
        rows = pl.ds(aligned(n * BLOCK, BLOCK), BLOCK)
        res = x_own[rows, :].astype(F32) + (dot_nn(ctxp[rows, :], wo[...]) + par[4:5, :])
        resid[rows, :] = res
        xhat, _ = norm_parts(res)
        hid[pl.ds(aligned(c * 512 + n * BLOCK, BLOCK), BLOCK), :] = (xhat * par[5:6, :] + par[6:7, :]).astype(BF)
        h2_copy(n, c).start()
        return carry

    lax.fori_loop(0, 2, output, 0)
    small_o[...] = jnp.zeros_like(small_o)
    transpose_features(hid, h2t, own)
    for n in range(2):
        h2_copy(n, 1 - c).wait_recv()
    transpose_features(hid, h2t, far)
    for b in range(4):
        block_copy(cot, b, False, fs, fr).wait_recv()

    def up_copy(k, t, j):
        return Scatter(place, k, UP_ORDERS[j], bup, rup, (t, j), ups, upr, (k - 1, t, j))

    def down_copy(k, t, g):
        p0, p1, order, _ = DOWN_GROUPS[g]
        return Scatter(place, k, order, bdown, rdown, (t, slice(p0, p1)), dns, dnr, (k - 1, t, g))

    def start(k, t):
        for j in range(2):
            up_copy(k, t, j).start()
        for g in range(3):
            down_copy(k, t, g).start()

    def tile_slot(t, rest):
        bits = {"x1": lax.div(t, jnp.int32(4)), "y": lax.rem(t, jnp.int32(4))}
        slot = jnp.int32(0)
        for name in rest:
            slot = width(name) * slot + bits[name]
        return slot

    def finish(k, t):
        for j in range(2):
            up_copy(k, t, j).wait()
        for g in range(3):
            down_copy(k, t, g).wait()
        for j, order in enumerate(UP_ORDERS):
            mine, total = scatter_sum(place, k, order, bup, rup, (t, j))
            if k < 3:
                bup[mine] = total.astype(BF)
            else:
                upleft[j, t] = total.astype(BF)
        for p0, p1, order, rest in DOWN_GROUPS:
            for p in range(p0, p1):
                mine, total = scatter_sum(place, k, order, bdown, rdown, (t, p))
                if k < 3:
                    bdown[mine] = total.astype(BF)
                else:
                    downleft[p, pl.ds(tile_slot(t, rest), 1)] = total.astype(BF)
        if k < 3:
            start(k + 1, t)

    def tile(t, carry):
        four = jnp.int32(4)
        ring = lax.rem(t, four)
        up_load(t).wait()
        down_load(t).wait()
        col = 2 * t + c
        up_row = 8 + lax.div(col, four)
        up_cols = pl.ds(aligned(lax.rem(col, four) * 256, 256), 256)
        up_bias = par[pl.ds(up_row, 1), up_cols]
        dbias = jnp.zeros((1, 256), F32)
        for b in range(4):
            rows = slice(b * BLOCK, (b + 1) * BLOCK)
            u = dot_nn(hid[rows, :], wu[ring]) + up_bias
            dact = dot_nt(cot[rows, :], wd[ring])
            square = u * u
            th = jnp.tanh(GELU * u * (1.0 + CUBIC * square))
            act_s[rows, :] = (0.5 * u * (1.0 + th)).astype(BF)
            slope = 0.5 * (1.0 + th) + 0.5 * u * (1.0 - th * th) * (GELU * (1.0 + (3.0 * CUBIC) * square))
            dup = (dact * slope).astype(BF)
            dup_s[rows, :] = dup
            dbias = dbias + jnp.sum(dup.astype(F32), axis=0, keepdims=True)
        small_o[pl.ds(up_row, 1), up_cols] = dbias

        for k in (3, 2, 1):

            @pl.when(t >= LAG[k])
            def _(k=k):
                finish(k, t - LAG[k])

        xh = lax.div(t, four)
        grad = dot_tn(act_s[...], cot[...]).astype(BF)
        for s in range(8):
            bits = bits_of(s)
            x0 = lax.rem(xh + (s >> 2), jnp.int32(2))
            for p0, p1, order, _ in DOWN_GROUPS:
                fixed = sum(bits[name] << (2 - n) for n, name in enumerate(order) if name != "x0")
                slot = fixed + x0 * (1 << (2 - order.index("x0")))
                for j in range(p0, p1):
                    bdown[t, j, slot] = grad[s * 32 : (s + 1) * 32, j * 128 : (j + 1) * 128]
        for b in range(4):
            grad = dot_nn(h2t[b * 256 : (b + 1) * 256, :], dup_s[...]).astype(BF)
            for s in range(16):
                for j, order in enumerate(UP_ORDERS):
                    bup[t, j, slot_of(b * 16 + s, order)] = grad[s * 16 : (s + 1) * 16, j * 128 : (j + 1) * 128]
        start(1, t)

        @pl.when(t == 0)
        def _():
            for b in range(4):
                rows = slice(b * BLOCK, (b + 1) * BLOCK)
                down_acc[rows, :] = dot_nn(act_s[rows, :], wd[ring])
                dh_acc[rows, :] = dot_nt(dup_s[rows, :], wu[ring])

        @pl.when(t > 0)
        def _():
            for b in range(4):
                rows = slice(b * BLOCK, (b + 1) * BLOCK)
                down_acc[rows, :] = down_acc[rows, :] + dot_nn(act_s[rows, :], wd[ring])
                dh_acc[rows, :] = dh_acc[rows, :] + dot_nt(dup_s[rows, :], wu[ring])

        @pl.when(t < 4)
        def _():
            up_load(t + 4).start()
            down_load(t + 4).start()

        return carry

    lax.fori_loop(0, 8, tile, 0)

    def rounds(n):
        for k in (3, 2, 1):
            if 0 <= n - LAG[k] < 8:
                finish(k, n - LAG[k])

    dh_send, dh_got = qkv.at[0:512, 0:1024], qkv.at[512:1024, 0:1024]
    dn_send, dn_got = wq.at[0:512, 0:1024], wq.at[512:1024, 0:1024]
    dc_send = qkv.at[0:512, 1024:1536]
    ctxt = wq.at[:, 1024:1536]
    wo_send, wo_got = bup.at[0:2], bup.at[2:4]
    dh_send[...] = dh_acc[far, :].astype(BF)
    dh_copy = remote(dh_send, dh_got, es.at[0], er.at[0], mate)
    dh_copy.start()
    dn_send[...] = down_acc[far, :].astype(BF)
    dn_copy = remote(dn_send, dn_got, es.at[1], er.at[1], mate)
    dn_copy.start()
    rounds(8)

    transpose_features(ctxp, ctxt, slice(0, 512))
    dh_copy.wait()
    dn_copy.wait()

    def norm_back(n, sums):
        gain_sum, bias_sum, out_sum, down_sum = sums
        rows = pl.ds(aligned(n * 128, 128), 128)
        mine = pl.ds(aligned(c * 512 + n * 128, 128), 128)
        res = resid[rows, :]
        lout[rows, :] = (res + (down_acc[mine, :] + dn_got[rows, :].astype(F32) + par[7:8, :])).astype(BF)
        xhat, rstd = norm_parts(res)
        dn = dh_acc[mine, :] + dh_got[rows, :].astype(F32)
        e = dn * par[5:6, :]
        cf = cot[mine, :].astype(F32)
        dres = cf + rstd * (
            e - jnp.mean(e, axis=-1, keepdims=True) - xhat * jnp.mean(e * xhat, axis=-1, keepdims=True)
        )
        resid[rows, :] = dres
        low = dres.astype(BF)
        dat[rows, :] = low
        return (
            gain_sum + jnp.sum(dn * xhat, axis=0, keepdims=True),
            bias_sum + jnp.sum(dn, axis=0, keepdims=True),
            out_sum + jnp.sum(low.astype(F32), axis=0, keepdims=True),
            down_sum + jnp.sum(cf, axis=0, keepdims=True),
        )

    nothing = jnp.zeros((1, 1024), F32)
    gain_sum, bias_sum, out_sum, down_sum = lax.fori_loop(0, 4, norm_back, (nothing,) * 4)
    small_o[5:6, :] = gain_sum
    small_o[6:7, :] = bias_sum
    small_o[4:5, :] = out_sum
    small_o[7:8, :] = down_sum
    saves(4, resid, dres_o).start()
    saves(5, lout, lout_o).start()

    dc_send[...] = dot_nt(dat[...], wo[far, :]).astype(BF)
    dc_copy = remote(dc_send, dctx.at[own], es.at[2], er.at[2], mate)
    dc_copy.start()
    rounds(9)

    def out_grad(cols, dst, lead):
        for b in range(4):
            grad = dot_nn(ctxt[b * 256 : (b + 1) * 256, :], dat[:, cols]).astype(BF)
            for s in range(16):
                for j, order in enumerate(OUT_ORDERS):
                    dst[lead(j) + (slot_of(b * 16 + s, order),)] = grad[s * 16 : (s + 1) * 16, j * 128 : (j + 1) * 128]

    out_grad(far, wo_send, lambda j: (j // 2, j % 2))
    wo_copy = remote(wo_send, wo_got, es.at[3], er.at[3], mate)
    wo_copy.start()
    dctx[own, :] = dot_nt(dat[...], wo[own, :]).astype(BF)
    rounds(10)
    out_grad(own, bout, lambda j: (j,))
    dc_copy.wait_send()
    remote(dc_send, dctx.at[far], es.at[2], er.at[2], mate).wait_recv()
    saves(6, dctx, dctx_o).start()
    for n in range(11, 8 + LAG[3]):
        rounds(n)
    saves(7, upleft, upleft_o).start()
    saves(8, downleft, downleft_o).start()
    wo_copy.wait()
    for j in range(4):
        bout[j] = bout[j] + wo_got[j // 2, j % 2]
    saves(9, bout, bout_o).start()

    exchange_sent(place, x_src, x_dst, xs, xr)
    exchange_sent(place, c_src, c_dst, cs, cr)
    for b in range(4):
        block_copy(cot, b, True, fs, fr).wait_send()
        ctx_copy(b, c).wait_send()
    for n in range(2):
        h2_copy(n, c).wait_send()
    saves(0, x_own, x_o).wait()
    saves(3, ctxh, ctxh_o).wait()
    saves(4, resid, dres_o).wait()
    saves(5, lout, lout_o).wait()
    saves(6, dctx, dctx_o).wait()
    saves(7, upleft, upleft_o).wait()
    saves(8, downleft, downleft_o).wait()
    saves(9, bout, bout_o).wait()


def run_first(*args):
    outs = (
        shaped((1024, 1024), BF), shaped((1024, 1536), BF), shaped((512, 1024), BF), shaped((1024, 512), BF),
        shaped((512, 1024), F32), shaped((1024, 512), BF), shaped((512, 1024), BF), shaped((2, 8, 8, 16, 128), BF),
        shaped((8, 8, 32, 128), BF), shaped((4, 64, 16, 128), BF), shaped((16, 1024), F32), shaped((8, 1024), F32),
        shaped((16, 1024), F32), shaped((16, 1024), F32),
    )
    v = pltpu.VMEM
    return pl.pallas_call(
        first_kernel,
        out_shape=outs,
        in_specs=[anywhere(), anywhere()] + [vmem()] * 10 + [anywhere()] * 4,
        out_specs=(anywhere(),) * 10 + (vmem(),) * 4,
        scratch_shapes=[
            v((1024, 1024), BF), v((1024, 1024), BF), v((1024, 1536), BF), v((512, 1024), BF), v((1024, 512), BF),
            v((512, 1024), BF), v((512, 1024), F32), v((1024, 1024), BF), v((1024, 128), F32), v((1024, 1536), BF),
            v((1024, 1024), BF), v((4, 1024, 256), BF), v((4, 256, 1024), BF), v((1024, 1024), F32),
            v((1024, 1024), F32), v((1024, 256), BF), v((1024, 256), BF), v((512, 1024), BF), v((512, 1024), BF),
            v((1024, 512), BF), v((8, 2, 64, 16, 128), BF), v((8, 2, 56, 16, 128), BF), v((8, 8, 8, 32, 128), BF),
            v((8, 8, 7, 32, 128), BF), v((4, 64, 16, 128), BF), v((2, 8, 8, 16, 128), BF), v((8, 8, 32, 128), BF),
            v((2, 4, 1024), jnp.int32),
            dma(4), dma(4), dma(4), dma(4), dma(4), dma(4), dma(4), dma(4), dma(4), dma(4), dma(2), dma(2), dma(2),
            dma(2), dma(4), dma(8), dma(8), dma(4), dma(4), dma(3, 8, 2, 1), dma(3, 8, 2, 1), dma(3, 8, 3, 1),
            dma(3, 8, 3, 1), dma(10),
        ],
        compiler_params=pltpu.CompilerParams(collective_id=0, has_side_effects=True, vmem_limit_bytes=VMEM_LIMIT),
        name="first",
    )(*args)


MAIN = (
    tuple((0, (j, slice(0, 8)), UP_ORDERS[j][3:]) for j in range(2))
    + tuple((1, (slice(p0, p1),), rest) for p0, p1, _, rest in DOWN_GROUPS)
    + tuple((2, (j,), order) for j, order in enumerate(OUT_ORDERS))
)
LEFT = (0, 1, 2, 3, 4)
OUT = (5, 6, 7, 8)
EVENTS = {
    (1, 1): (("left", 1), ("early", 0)),
    (2, 1): (("left", 2), ("early", 1)),
    (2, 2): (("out", 1),),
    (3, 1): (("early", 2),),
    (3, 3): (("out", 2),),
}


def backward_kernel(
    lse, seg, small_in, par, upleft, downleft, bout_in, qkv_in, dctx_in, ctxh_in, h1_in, lout_in, wqkv, x_in, dres_in,
    lout_o, gin_o, gqkv_o, gout_o, gup_o, gdown_o, small_o,
    qkv, dctx, ctxh, h1, lout, x_own, dres,
    wq, h1t, dqkv, dk_acc, dv_acc, drow, t0, t1, t2, t3, bup, bdown, bout, bqkv, rup, rdown, rout, rqkv,
    fin_up, fin_out, fin_qkv, far_up, far_out, far_qkv, dh_send, dh_got, dh_acc, gin_s, gain_acc, bias_acc,
    early, early_got, early_far, late, late_got, late_far,
    ws, ms, mr, qs, qr, ls, lr, gs, gr, hs, hr, es, er, ps, pr, vs, vr,
):
    place = Place()
    c, xl, z = place.c, place.xl, place.z
    mate = place.partner("c")
    place.prepare(tuple(order for _, _, order in MAIN) + QKV_ORDERS)
    moves = (
        (upleft, bup), (downleft, bdown), (bout_in, bout), (qkv_in, qkv), (dctx_in, dctx), (ctxh_in, ctxh), (h1_in, h1),
        (lout_in, lout), (x_in, x_own), (dres_in, dres),
    )
    loads = [pltpu.make_async_copy(src, dst, ws.at[n]) for n, (src, dst) in enumerate(moves)]
    for p in range(4):
        for j in range(3):
            loads.append(
                pltpu.make_async_copy(
                    wqkv.at[:, pl.ds(aligned(j * 1024 + c * 512 + p * 128, 128), 128)],
                    wq.at[:, pl.ds(p * 384 + j * 128, 128)],
                    ws.at[10 + p * 3 + j],
                )
            )
    for load in loads:
        load.start()
    peers = [mate] + [place.partner(d) for d in DIMS] + [place.ring(a, s) for a in "xyz" for s in (1, 2, 3)]
    greet(place, peers, True)

    def l_src(r):
        return lout.at[pl.ds(r * 128, 128)]

    def l_dst(r):
        return lout_o.at[z]

    for load in loads[:3]:
        load.wait()
    bufs, gots = (bup, bdown, bout), (rup, rdown, rout)

    def main_copy(k, n):
        which, lead, order = MAIN[n]
        return Scatter(place, k, order, bufs[which], gots[which], lead, ms, mr, (k - 1, n))

    def main_start(k, which):
        for n in which:
            main_copy(k, n).start()

    def main_finish(k, which):
        for n in which:
            main_copy(k, n).wait()
        for n in which:
            b, lead, order = MAIN[n]
            if k < len(order):
                scatter_add(place, k, order, bufs[b], gots[b], lead)
        if k < len(MAIN[which[0]][2]):
            main_start(k + 1, which)
        elif which is LEFT:
            left_last()
        else:
            out_last()

    def vector_copy(ref, got, sends, recvs, n, s):
        return remote(ref.at[n], got.at[n, s - 1], sends.at[n, s - 1], recvs.at[n, s - 1], place.ring("zxy"[n], s))

    def vector_start(ref, got, sends, recvs, n):
        for s in (1, 2, 3):
            vector_copy(ref, got, sends, recvs, n, s).start()

    def vector_finish(ref, got, sends, recvs, n):
        for s in (1, 2, 3):
            vector_copy(ref, got, sends, recvs, n, s).wait()
        ref[n + 1] = ref[n] + got[n, 0] + got[n, 1] + got[n, 2]
        if n < 2:
            vector_start(ref, got, sends, recvs, n + 1)

    early_copy = remote(early.at[3], early_far, es.at[3], er.at[3], mate)
    late_copy = remote(late.at[3], late_far, es.at[5], er.at[5], mate)

    def happen(what, k):
        if what == "left":
            main_finish(k, LEFT)
        elif what == "out":
            main_finish(k, OUT)
        else:
            vector_finish(early, early_got, ps, pr, k)
            if k == 2:
                early_copy.start()

    main_start(1, LEFT)
    early[0] = small_in[4:12, :]
    vector_start(early, early_got, ps, pr, 0)
    main_start(1, OUT)
    loads[7].wait()
    exchange_start(place, l_src, l_dst, l_dst, ls, lr)
    late[0] = jnp.zeros((32, 128), F32)

    key_col = jnp.broadcast_to(seg[1:2, :], (128, 1024)).T
    for i, ref in enumerate((t0, t1, t2, t3)):
        w0, w1 = window(i)
        rows = lax.broadcasted_iota(jnp.int32, (w1 - w0, BLOCK), 0) + w0
        cols = lax.broadcasted_iota(jnp.int32, (w1 - w0, BLOCK), 1) + i * BLOCK
        same = key_col[w0:w1, 0:1] == seg[0:1, i * BLOCK : (i + 1) * BLOCK]
        ref[...] = jnp.where((same & (rows <= cols)) | (rows == cols), 0.0, MASKED)
    for load in loads[3:7]:
        load.wait()
    transpose_features(h1, h1t, slice(0, 1024))
    gain_acc[...] = jnp.zeros_like(gain_acc)
    bias_acc[...] = jnp.zeros_like(bias_acc)

    lane = lax.broadcasted_iota(jnp.int32, (BLOCK, 128), 1)
    row = lax.broadcasted_iota(jnp.int32, (128, BLOCK), 0)
    head_of = lax.broadcasted_iota(jnp.int32, (16, 128), 1)
    row_of = lax.broadcasted_iota(jnp.int32, (16, 128), 0)
    pick = jnp.where(lax.div(head_of, jnp.int32(64)) == row_of, 1.0, 0.0).astype(BF)

    def far_copy(src, dst, at):
        return remote(src.at[pl.ds(aligned((1 - c) * 8, 8), 8)], dst, es.at[at], er.at[at], mate)

    def left_last():
        for j in range(2):
            for t in range(8):
                p = 2 * t + j
                fin_up[:, p * 128 : (p + 1) * 128] = scatter_last(place, UP_ORDERS[j][3:], bup, rup, (j, t))
        far_copy(fin_up, far_up, 0).start()
        for p0, p1, _, rest in DOWN_GROUPS:
            for p in range(p0, p1):
                gdown_o[:, p * 128 : (p + 1) * 128] = scatter_last(place, rest, bdown, rdown, (p,))

    def out_last():
        for j, order in enumerate(OUT_ORDERS):
            fin_out[:, j * 128 : (j + 1) * 128] = scatter_last(place, order, bout, rout, (j,))
        far_copy(fin_out, far_out, 1).start()

    def qkv_copy(k, p, j):
        return Scatter(place, k, QKV_ORDERS[j], bqkv, rqkv, (p, j), qs, qr, (k - 1, p, j))

    def qkv_start(k, p):
        for j in range(3):
            qkv_copy(k, p, j).start()

    def qkv_finish(k, p):
        for j in range(3):
            qkv_copy(k, p, j).wait()
        for j, order in enumerate(QKV_ORDERS):
            if k < 3:
                scatter_add(place, k, order, bqkv, rqkv, (p, j))
            else:
                fin_qkv[:, pl.ds(aligned(j * 512 + p * 128, 128), 128)] = scatter_last(place, order, bqkv, rqkv, (p, j))
        if k < 3:
            qkv_start(k + 1, p)

    def pair(p, carry):
        lo = aligned(p * 128, 128)
        prod = (dctx[:, pl.ds(lo, 128)].astype(F32) * ctxh[:, pl.ds(lo, 128)].astype(F32)).astype(BF)
        drow[...] = dot_nt(pick, prod)
        dk_acc[...] = jnp.zeros_like(dk_acc)
        dv_acc[...] = jnp.zeros_like(dv_acc)
        at = p * 384
        for i, ref in enumerate((t0, t1, t2, t3)):
            w0, w1 = window(i)
            rows = slice(i * BLOCK, (i + 1) * BLOCK)
            query = qkv[rows, pl.ds(lo, 128)] * jnp.asarray(0.125, BF)
            keys = qkv[w0:w1, pl.ds(aligned(512 + lo, 128), 128)]
            values = qkv[w0:w1, pl.ds(aligned(1024 + lo, 128), 128)]
            grad = dctx[rows, pl.ds(lo, 128)]
            zero = jnp.zeros_like(query)
            both = jnp.concatenate([jnp.where(lane < 64, query, zero), jnp.where(lane < 64, zero, query)], axis=0)
            grads = jnp.concatenate([jnp.where(lane < 64, grad, zero), jnp.where(lane < 64, zero, grad)], axis=0)
            mask = ref[...]
            log_total = jnp.concatenate([lse[pl.ds(2 * p, 1), rows], lse[pl.ds(2 * p + 1, 1), rows]], axis=1)
            inner = jnp.concatenate([drow[0:1, rows], drow[1:2, rows]], axis=1)
            probs = jnp.exp(dot_nt(keys, both) + jnp.concatenate([mask, mask], axis=1) - log_total)
            dscores = (probs * (dot_nt(values, grads) - inner)).astype(BF)
            dv_acc[w0:w1, :] = dv_acc[w0:w1, :] + dot_nn(probs.astype(BF), grads)
            dk_acc[w0:w1, :] = dk_acc[w0:w1, :] + dot_nn(dscores, both)
            dq = dot_tn(keys, dscores)
            dq = jnp.where(row < 64, dq[:, :BLOCK], dq[:, BLOCK:]).T
            dqkv[rows, pl.ds(aligned(at, 128), 128)] = (dq * 0.125).astype(BF)
            for (ep, ei), events in EVENTS.items():
                if ei == i:

                    @pl.when(p == ep)
                    def _(events=events):
                        for event in events:
                            happen(*event)

            if i == 2:
                for back in (3, 2):

                    @pl.when(p >= back)
                    def _(back=back):
                        qkv_finish(back - 1, p - back)

        dqkv[:, pl.ds(aligned(at + 128, 128), 128)] = dk_acc[...].astype(BF)
        dqkv[:, pl.ds(aligned(at + 256, 128), 128)] = dv_acc[...].astype(BF)
        cols = pl.ds(aligned(at, 128), 384)
        sums = jnp.sum(dqkv[:, cols].astype(F32), axis=0, keepdims=True)
        late[0, pl.ds(16 + c * 4 + p, 1), :] = sums[:, 0:128]
        late[0, pl.ds(24 + c * 4 + p, 1), :] = sums[:, 256:384]

        @pl.when(p == 0)
        def _():
            for load in loads[10:]:
                load.wait()

        for b in range(4):
            block = slice(b * 256, (b + 1) * 256)
            grad = dot_nn(h1t[block, :], dqkv[:, cols])
            low = grad.astype(BF)
            for s in range(16):
                for j, order in enumerate(QKV_ORDERS):
                    bqkv[p, j, slot_of(b * 16 + s, order)] = low[s * 16 : (s + 1) * 16, j * 128 : (j + 1) * 128]
            weight = wq[block, cols].astype(F32)
            weight = jnp.concatenate([feature_rows(weight[0:128]), feature_rows(weight[128:256])], axis=0)
            by_gain, by_bias = grad * weight, weight * sums
            gain_acc[block, :] = gain_acc[block, :] + by_gain[:, 0:128] + by_gain[:, 128:256] + by_gain[:, 256:384]
            bias_acc[block, :] = bias_acc[block, :] + by_bias[:, 0:128] + by_bias[:, 128:256] + by_bias[:, 256:384]

        @pl.when(p == 1)
        def _():
            for b in range(4):
                block = slice(b * 256, (b + 1) * 256)
                dh_acc[block, :] = dot_nt(dqkv[block, 0:768], wq[:, 0:768])

        qkv_start(1, p)
        return carry

    lax.fori_loop(0, 4, pair, 0)

    def tail(n):
        for k in (3, 2, 1):
            p = n + 2 - k
            if p < 4 and (k, p) not in ((2, 0), (1, 1), (1, 0)):
                qkv_finish(k, p)

    def total_of(acc):
        flat = jnp.concatenate([natural_rows(acc[g * 128 : (g + 1) * 128, :]) for g in range(8)], axis=0)
        return jnp.sum(flat.T, axis=0, keepdims=True)

    bias_sum = total_of(bias_acc)
    gain_sum = (total_of(gain_acc) - par[1:2, :] * bias_sum) / par[0:1, :]
    for l in range(8):
        late[0, l : l + 1, :] = gain_sum[:, l * 128 : (l + 1) * 128]
        late[0, 8 + l : 9 + l, :] = bias_sum[:, l * 128 : (l + 1) * 128]
    vector_start(late, late_got, vs, vr, 0)

    def dh_copy(n):
        rows = pl.ds(aligned(n * BLOCK, BLOCK), BLOCK)
        return remote(dh_send.at[rows], dh_got.at[rows], hs.at[n], hr.at[n], mate)

    def second_half(rows):
        return dh_acc[rows, :] + dot_nt(dqkv[rows, 768:1536], wq[:, 768:1536])

    for n in range(2):
        rows = pl.ds(aligned((1 - c) * 512 + n * BLOCK, BLOCK), BLOCK)
        dh_send[n * BLOCK : (n + 1) * BLOCK, :] = second_half(rows).astype(BF)
        dh_copy(n).start()
    tail(1)
    for load in loads[8:10]:
        load.wait()

    def g_src(r):
        return gin_s.at[pl.ds(r * 128, 128)]

    def g_dst(r):
        return gin_o.at[z]

    for n in range(2):
        block = slice(n * BLOCK, (n + 1) * BLOCK)
        dh = second_half(pl.ds(aligned(c * 512 + n * BLOCK, BLOCK), BLOCK))
        dh_copy(n).wait()
        xhat, rstd = norm_parts(x_own[block, :].astype(F32))
        e = (dh + dh_got[block, :].astype(F32)) * par[0:1, :]
        gin_s[block, :] = (
            dres[block, :]
            + rstd * (e - jnp.mean(e, axis=-1, keepdims=True) - xhat * jnp.mean(e * xhat, axis=-1, keepdims=True))
        ).astype(BF)
        if n == 0:
            vector_finish(late, late_got, vs, vr, 0)
            tail(2)
        exchange_start(place, g_src, g_dst, g_dst, gs, gr, (2 * n, 2 * n + 1))
    vector_finish(late, late_got, vs, vr, 1)
    tail(3)
    main_finish(3, OUT)
    vector_finish(late, late_got, vs, vr, 2)
    late_copy.start()
    tail(4)
    far_copy(fin_qkv, far_qkv, 4).start()

    own8 = pl.ds(aligned(c * 8, 8), 8)
    far_copy(fin_up, far_up, 0).wait()
    for t in range(8):
        mine, theirs = fin_up[own8, t * 256 : (t + 1) * 256], far_up[:, t * 256 : (t + 1) * 256]
        gup_o[:, t * 512 : t * 512 + 256] = jnp.where(c == 0, mine, theirs)
        gup_o[:, t * 512 + 256 : t * 512 + 512] = jnp.where(c == 0, theirs, mine)
    far_copy(fin_out, far_out, 1).wait()
    mine, theirs = fin_out[own8, :], far_out[...]
    gout_o[:, 0:512] = jnp.where(c == 0, mine, theirs)
    gout_o[:, 512:1024] = jnp.where(c == 0, theirs, mine)
    far_copy(fin_qkv, far_qkv, 4).wait()
    for j in range(3):
        mine, theirs = fin_qkv[own8, j * 512 : (j + 1) * 512], far_qkv[:, j * 512 : (j + 1) * 512]
        gqkv_o[:, j * 1024 : j * 1024 + 512] = jnp.where(c == 0, mine, theirs)
        gqkv_o[:, j * 1024 + 512 : j * 1024 + 1024] = jnp.where(c == 0, theirs, mine)
    early_copy.wait()
    small_o[4:12, :] = early[3] + early_far[...]
    small_o[12:16, :] = jnp.zeros((4, 1024), F32)
    late_copy.wait()
    total = late[3] + late_far[...]
    for n in range(4):
        for l in range(8):
            small_o[n : n + 1, l * 128 : (l + 1) * 128] = total[n * 8 + l : n * 8 + l + 1, :]

    exchange_sent(place, l_src, l_dst, ls, lr)
    exchange_sent(place, g_src, g_dst, gs, gr)
    for b in range(4):
        pltpu.make_async_copy(lout.at[pl.ds(0, 128)], lout_o.at[b], lr.at[b]).wait()
        pltpu.make_async_copy(gin_s.at[pl.ds(0, 128)], gin_o.at[b], gr.at[b]).wait()


def run_backward(*args):
    outs = (
        shaped((4, 128, 1024), BF), shaped((4, 128, 1024), BF), shaped((8, 3072), F32), shaped((8, 1024), F32),
        shaped((8, 4096), F32), shaped((32, 1024), F32), shaped((16, 1024), F32),
    )
    v = pltpu.VMEM
    return pl.pallas_call(
        backward_kernel,
        out_shape=outs,
        in_specs=[vmem()] * 4 + [anywhere()] * 11,
        out_specs=(anywhere(), anywhere()) + (vmem(),) * 5,
        scratch_shapes=[
            v((1024, 1536), BF), v((1024, 512), BF), v((1024, 512), BF), v((1024, 1024), BF), v((512, 1024), BF),
            v((512, 1024), BF), v((512, 1024), F32),
            v((1024, 1536), BF), v((1024, 1024), BF), v((1024, 1536), BF), v((1024, 128), F32), v((1024, 128), F32),
            v((16, 1024), F32), v((256, 256), F32), v((512, 256), F32), v((768, 256), F32), v((768, 256), F32),
            v((2, 8, 8, 16, 128), BF), v((8, 8, 32, 128), BF), v((4, 64, 16, 128), BF), v((4, 3, 64, 16, 128), BF),
            v((2, 8, 7, 16, 128), BF), v((8, 7, 32, 128), BF), v((4, 63, 16, 128), BF), v((4, 3, 63, 16, 128), BF),
            v((16, 2048), F32), v((16, 512), F32), v((16, 1536), F32), v((8, 2048), F32), v((8, 512), F32),
            v((8, 1536), F32), v((512, 1024), BF), v((512, 1024), BF), v((1024, 1024), F32), v((512, 1024), BF),
            v((1024, 128), F32), v((1024, 128), F32),
            v((4, 8, 1024), F32), v((3, 3, 8, 1024), F32), v((8, 1024), F32), v((4, 32, 128), F32), v((3, 3, 32, 128), F32),
            v((32, 128), F32), dma(22), dma(3, 9, 3), dma(3, 9, 3), dma(3, 4, 3, 3), dma(3, 4, 3, 3), dma(4), dma(4), dma(4), dma(4), dma(2), dma(2),
            dma(6), dma(6), dma(3, 3), dma(3, 3), dma(3, 3), dma(3, 3),
        ],
        compiler_params=pltpu.CompilerParams(collective_id=1, has_side_effects=True, vmem_limit_bytes=VMEM_LIMIT),
        name="backward",
    )(*args)


VECTORS = ((0, 8), (1, 8), (2, 16), (4, 8), (5, 8), (6, 8), (8, 32), (7, 8))


def finish_kernel(*refs):
    lout, gin, gqkv, gout, gup, gdown, sums = refs[:7]
    outs, vectors = refs[7:13], refs[13:21]
    for src, dst in zip((lout, gin, gqkv, gout, gup, gdown), outs):
        dst[...] = src[...]
    place = Place()
    device = ((place.xh * 4 + place.y) * 2 + place.c) * 8 + place.xl * 4 + place.z
    for (row, size), out in zip(VECTORS, vectors):
        first = device * size
        line = row + lax.div(first, jnp.int32(1024))
        turned = pltpu.roll(sums[pl.ds(line, 1), :], 1024 - lax.rem(first, jnp.int32(1024)), 1)
        out[...] = turned[0, :size]


def run_finish(*args):
    outs = tuple(shaped(a.shape, a.dtype) for a in args[:6]) + tuple(shaped((size,), F32) for _, size in VECTORS)
    return pl.pallas_call(
        finish_kernel,
        out_shape=outs,
        in_specs=[vmem()] * 7,
        out_specs=(vmem(),) * 14,
        name="finish",
    )(*args)


def on_device(
    block_input, segment_ids, padding_flags, cotangent, norm_one_gain, norm_one_bias, query_key_value, query_value_bias,
    out_weight, out_bias, norm_two_gain, norm_two_bias, up_weight, up_bias, down_weight, down_bias,
):
    h1, qkv, x_own, ctxh, dres, dctx, lout, upleft, downleft, bout, lse, seg, par, small = run_first(
        block_input, cotangent, segment_ids, padding_flags, norm_one_gain, norm_one_bias, query_value_bias, out_bias,
        norm_two_gain, norm_two_bias, down_bias, up_bias, query_key_value, out_weight, up_weight, down_weight,
    )
    results = run_backward(
        lse, seg, small, par, upleft, downleft, bout, qkv, dctx, ctxh, h1, lout, query_key_value, x_own, dres
    )
    lout, gin, gqkv, gout, gup, gdown, n1g, n1b, qvb, ob, n2g, n2b, ub, db = run_finish(*results)
    return (lout, gin, n1g, n1b, gqkv, qvb, gout, ob, n2g, n2b, gup, ub, gdown, db)


def solution(mesh):
    wide = Mesh(mesh.devices.reshape(2, 4, 2, 2, 4), AXES)
    rows, seq = ("xh", "y", "c"), ("xl", "z")
    everything = rows + seq
    whole = P()
    return jax.shard_map(
        on_device,
        mesh=wide,
        in_specs=(P(rows, seq, None), P(rows, None), P(rows, None), P(rows, seq, None)) + (whole,) * 12,
        out_specs=(
            P(rows, seq, None), P(rows, seq, None), P(everything), P(everything), P(everything, None), P(everything),
            P(everything, None), P(everything), P(everything), P(everything), P(everything, None), P(everything),
            P(everything, None), P(everything),
        ),
        check_vma=False,
    )
```
